32 devices in a mesh: gx: 2 (over y), gy: 4 (over x, core), shot: 4 (over z).
Axes of the slice: x: 2, y: 2, z: 4, core: 2. Of those that a mesh axis runs over, the one named last changes fastest.
Arguments:
- adj_prev: float32 [4, 64, 64, 256], P('shot', 'gx', 'gy'), may hold values from -6 to 6
- adj_cur: float32 [4, 64, 64, 256], P('shot', 'gx', 'gy'), may hold values from -6 to 6
- fwd_accel: bfloat16 [4, 4, 64, 64, 256], P('shot', None, 'gx', 'gy'), may hold values from -6 to 6
- courant2: float32 [64, 64, 256], P('gx', 'gy'), may hold values from 0.05 to 0.18
- traces: bfloat16 [4, 4, 512], P('shot', None, ('gx', 'gy')), may hold values from -6 to 6
- weights: bfloat16 [2, 4, 64, 16, 256], P('gx', 'gy'), may hold values from -3 to 3
- rblock: int32 [2, 4, 64], P('gx', 'gy'), may hold values from 0 to 31
- column: int32 [2, 4, 64], P('gx', 'gy'), may hold values from 0 to 511
- counts: int32 [2, 4], P('gx', 'gy'), may hold values from 16 to 64
Outputs:
- adj_prev_out: float32 [4, 64, 64, 256], P('shot', 'gx', 'gy')
- adj_cur_out: float32 [4, 64, 64, 256], P('shot', 'gx', 'gy')
- gradient: float32 [32, 32, 128], P('gx', 'gy')
The draws below stay inside these ranges and needn't reach their ends.
All inputs are finite; a program needn't handle non-finite values.
Results may differ from the reference program's by a relative error of at most 0.00045.
Values may be sent and summed in bfloat16 or wider, within the bound.
No kernel may reach another device: no remote copies, remote signals or barrier semaphores. Data moves between devices by JAX's collectives and lax.ppermute only.
A program may use at most 128 MiB of HBM per device.

```python
import jax
import jax.numpy as jnp
from jax import lax

CX = 32
CY = 16
NZ = 256
STEPS = 4
SLOTS = 64
RB = 16
TX = 2
TY = 4
SHOTS = 4
NX = 64
NY = 64
NREC = 512


def draw_counts(key, part):
    tiles = TX * TY
    drawn = jax.random.randint(key, (tiles,), SLOTS // 4, SLOTS + 1)
    chosen = jax.random.randint(jax.random.fold_in(key, 7), (), 0, tiles)
    drawn = jnp.where(jnp.arange(tiles) == chosen, SLOTS, drawn)
    return drawn.reshape(TX, TY).astype(jnp.int32)


def set_ends(values, stream_key, smallest, largest):
    spot = [jax.random.randint(jax.random.fold_in(stream_key, axis), (), 0, length) for axis, length in enumerate(values.shape)]
    longest = values.shape.index(max(values.shape))
    neighbour = spot[:longest] + [(spot[longest] + 1) % values.shape[longest]] + spot[longest + 1:]
    return values.at[tuple(spot)].set(smallest).at[tuple(neighbour)].set(largest)


def block_levels(stream_key, dims, pieces, least, high):
    def one(axis_at, shards_of):
        steps = jax.random.uniform(jax.random.fold_in(jax.random.fold_in(stream_key, 6), axis_at), (shards_of,), jnp.float32, least / len(pieces), high / len(pieces))
        return jnp.repeat(jnp.exp(steps), dims[axis_at] // shards_of).reshape((-1,) + (1,) * (len(dims) - axis_at - 1))

    level = one(*pieces[0])
    for cut in pieces[1:]:
        level = level * one(*cut)
    return level


def centred(key, extent, deviation, most, split=(), held_as=jnp.bfloat16):
    array = jax.random.normal(key, extent, jnp.float32) * deviation
    if len(split) > 0:
        array = block_levels(key, extent, split, -0.22, 0.18) * array
    return jnp.clip(array, min=-most, max=most).astype(held_as)


def setup_inputs(seed: int = 0) -> dict:
    key_list = jax.random.split(jax.random.key(seed), 10)
    adj_prev = centred(key_list[0], (SHOTS, NX, NY, NZ), 1.0, 6.0, ((0, 4), (1, 2), (2, 4)), jnp.float32)
    adj_cur = centred(key_list[1], (SHOTS, NX, NY, NZ), 1.0, 6.0, ((0, 4), (1, 2), (2, 4)), jnp.float32)
    fwd_accel = centred(key_list[2], (SHOTS, STEPS, NX, NY, NZ), 1.0, 6.0, ((0, 4), (2, 2), (3, 4)))
    courant2 = jnp.clip(0.05 + 0.13000001 * jax.random.uniform(key_list[3], (NX, NY, NZ), jnp.float32) ** block_levels(key_list[3], (NX, NY, NZ), ((0, 2), (1, 4)), -0.2, 0.2), 0.05, 0.18)
    traces = centred(key_list[4], (SHOTS, STEPS, NREC), 1.0, 6.0, ((0, 4), (2, 8)))
    weights = centred(key_list[5], (TX, TY, SLOTS, RB, NZ), 0.5, 3.0, ((0, 2), (1, 4)))
    rblock = set_ends(jax.random.randint(key_list[6], (TX, TY, SLOTS), 0, NREC // RB), jax.random.fold_in(key_list[6], 1), 0, (NREC // RB) - 1).astype(jnp.int32)
    column = set_ends(jax.random.randint(key_list[7], (TX, TY, SLOTS), 0, CX * CY), jax.random.fold_in(key_list[7], 1), 0, (CX * CY) - 1).astype(jnp.int32)
    counts = draw_counts(jax.random.fold_in(key_list[9], 71), 0)
    return dict(adj_prev=adj_prev, adj_cur=adj_cur, fwd_accel=fwd_accel, courant2=courant2, traces=traces, weights=weights, rblock=rblock, column=column, counts=counts)


LAPLACE_COEFS = (-205.0 / 72.0, 8.0 / 5.0, -1.0 / 5.0, 8.0 / 315.0, -1.0 / 560.0)


def laplace(field):
    padded = jnp.pad(field, 4)
    size_x, size_y, size_z = field.shape
    center = padded[4:4 + size_x, 4:4 + size_y, 4:4 + size_z]
    total = 3.0 * LAPLACE_COEFS[0] * center
    for offset in range(1, 5):
        weight = LAPLACE_COEFS[offset]
        total = total + weight * (padded[4 + offset:4 + offset + size_x, 4:4 + size_y, 4:4 + size_z] + padded[4 - offset:4 - offset + size_x, 4:4 + size_y, 4:4 + size_z])
        total = total + weight * (padded[4:4 + size_x, 4 + offset:4 + offset + size_y, 4:4 + size_z] + padded[4:4 + size_x, 4 - offset:4 - offset + size_y, 4:4 + size_z])
        total = total + weight * (padded[4:4 + size_x, 4:4 + size_y, 4 + offset:4 + offset + size_z] + padded[4:4 + size_x, 4:4 + size_y, 4 - offset:4 - offset + size_z])
    return total


def restrict(fine):
    size_x, size_y, size_z = fine.shape
    return fine.reshape(size_x // 2, 2, size_y // 2, 2, size_z // 2, 2).mean(axis=(1, 3, 5))


def reference(adj_prev, adj_cur, fwd_accel, courant2, traces, weights, rblock, column, counts):
    tiles_x, tiles_y = counts.shape
    slots = rblock.shape[2]
    recv_block = weights.shape[3]
    live_slots = (jnp.arange(slots, dtype=jnp.int32)[None, None, :] < counts[:, :, None]).astype(jnp.float32)
    onehot = (column[..., None] == jnp.arange(CX * CY, dtype=jnp.int32)).astype(jnp.float32) * live_slots[..., None]
    weights_wide = weights.astype(jnp.float32)

    def one_shot(shot_data):
        previous, current, accel, trace = shot_data
        blocks = trace.reshape(STEPS, -1, recv_block)
        picked = blocks[:, rblock].astype(jnp.float32)
        contrib = jnp.einsum("tabsr,absrz->tabsz", picked, weights_wide, precision=lax.Precision.HIGHEST)
        source = jnp.einsum("absc,tabsz->tabcz", onehot, contrib, precision=lax.Precision.HIGHEST)
        source = source.reshape(STEPS, tiles_x, tiles_y, CX, CY, NZ).transpose(0, 1, 3, 2, 4, 5).reshape(STEPS, tiles_x * CX, tiles_y * CY, NZ)
        fine = jnp.zeros(current.shape, jnp.float32)
        for step_index in range(STEPS):
            next_field = 2.0 * current - previous + courant2 * laplace(current) + source[step_index]
            fine = fine + accel[step_index].astype(jnp.float32) * next_field
            previous, current = current, next_field
        return previous, current, restrict(fine)

    outputs = lax.map(one_shot, (adj_prev, adj_cur, fwd_accel, traces))
    return outputs[0], outputs[1], jnp.sum(outputs[2], axis=0)
```

```python
import functools

import jax
import jax.numpy as jnp
from jax import lax
from jax.experimental import pallas as pl
from jax.experimental.pallas import tpu as pltpu
from jax.sharding import PartitionSpec as P

LAPLACE_COEFS = (-205.0 / 72.0, 8.0 / 5.0, -1.0 / 5.0, 8.0 / 315.0, -1.0 / 560.0)
REACH = 4
F32 = jnp.float32
BF16 = jnp.bfloat16


def vmem_call(kernel, outs, args, scratch=(), aliases=None, flops=0, smem=(), name=None):
    in_specs = [pl.BlockSpec(memory_space=pltpu.SMEM if i in smem else pltpu.VMEM) for i in range(len(args))]
    moved = sum(a.size * a.dtype.itemsize for a in args) + sum(o.size * o.dtype.itemsize for o in outs)
    return pl.pallas_call(
        kernel,
        out_shape=tuple(outs),
        in_specs=in_specs,
        out_specs=tuple(pl.BlockSpec(memory_space=pltpu.VMEM) for _ in outs),
        scratch_shapes=list(scratch),
        input_output_aliases=aliases or {},
        cost_estimate=pl.CostEstimate(flops=flops, bytes_accessed=moved, transcendentals=0),
        name=name,
    )(*args)


def sds(shape, dtype=F32):
    return jax.ShapeDtypeStruct(shape, dtype)


def even_pairs(n):
    pairs = []
    for i in range(0, n - 1, 2):
        pairs += [(i, i + 1), (i + 1, i)]
    return pairs


def odd_pairs(n):
    pairs = []
    for i in range(1, n - 1, 2):
        pairs += [(i, i + 1), (i + 1, i)]
    return pairs


def split2(v):
    hi = v.astype(BF16)
    return hi, (v - hi.astype(F32)).astype(BF16)


def dot(a, b):
    return jnp.dot(a, b, preferred_element_type=F32)


def put_y_face(cur, out, high):
    cx, cy, _ = cur.shape
    start = cy - REACH if high else 0
    for i in range(cx // 2):
        out[i, 0:REACH, :] = cur[2 * i, start : start + REACH, :]
        out[i, REACH : 2 * REACH, :] = cur[2 * i + 1, start : start + REACH, :]


def put_faces(cur, gx_index, gy_index, ye, yo, xe, xo):
    cx, cy, _ = cur.shape
    y_even = gy_index % 2 == 0
    x_even = gx_index % 2 == 0

    @pl.when(y_even)
    def _():
        put_y_face(cur, ye, True)
        if yo is not None:
            put_y_face(cur, yo, False)

    @pl.when(jnp.logical_not(y_even))
    def _():
        put_y_face(cur, ye, False)
        if yo is not None:
            put_y_face(cur, yo, True)

    half = cy // 8
    low = jnp.where(x_even, cx - REACH, 0)
    for r in range(REACH):
        for h in range(half):
            xe[r * half + h, :, :] = cur[low + r, 8 * h : 8 * h + 8, :]
            if xo is not None:
                xo[r * half + h, :, :] = cur[cx - REACH - low + r, 8 * h : 8 * h + 8, :]


def add_y_halo(nxt, c2, recv, high):
    cx, cy, nz = nxt.shape
    w = LAPLACE_COEFS
    row = lax.broadcasted_iota(jnp.int32, (8, nz), 0) % REACH
    coefs = {}
    for k in range(1, REACH + 1):
        shift = REACH - k
        keep = (row >= shift) if high else (row < k)
        coefs[k] = jnp.where(keep, w[k], 0.0)
    start = cy - REACH if high else 0
    for i in range(cx // 2):
        m = recv[i, :, :]
        total = w[REACH] * m
        for k in range(1, REACH):
            shift = REACH - k
            total = total + coefs[k] * pltpu.roll(m, shift if high else 8 - shift, 0)
        for h in range(2):
            rows = slice(start, start + REACH)
            nxt[2 * i + h, rows, :] = (
                nxt[2 * i + h, rows, :] + c2[2 * i + h, rows, :] * total[REACH * h : REACH * h + REACH, :]
            )


def add_x_halo(nxt, c2, recv, high):
    cx, cy, nz = nxt.shape
    w = LAPLACE_COEFS
    half = cy // 8
    for r in range(REACH):
        x = cx - 1 - r if high else r
        for h in range(half):
            total = None
            for k in range(r + 1, REACH + 1):
                row = (k - r - 1) if high else (REACH + r - k)
                term = w[k] * recv[row * half + h, :, :]
                total = term if total is None else total + term
            ys = slice(8 * h, 8 * h + 8)
            nxt[x, ys, :] = nxt[x, ys, :] + c2[x, ys, :] * total


def add_halos(nxt, c2, gx_index, gy_index, ye, yo, xe, xo):
    for index, even, odd, add in ((gy_index, ye, yo, add_y_halo), (gx_index, xe, xo, add_x_halo)):
        is_even = index % 2 == 0

        @pl.when(is_even)
        def _(even=even, odd=odd, add=add):
            add(nxt, c2, even, True)
            if odd is not None:
                add(nxt, c2, odd, False)

        @pl.when(jnp.logical_not(is_even))
        def _(even=even, odd=odd, add=add):
            add(nxt, c2, even, False)
            if odd is not None:
                add(nxt, c2, odd, True)


def first_faces_kernel(cur, tr, ye, yo, xe, own, *, with_yo):
    gx_index, gy_index = lax.axis_index("gx"), lax.axis_index("gy")
    put_faces(cur, gx_index, gy_index, ye, yo if with_yo else None, xe, None)
    steps, per = tr.shape
    last = ye.shape[0] - 1
    ye[last, :, :] = jnp.zeros(ye.shape[1:], F32)
    ye[last, 0:steps, 0:per] = tr[...].astype(F32)
    own[...] = jnp.zeros(own.shape, F32)
    own[0, 0:steps, 0:per] = tr[...].astype(F32)


def prepare_kernel(col, toeplitz, select):
    nz = toeplitz.shape[1]
    distance = jnp.abs(
        lax.broadcasted_iota(jnp.int32, (nz, nz), 0) - lax.broadcasted_iota(jnp.int32, (nz, nz), 1)
    )
    band = jnp.where(distance == 0, 3.0 * LAPLACE_COEFS[0], 0.0)
    for k in range(1, REACH + 1):
        band = band + jnp.where(distance == k, LAPLACE_COEFS[k], 0.0)
    hi, lo = split2(band)
    toeplitz[0:nz, :] = hi
    toeplitz[nz : 2 * nz, :] = lo
    wide = jnp.concatenate([col[...]] * 3, axis=1)
    rows = lax.broadcasted_iota(jnp.int32, select.shape, 0)
    select[...] = jnp.where(rows == wide, 1.0, 0.0).astype(BF16)


def update(cur, prev, c2, toeplitz, out, ypad, source=None, fine=None):
    cx, cy, nz = cur.shape
    w = LAPLACE_COEFS
    zero = jnp.zeros((8, nz), F32)
    for x in range(cx):
        ypad[x, 0:8, :] = zero
        ypad[x, 8 : 8 + cy, :] = cur[x, :, :]
        ypad[x, 8 + cy : 16 + cy, :] = zero
    chunk = 8
    rows = chunk * cy
    t_hi = toeplitz[0:nz, :]
    t_lo = toeplitz[nz : 2 * nz, :]
    for m in range(cx // chunk):
        v = cur[m * chunk : (m + 1) * chunk, :, :].reshape(rows, nz)
        hi, lo = split2(v)
        lz = dot(hi, t_hi) + dot(lo, t_hi) + dot(hi, t_lo)
        if source is not None:
            select, contrib = source
            src = dot(select[m * rows : (m + 1) * rows, :], contrib)
        for j in range(chunk):
            x = m * chunk + j
            total = lz[j * cy : (j + 1) * cy, :]
            for k in range(1, REACH + 1):
                pair = ypad[x, 8 - k : 8 - k + cy, :] + ypad[x, 8 + k : 8 + k + cy, :]
                if x - k >= 0:
                    pair = pair + cur[x - k, :, :]
                if x + k < cx:
                    pair = pair + cur[x + k, :, :]
                total = total + w[k] * pair
            here = cur[x, :, :]
            value = (2.0 * here - prev[x, :, :]) + c2[x, :, :] * total
            if source is not None:
                value = value + src[j * cy : (j + 1) * cy, :]
            out[x, :, :] = value
            if fine is not None:
                fine_in, accel, fine_out = fine
                term = accel[x, :, :].astype(F32) * here
                fine_out[x, :, :] = term if fine_in is None else fine_in[x, :, :] + term


def first_update_kernel(cur, prev, c2, toeplitz, out, ypad):
    update(cur, prev, c2, toeplitz, out, ypad)


def update_kernel(cur, prev, c2, toeplitz, select, contrib, accel, *rest, step):
    if step == 1:
        out, fine_out, ypad = rest
        fine_in = None
    else:
        fine_in, out, fine_out, ypad = rest
    update(
        cur, prev, c2, toeplitz, out, ypad,
        source=(select, contrib[step]), fine=(fine_in, accel.at[step - 1], fine_out),
    )


def contributions(counts, rb, weights, blocks, patterns, contrib, wide, me, per):
    slots, rblk, nz = weights.shape
    steps = contrib.shape[0]
    lanes = 128
    each = per // rblk
    eye = lax.broadcasted_iota(jnp.int32, (slots, slots), 0) == lax.broadcasted_iota(jnp.int32, (slots, slots), 1)
    block_of = jnp.sum(jnp.where(eye, jnp.broadcast_to(rb[...], (slots, slots)), 0), axis=1, keepdims=True)
    owner = lax.div(block_of, jnp.int32(each))
    group = block_of - owner * each
    live = lax.broadcasted_iota(jnp.int32, (slots, 1), 0) < counts[0, 0]
    relative = jnp.where(live, jnp.bitwise_xor(owner, me), -1)
    lane = lax.broadcasted_iota(jnp.int32, (slots, lanes), 1)
    fits = lax.div(lane, jnp.int32(rblk)) == group
    picked = [jnp.zeros((slots, lanes), F32) for _ in range(steps)]
    for tile, pattern in zip(blocks, patterns):
        mask = jnp.logical_and(fits, relative == pattern)
        for t in range(steps):
            picked[t] = jnp.where(mask, tile[t : t + 1, :], picked[t])
    spread = (
        lax.rem(lax.broadcasted_iota(jnp.int32, (lanes, lanes), 0), jnp.int32(rblk))
        == lax.rem(lax.broadcasted_iota(jnp.int32, (lanes, lanes), 1), jnp.int32(rblk))
    )
    spread = jnp.where(spread, 1.0, 0.0).astype(BF16)
    tiled = [dot(p.astype(BF16), spread) for p in picked]
    together = lanes // rblk
    diagonal = lax.broadcasted_iota(jnp.int32, (together, lanes), 0) == lax.div(
        lax.broadcasted_iota(jnp.int32, (together, lanes), 1), jnp.int32(rblk)
    )
    for q in range(slots // together):
        rows = slice(q * together, (q + 1) * together)
        left = jnp.concatenate([jnp.where(diagonal, v[rows, :], 0.0) for v in tiled], axis=0).astype(BF16)
        right = weights[q * together : (q + 1) * together, :, :].reshape(together * rblk, nz)
        got = dot(left, right)
        for t in range(steps):
            wide[t, rows, :] = got[t * together : (t + 1) * together, :]
    for t in range(steps):
        hi, mid = split2(wide[t, :, :])
        rest = wide[t, :, :] - hi.astype(F32) - mid.astype(F32)
        contrib[t, 0:slots, :] = hi
        contrib[t, slots : 2 * slots, :] = mid
        contrib[t, 2 * slots : 3 * slots, :] = rest.astype(BF16)


def unpack(refs, with_yo, with_xo):
    refs = list(refs)
    ye = refs.pop(0)
    yo = refs.pop(0) if with_yo else None
    xe = refs.pop(0)
    xo = refs.pop(0) if with_xo else None
    return ye, yo, xe, xo, refs


def first_correct_kernel(counts, rb, weights, select, part, c2, own, *refs, with_yo, with_xo, hops, patterns, per):
    gx_index, gy_index = lax.axis_index("gx"), lax.axis_index("gy")
    ny = lax.axis_size("gy")
    ye, yo, xe, xo, refs = unpack(refs, with_yo, with_xo)
    late, refs = refs[:hops], refs[hops:]
    nxt, contrib, refs = refs[0], refs[1], refs[2:]
    oye, oyo, oxe, oxo, refs = unpack(refs, with_yo, with_xo)
    wide = refs[0]
    lanes = 128
    tiles = [own[0], ye[ye.shape[0] - 1][:, 0:lanes]]
    last = xe.shape[0] - 1
    tiles += [xe[last][:, 0:lanes], xe[last][:, lanes : 2 * lanes]]
    for ref in late:
        for i in range(ref.shape[0]):
            tiles += [ref[i][:, 0:lanes], ref[i][:, lanes : 2 * lanes]]
    contributions(counts, rb, weights, tiles, patterns, contrib, wide, gx_index * ny + gy_index, per)
    cx, cy, nz = nxt.shape
    chunk = 8
    rows = chunk * cy
    for m in range(cx // chunk):
        src = dot(select[m * rows : (m + 1) * rows, :], contrib[0])
        at = slice(m * chunk, (m + 1) * chunk)
        nxt[at, :, :] = part[at, :, :] + src.reshape(chunk, cy, nz)
    add_halos(nxt, c2, gx_index, gy_index, ye, yo, xe, xo)
    put_faces(nxt, gx_index, gy_index, oye, oyo, oxe, oxo)


def correct_kernel(part, c2, *refs, with_yo, with_xo):
    gx_index, gy_index = lax.axis_index("gx"), lax.axis_index("gy")
    ye, yo, xe, xo, refs = unpack(refs, with_yo, with_xo)
    nxt, refs = refs[0], refs[1:]
    oye, oyo, oxe, oxo, refs = unpack(refs, with_yo, with_xo)
    nxt[...] = part[...]
    add_halos(nxt, c2, gx_index, gy_index, ye, yo, xe, xo)
    put_faces(nxt, gx_index, gy_index, oye, oyo, oxe, oxo)


def last_kernel(part, c2, accel, fine, *refs, with_yo, with_xo, step):
    gx_index, gy_index = lax.axis_index("gx"), lax.axis_index("gy")
    ye, yo, xe, xo, refs = unpack(refs, with_yo, with_xo)
    nxt, coarse, middle = refs
    cx, cy, nz = nxt.shape
    nxt[...] = part[...]
    add_halos(nxt, c2, gx_index, gy_index, ye, yo, xe, xo)
    pairs = lax.div(lax.broadcasted_iota(jnp.int32, (nz, nz // 2), 0), jnp.int32(2)) == lax.broadcasted_iota(
        jnp.int32, (nz, nz // 2), 1
    )
    pairs = jnp.where(pairs, 0.125, 0.0).astype(BF16)
    chunk = 8
    for m in range(cx // (2 * chunk)):
        summed = []
        for j in range(chunk):
            x = 2 * (m * chunk + j)
            a = fine[x, :, :] + accel[step, x, :, :].astype(F32) * nxt[x, :, :]
            b = fine[x + 1, :, :] + accel[step, x + 1, :, :].astype(F32) * nxt[x + 1, :, :]
            summed.append(a + b)
        hi, lo = split2(jnp.concatenate(summed, axis=0))
        got = dot(hi, pairs) + dot(lo, pairs)
        middle[m * chunk * cy : (m + 1) * chunk * cy, :] = got
    half = cx * cy // 4
    both = middle[pl.ds(0, half, 2), :] + middle[pl.ds(1, half, 2), :]
    coarse[...] = both.reshape(coarse.shape)


def local(adj_prev, adj_cur, fwd_accel, courant2, traces, weights, rblock, column, counts):
    prev, cur, accel = adj_prev[0], adj_cur[0], fwd_accel[0]
    cx, cy, nz = cur.shape
    steps = accel.shape[0]
    slots = weights.shape[2]
    per = traces.shape[2]
    nx, ny, nshot = lax.axis_size("gx"), lax.axis_size("gy"), lax.axis_size("shot")
    with_yo, with_xo = ny > 2, nx > 2
    y_msg, x_msg = (cx // 2, 8, nz), (REACH * cy // 8, 8, nz)
    cells = cx * cy * nz

    ye, yo, xe, own = vmem_call(
        functools.partial(first_faces_kernel, with_yo=with_yo),
        [sds((y_msg[0] + 1,) + y_msg[1:]), sds(y_msg), sds(x_msg), sds((1, 8, nz // 2))],
        [cur, traces[0]],
        name="first_faces",
    )

    def exchange(ye, yo, xe, xo):
        return (
            lax.ppermute(xe, "gx", even_pairs(nx)),
            lax.ppermute(xo, "gx", odd_pairs(nx)) if with_xo else None,
            lax.ppermute(ye, "gy", even_pairs(ny)),
            lax.ppermute(yo, "gy", odd_pairs(ny)) if with_yo else None,
        )

    rye = lax.ppermute(ye, "gy", even_pairs(ny))
    ryo = lax.ppermute(yo, "gy", odd_pairs(ny)) if with_yo else None
    pair = jnp.concatenate([own, rye[cx // 2 :, :, 0 : nz // 2]], axis=2)
    rxe = lax.ppermute(jnp.concatenate([xe, pair], axis=0), "gx", even_pairs(nx))
    rxo = None
    if with_xo:
        half = cy // 8
        low = cur[0:REACH].reshape(x_msg)
        high = cur[cx - REACH :].reshape(x_msg)
        rxo = lax.ppermute(jnp.where(lax.axis_index("gx") % 2 == 0, low, high), "gx", odd_pairs(nx))
    patterns = [0, 1, ny, ny + 1]
    held = jnp.concatenate([pair, rxe[x_msg[0] :]], axis=0)
    late = []
    for axis, size, stride in (("gy", ny, 1), ("gx", nx, ny)):
        bit = 2
        while bit < size:
            swap = [(i, i ^ bit) for i in range(size)]
            got = lax.ppermute(held, axis, swap)
            late.append(got)
            patterns = patterns + [p ^ (bit * stride) for p in patterns]
            held = jnp.concatenate([held, got], axis=0)
            bit *= 2

    toeplitz, select = vmem_call(
        prepare_kernel,
        [sds((2 * nz, nz), BF16), sds((cx * cy, 3 * slots), BF16)],
        [column[0]],
        name="prepare",
    )
    ypad = pltpu.VMEM((cx, cy + 16, nz), F32)
    part = vmem_call(
        first_update_kernel, [sds(cur.shape)], [cur, prev, courant2, toeplitz], [ypad],
        flops=cells * 60, name="update_0",
    )[0]

    def given(ye, yo, xe, xo):
        return [a for a in (ye, yo, xe, xo) if a is not None]

    def face_shapes():
        return given(sds(y_msg), sds(y_msg) if with_yo else None, sds(x_msg), sds(x_msg) if with_xo else None)

    def taken(faces):
        faces = list(faces)
        ye = faces.pop(0)
        yo = faces.pop(0) if with_yo else None
        xe = faces.pop(0)
        xo = faces.pop(0) if with_xo else None
        return ye, yo, xe, xo

    nxt, contrib, *faces = vmem_call(
        functools.partial(
            first_correct_kernel, with_yo=with_yo, with_xo=with_xo, hops=len(late), patterns=tuple(patterns), per=per
        ),
        [sds(cur.shape), sds((steps, 3 * slots, nz), BF16)] + face_shapes(),
        [counts, rblock[0], weights[0, 0], select, part, courant2, own] + given(rye, ryo, rxe, rxo) + late,
        [pltpu.VMEM((steps, slots, nz), F32)],
        smem=(0,),
        name="correct_0",
    )
    previous, current = cur, nxt
    fine = None
    for step in range(1, steps):
        rxe, rxo, rye, ryo = exchange(*taken(faces))
        args = [current, previous, courant2, toeplitz, select, contrib, accel]
        if fine is not None:
            args.append(fine)
        part, fine = vmem_call(
            functools.partial(update_kernel, step=step), [sds(cur.shape), sds(cur.shape)], args, [ypad],
            flops=cells * 60, name=f"update_{step}",
        )
        halos = given(rye, ryo, rxe, rxo)
        if step < steps - 1:
            nxt, *faces = vmem_call(
                functools.partial(correct_kernel, with_yo=with_yo, with_xo=with_xo),
                [sds(cur.shape)] + face_shapes(),
                [part, courant2] + halos,
                name=f"correct_{step}",
            )
        else:
            nxt, coarse = vmem_call(
                functools.partial(last_kernel, with_yo=with_yo, with_xo=with_xo, step=step),
                [sds(cur.shape), sds((cx // 2, cy // 2, nz // 2))],
                [part, courant2, accel, fine] + halos,
                [pltpu.VMEM((cx * cy // 2, nz // 2), F32)],
                name="correct_last",
            )
        previous, current = current, nxt
    bit = 1
    while bit < nshot:
        coarse = coarse + lax.ppermute(coarse, "shot", [(i, i ^ bit) for i in range(nshot)])
        bit *= 2
    return (previous[None], current[None], coarse)


def solution(mesh):
    return jax.shard_map(
        local,
        mesh=mesh,
        in_specs=(
            P("shot", "gx", "gy", None),
            P("shot", "gx", "gy", None),
            P("shot", None, "gx", "gy", None),
            P("gx", "gy", None),
            P("shot", None, ("gx", "gy")),
            P("gx", "gy", None, None, None),
            P("gx", "gy", None),
            P("gx", "gy", None),
            P("gx", "gy"),
        ),
        out_specs=(P("shot", "gx", "gy", None), P("shot", "gx", "gy", None), P("gx", "gy", None)),
        check_vma=False,
    )
```

```python
import functools

import jax
import jax.numpy as jnp
from jax import lax
from jax.experimental import pallas as pl
from jax.experimental.pallas import tpu as pltpu
from jax.sharding import PartitionSpec as P

LAPLACE_COEFS = (-205.0 / 72.0, 8.0 / 5.0, -1.0 / 5.0, 8.0 / 315.0, -1.0 / 560.0)
REACH = 4
VMEM_LIMIT = 16 << 20
F32 = jnp.float32
BF16 = jnp.bfloat16


def vmem_call(kernel, outs, args, scratch=(), aliases=None, flops=0, smem=(), name=None):
    in_specs = [pl.BlockSpec(memory_space=pltpu.SMEM if i in smem else pltpu.VMEM) for i in range(len(args))]
    moved = sum(a.size * a.dtype.itemsize for a in args) + sum(o.size * o.dtype.itemsize for o in outs)
    return pl.pallas_call(
        kernel,
        out_shape=tuple(outs),
        in_specs=in_specs,
        out_specs=tuple(pl.BlockSpec(memory_space=pltpu.VMEM) for _ in outs),
        scratch_shapes=list(scratch),
        input_output_aliases=aliases or {},
        cost_estimate=pl.CostEstimate(flops=flops, bytes_accessed=moved, transcendentals=0),
        compiler_params=pltpu.CompilerParams(vmem_limit_bytes=VMEM_LIMIT),
        name=name,
    )(*args)


def sds(shape, dtype=F32):
    return jax.ShapeDtypeStruct(shape, dtype)


def even_pairs(n):
    pairs = []
    for i in range(0, n - 1, 2):
        pairs += [(i, i + 1), (i + 1, i)]
    return pairs


def odd_pairs(n):
    pairs = []
    for i in range(1, n - 1, 2):
        pairs += [(i, i + 1), (i + 1, i)]
    return pairs


def split2(v):
    hi = v.astype(BF16)
    return hi, (v - hi.astype(F32)).astype(BF16)


def dot(a, b):
    return jnp.dot(a, b, preferred_element_type=F32)


def put_y_face(cur, out, high):
    cx, cy, _ = cur.shape
    start = cy - REACH if high else 0
    for i in range(cx // 2):
        out[i, 0:REACH, :] = cur[2 * i, start : start + REACH, :]
        out[i, REACH : 2 * REACH, :] = cur[2 * i + 1, start : start + REACH, :]


def put_faces(cur, gx_index, gy_index, ye, yo, xe, xo):
    cx, cy, _ = cur.shape
    y_even = gy_index % 2 == 0
    x_even = gx_index % 2 == 0

    @pl.when(y_even)
    def _():
        put_y_face(cur, ye, True)
        if yo is not None:
            put_y_face(cur, yo, False)

    @pl.when(jnp.logical_not(y_even))
    def _():
        put_y_face(cur, ye, False)
        if yo is not None:
            put_y_face(cur, yo, True)

    half = cy // 8
    low = jnp.where(x_even, cx - REACH, 0)
    for r in range(REACH):
        for h in range(half):
            xe[r * half + h, :, :] = cur[low + r, 8 * h : 8 * h + 8, :]
            if xo is not None:
                xo[r * half + h, :, :] = cur[cx - REACH - low + r, 8 * h : 8 * h + 8, :]


def add_y_halo(nxt, c2, recv, high):
    cx, cy, nz = nxt.shape
    w = LAPLACE_COEFS
    row = lax.broadcasted_iota(jnp.int32, (8, nz), 0) % REACH
    coefs = {}
    for k in range(1, REACH + 1):
        shift = REACH - k
        keep = (row >= shift) if high else (row < k)
        coefs[k] = jnp.where(keep, w[k], 0.0)
    start = cy - REACH if high else 0
    for i in range(cx // 2):
        m = recv[i, :, :]
        total = w[REACH] * m
        for k in range(1, REACH):
            shift = REACH - k
            total = total + coefs[k] * pltpu.roll(m, shift if high else 8 - shift, 0)
        for h in range(2):
            rows = slice(start, start + REACH)
            nxt[2 * i + h, rows, :] = (
                nxt[2 * i + h, rows, :] + c2[2 * i + h, rows, :] * total[REACH * h : REACH * h + REACH, :]
            )


def add_x_halo(nxt, c2, recv, high):
    cx, cy, nz = nxt.shape
    w = LAPLACE_COEFS
    half = cy // 8
    for r in range(REACH):
        x = cx - 1 - r if high else r
        for h in range(half):
            total = None
            for k in range(r + 1, REACH + 1):
                row = (k - r - 1) if high else (REACH + r - k)
                term = w[k] * recv[row * half + h, :, :]
                total = term if total is None else total + term
            ys = slice(8 * h, 8 * h + 8)
            nxt[x, ys, :] = nxt[x, ys, :] + c2[x, ys, :] * total


def add_halos(nxt, c2, gx_index, gy_index, ye, yo, xe, xo):
    for index, even, odd, add in ((gy_index, ye, yo, add_y_halo), (gx_index, xe, xo, add_x_halo)):
        is_even = index % 2 == 0

        @pl.when(is_even)
        def _(even=even, odd=odd, add=add):
            add(nxt, c2, even, True)
            if odd is not None:
                add(nxt, c2, odd, False)

        @pl.when(jnp.logical_not(is_even))
        def _(even=even, odd=odd, add=add):
            add(nxt, c2, even, False)
            if odd is not None:
                add(nxt, c2, odd, True)


def first_faces_kernel(cur, tr, ye, yo, xe, own, *, with_yo):
    gx_index, gy_index = lax.axis_index("gx"), lax.axis_index("gy")
    put_faces(cur, gx_index, gy_index, ye, yo if with_yo else None, xe, None)
    steps, per = tr.shape
    last = ye.shape[0] - 1
    ye[last, :, :] = jnp.zeros(ye.shape[1:], F32)
    ye[last, 0:steps, 0:per] = tr[...].astype(F32)
    own[...] = jnp.zeros(own.shape, F32)
    own[0, 0:steps, 0:per] = tr[...].astype(F32)


def prepare_kernel(col, toeplitz, select):
    nz = toeplitz.shape[1]
    distance = jnp.abs(
        lax.broadcasted_iota(jnp.int32, (nz, nz), 0) - lax.broadcasted_iota(jnp.int32, (nz, nz), 1)
    )
    band = jnp.where(distance == 0, 3.0 * LAPLACE_COEFS[0], 0.0)
    for k in range(1, REACH + 1):
        band = band + jnp.where(distance == k, LAPLACE_COEFS[k], 0.0)
    hi, lo = split2(band)
    toeplitz[0:nz, :] = hi
    toeplitz[nz : 2 * nz, :] = lo
    wide = jnp.concatenate([col[...]] * 3, axis=1)
    rows = lax.broadcasted_iota(jnp.int32, select.shape, 0)
    select[...] = jnp.where(rows == wide, 1.0, 0.0).astype(BF16)


def update(cur, prev, c2, toeplitz, out, ypad, source=None, fine=None):
    cx, cy, nz = cur.shape
    w = LAPLACE_COEFS
    zero = jnp.zeros((8, nz), F32)
    for x in range(cx):
        ypad[x, 0:8, :] = zero
        ypad[x, 8 : 8 + cy, :] = cur[x, :, :]
        ypad[x, 8 + cy : 16 + cy, :] = zero
    chunk = 8
    rows = chunk * cy
    t_hi = toeplitz[0:nz, :]
    t_lo = toeplitz[nz : 2 * nz, :]
    for m in range(cx // chunk):
        v = cur[m * chunk : (m + 1) * chunk, :, :].reshape(rows, nz)
        hi, lo = split2(v)
        lz = dot(hi, t_hi) + dot(lo, t_hi) + dot(hi, t_lo)
        if source is not None:
            select, contrib = source
            src = dot(select[m * rows : (m + 1) * rows, :], contrib)
        for j in range(chunk):
            x = m * chunk + j
            total = lz[j * cy : (j + 1) * cy, :]
            for k in range(1, REACH + 1):
                pair = ypad[x, 8 - k : 8 - k + cy, :] + ypad[x, 8 + k : 8 + k + cy, :]
                if x - k >= 0:
                    pair = pair + cur[x - k, :, :]
                if x + k < cx:
                    pair = pair + cur[x + k, :, :]
                total = total + w[k] * pair
            here = cur[x, :, :]
            value = (2.0 * here - prev[x, :, :]) + c2[x, :, :] * total
            if source is not None:
                value = value + src[j * cy : (j + 1) * cy, :]
            out[x, :, :] = value
            if fine is not None:
                fine_in, accel, fine_out = fine
                term = accel[x, :, :].astype(F32) * here
                fine_out[x, :, :] = term if fine_in is None else fine_in[x, :, :] + term


def first_update_kernel(cur, prev, c2, toeplitz, out, ypad):
    update(cur, prev, c2, toeplitz, out, ypad)


def update_kernel(cur, prev, c2, toeplitz, select, contrib, accel, *rest, step):
    if step == 1:
        out, fine_out, ypad = rest
        fine_in = None
    else:
        fine_in, out, fine_out, ypad = rest
    update(
        cur, prev, c2, toeplitz, out, ypad,
        source=(select, contrib[step]), fine=(fine_in, accel.at[step - 1], fine_out),
    )


def contributions(counts, rb, weights, blocks, patterns, contrib, wide, me, per):
    slots, rblk, nz = weights.shape
    steps = contrib.shape[0]
    lanes = 128
    each = per // rblk
    eye = lax.broadcasted_iota(jnp.int32, (slots, slots), 0) == lax.broadcasted_iota(jnp.int32, (slots, slots), 1)
    block_of = jnp.sum(jnp.where(eye, jnp.broadcast_to(rb[...], (slots, slots)), 0), axis=1, keepdims=True)
    owner = lax.div(block_of, jnp.int32(each))
    group = block_of - owner * each
    live = lax.broadcasted_iota(jnp.int32, (slots, 1), 0) < counts[0, 0]
    relative = jnp.where(live, jnp.bitwise_xor(owner, me), -1)
    lane = lax.broadcasted_iota(jnp.int32, (slots, lanes), 1)
    fits = lax.div(lane, jnp.int32(rblk)) == group
    picked = [jnp.zeros((slots, lanes), F32) for _ in range(steps)]
    for tile, pattern in zip(blocks, patterns):
        mask = jnp.logical_and(fits, relative == pattern)
        for t in range(steps):
            picked[t] = jnp.where(mask, tile[t : t + 1, :], picked[t])
    spread = (
        lax.rem(lax.broadcasted_iota(jnp.int32, (lanes, lanes), 0), jnp.int32(rblk))
        == lax.rem(lax.broadcasted_iota(jnp.int32, (lanes, lanes), 1), jnp.int32(rblk))
    )
    spread = jnp.where(spread, 1.0, 0.0).astype(BF16)
    tiled = [dot(p.astype(BF16), spread) for p in picked]
    together = lanes // rblk
    diagonal = lax.broadcasted_iota(jnp.int32, (together, lanes), 0) == lax.div(
        lax.broadcasted_iota(jnp.int32, (together, lanes), 1), jnp.int32(rblk)
    )
    for q in range(slots // together):
        rows = slice(q * together, (q + 1) * together)
        left = jnp.concatenate([jnp.where(diagonal, v[rows, :], 0.0) for v in tiled], axis=0).astype(BF16)
        right = weights[q * together : (q + 1) * together, :, :].reshape(together * rblk, nz)
        got = dot(left, right)
        for t in range(steps):
            wide[t, rows, :] = got[t * together : (t + 1) * together, :]
    for t in range(steps):
        hi, mid = split2(wide[t, :, :])
        rest = wide[t, :, :] - hi.astype(F32) - mid.astype(F32)
        contrib[t, 0:slots, :] = hi
        contrib[t, slots : 2 * slots, :] = mid
        contrib[t, 2 * slots : 3 * slots, :] = rest.astype(BF16)


def unpack(refs, with_yo, with_xo):
    refs = list(refs)
    ye = refs.pop(0)
    yo = refs.pop(0) if with_yo else None
    xe = refs.pop(0)
    xo = refs.pop(0) if with_xo else None
    return ye, yo, xe, xo, refs


def first_correct_kernel(counts, rb, weights, select, part, c2, own, *refs, with_yo, with_xo, hops, patterns, per):
    gx_index, gy_index = lax.axis_index("gx"), lax.axis_index("gy")
    ny = lax.axis_size("gy")
    ye, yo, xe, xo, refs = unpack(refs, with_yo, with_xo)
    late, refs = refs[:hops], refs[hops:]
    nxt, contrib, refs = refs[0], refs[1], refs[2:]
    oye, oyo, oxe, oxo, refs = unpack(refs, with_yo, with_xo)
    wide = refs[0]
    lanes = 128
    tiles = [own[0], ye[ye.shape[0] - 1][:, 0:lanes]]
    last = xe.shape[0] - 1
    tiles += [xe[last][:, 0:lanes], xe[last][:, lanes : 2 * lanes]]
    for ref in late:
        for i in range(ref.shape[0]):
            tiles += [ref[i][:, 0:lanes], ref[i][:, lanes : 2 * lanes]]
    contributions(counts, rb, weights, tiles, patterns, contrib, wide, gx_index * ny + gy_index, per)
    cx, cy, nz = nxt.shape
    chunk = 8
    rows = chunk * cy
    for m in range(cx // chunk):
        src = dot(select[m * rows : (m + 1) * rows, :], contrib[0])
        at = slice(m * chunk, (m + 1) * chunk)
        nxt[at, :, :] = part[at, :, :] + src.reshape(chunk, cy, nz)
    add_halos(nxt, c2, gx_index, gy_index, ye, yo, xe, xo)
    put_faces(nxt, gx_index, gy_index, oye, oyo, oxe, oxo)


def correct_kernel(part, c2, *refs, with_yo, with_xo):
    gx_index, gy_index = lax.axis_index("gx"), lax.axis_index("gy")
    ye, yo, xe, xo, refs = unpack(refs, with_yo, with_xo)
    nxt, refs = refs[0], refs[1:]
    oye, oyo, oxe, oxo, refs = unpack(refs, with_yo, with_xo)
    nxt[...] = part[...]
    add_halos(nxt, c2, gx_index, gy_index, ye, yo, xe, xo)
    put_faces(nxt, gx_index, gy_index, oye, oyo, oxe, oxo)


def last_kernel(part, c2, accel, fine, *refs, with_yo, with_xo, step):
    gx_index, gy_index = lax.axis_index("gx"), lax.axis_index("gy")
    ye, yo, xe, xo, refs = unpack(refs, with_yo, with_xo)
    nxt, coarse, middle = refs
    cx, cy, nz = nxt.shape
    nxt[...] = part[...]
    add_halos(nxt, c2, gx_index, gy_index, ye, yo, xe, xo)
    pairs = lax.div(lax.broadcasted_iota(jnp.int32, (nz, nz // 2), 0), jnp.int32(2)) == lax.broadcasted_iota(
        jnp.int32, (nz, nz // 2), 1
    )
    pairs = jnp.where(pairs, 0.125, 0.0).astype(BF16)
    chunk = 8
    for m in range(cx // (2 * chunk)):
        summed = []
        for j in range(chunk):
            x = 2 * (m * chunk + j)
            a = fine[x, :, :] + accel[step, x, :, :].astype(F32) * nxt[x, :, :]
            b = fine[x + 1, :, :] + accel[step, x + 1, :, :].astype(F32) * nxt[x + 1, :, :]
            summed.append(a + b)
        hi, lo = split2(jnp.concatenate(summed, axis=0))
        got = dot(hi, pairs) + dot(lo, pairs)
        middle[m * chunk * cy : (m + 1) * chunk * cy, :] = got
    half = cx * cy // 4
    both = middle[pl.ds(0, half, 2), :] + middle[pl.ds(1, half, 2), :]
    coarse[...] = both.reshape(coarse.shape)


def local(adj_prev, adj_cur, fwd_accel, courant2, traces, weights, rblock, column, counts):
    prev, cur, accel = adj_prev[0], adj_cur[0], fwd_accel[0]
    cx, cy, nz = cur.shape
    steps = accel.shape[0]
    slots = weights.shape[2]
    per = traces.shape[2]
    nx, ny, nshot = lax.axis_size("gx"), lax.axis_size("gy"), lax.axis_size("shot")
    with_yo, with_xo = ny > 2, nx > 2
    y_msg, x_msg = (cx // 2, 8, nz), (REACH * cy // 8, 8, nz)
    cells = cx * cy * nz

    ye, yo, xe, own = vmem_call(
        functools.partial(first_faces_kernel, with_yo=with_yo),
        [sds((y_msg[0] + 1,) + y_msg[1:]), sds(y_msg), sds(x_msg), sds((1, 8, nz // 2))],
        [cur, traces[0]],
        name="first_faces",
    )

    def exchange(ye, yo, xe, xo):
        return (
            lax.ppermute(xe, "gx", even_pairs(nx)),
            lax.ppermute(xo, "gx", odd_pairs(nx)) if with_xo else None,
            lax.ppermute(ye, "gy", even_pairs(ny)),
            lax.ppermute(yo, "gy", odd_pairs(ny)) if with_yo else None,
        )

    rye = lax.ppermute(ye, "gy", even_pairs(ny))
    ryo = lax.ppermute(yo, "gy", odd_pairs(ny)) if with_yo else None
    pair = jnp.concatenate([own, rye[cx // 2 :, :, 0 : nz // 2]], axis=2)
    rxe = lax.ppermute(jnp.concatenate([xe, pair], axis=0), "gx", even_pairs(nx))
    rxo = None
    if with_xo:
        half = cy // 8
        low = cur[0:REACH].reshape(x_msg)
        high = cur[cx - REACH :].reshape(x_msg)
        rxo = lax.ppermute(jnp.where(lax.axis_index("gx") % 2 == 0, low, high), "gx", odd_pairs(nx))
    patterns = [0, 1, ny, ny + 1]
    held = jnp.concatenate([pair, rxe[x_msg[0] :]], axis=0)
    late = []
    for axis, size, stride in (("gy", ny, 1), ("gx", nx, ny)):
        bit = 2
        while bit < size:
            swap = [(i, i ^ bit) for i in range(size)]
            got = lax.ppermute(held, axis, swap)
            late.append(got)
            patterns = patterns + [p ^ (bit * stride) for p in patterns]
            held = jnp.concatenate([held, got], axis=0)
            bit *= 2

    toeplitz, select = vmem_call(
        prepare_kernel,
        [sds((2 * nz, nz), BF16), sds((cx * cy, 3 * slots), BF16)],
        [column[0]],
        name="prepare",
    )
    ypad = pltpu.VMEM((cx, cy + 16, nz), F32)
    part = vmem_call(
        first_update_kernel, [sds(cur.shape)], [cur, prev, courant2, toeplitz], [ypad],
        flops=cells * 60, name="update_0",
    )[0]

    def given(ye, yo, xe, xo):
        return [a for a in (ye, yo, xe, xo) if a is not None]

    def face_shapes():
        return given(sds(y_msg), sds(y_msg) if with_yo else None, sds(x_msg), sds(x_msg) if with_xo else None)

    def taken(faces):
        faces = list(faces)
        ye = faces.pop(0)
        yo = faces.pop(0) if with_yo else None
        xe = faces.pop(0)
        xo = faces.pop(0) if with_xo else None
        return ye, yo, xe, xo

    nxt, contrib, *faces = vmem_call(
        functools.partial(
            first_correct_kernel, with_yo=with_yo, with_xo=with_xo, hops=len(late), patterns=tuple(patterns), per=per
        ),
        [sds(cur.shape), sds((steps, 3 * slots, nz), BF16)] + face_shapes(),
        [counts, rblock[0], weights[0, 0], select, part, courant2, own] + given(rye, ryo, rxe, rxo) + late,
        [pltpu.VMEM((steps, slots, nz), F32)],
        smem=(0,),
        name="correct_0",
    )
    previous, current = cur, nxt
    fine = None
    for step in range(1, steps):
        rxe, rxo, rye, ryo = exchange(*taken(faces))
        args = [current, previous, courant2, toeplitz, select, contrib, accel]
        if fine is not None:
            args.append(fine)
        part, fine = vmem_call(
            functools.partial(update_kernel, step=step), [sds(cur.shape), sds(cur.shape)], args, [ypad],
            flops=cells * 60, name=f"update_{step}",
        )
        halos = given(rye, ryo, rxe, rxo)
        if step < steps - 1:
            nxt, *faces = vmem_call(
                functools.partial(correct_kernel, with_yo=with_yo, with_xo=with_xo),
                [sds(cur.shape)] + face_shapes(),
                [part, courant2] + halos,
                name=f"correct_{step}",
            )
        else:
            nxt, coarse = vmem_call(
                functools.partial(last_kernel, with_yo=with_yo, with_xo=with_xo, step=step),
                [sds(cur.shape), sds((cx // 2, cy // 2, nz // 2))],
                [part, courant2, accel, fine] + halos,
                [pltpu.VMEM((cx * cy // 2, nz // 2), F32)],
                name="correct_last",
            )
        previous, current = current, nxt
    bit = 1
    while bit < nshot:
        coarse = coarse + lax.ppermute(coarse, "shot", [(i, i ^ bit) for i in range(nshot)])
        bit *= 2
    return (previous[None], current[None], coarse)


def solution(mesh):
    return jax.shard_map(
        local,
        mesh=mesh,
        in_specs=(
            P("shot", "gx", "gy", None),
            P("shot", "gx", "gy", None),
            P("shot", None, "gx", "gy", None),
            P("gx", "gy", None),
            P("shot", None, ("gx", "gy")),
            P("gx", "gy", None, None, None),
            P("gx", "gy", None),
            P("gx", "gy", None),
            P("gx", "gy"),
        ),
        out_specs=(P("shot", "gx", "gy", None), P("shot", "gx", "gy", None), P("gx", "gy", None)),
        check_vma=False,
    )
```

```python
import functools

import jax
import jax.numpy as jnp
from jax import lax
from jax.experimental import pallas as pl
from jax.experimental.pallas import tpu as pltpu
from jax.sharding import PartitionSpec as P


LAPLACE_COEFS = (-205.0 / 72.0, 8.0 / 5.0, -1.0 / 5.0, 8.0 / 315.0, -1.0 / 560.0)
REACH = 4
VMEM_LIMIT = 16 << 20
F32 = jnp.float32
BF16 = jnp.bfloat16


def vmem_call(kernel, outs, args, scratch=(), flops=0, hbm_in=(), hbm_out=(), smem_in=()):
    in_specs = [
        pl.BlockSpec(memory_space=pltpu.HBM if i in hbm_in else pltpu.SMEM if i in smem_in else pltpu.VMEM)
        for i in range(len(args))
    ]
    args = [pltpu.with_memory_space_constraint(a, pltpu.HBM) if i in hbm_in else a for i, a in enumerate(args)]
    moved = sum(a.size * a.dtype.itemsize for a in args) + sum(o.size * o.dtype.itemsize for o in outs)
    return pl.pallas_call(
        kernel,
        out_shape=tuple(outs),
        in_specs=in_specs,
        out_specs=tuple(
            pl.BlockSpec(memory_space=pltpu.HBM if i in hbm_out else pltpu.VMEM) for i in range(len(outs))
        ),
        scratch_shapes=list(scratch),
        cost_estimate=pl.CostEstimate(flops=flops, bytes_accessed=moved, transcendentals=0),
        compiler_params=pltpu.CompilerParams(vmem_limit_bytes=VMEM_LIMIT),
    )(*args)


def sds(shape, dtype=F32):
    return jax.ShapeDtypeStruct(shape, dtype)


def even_pairs(n):
    pairs = []
    for i in range(0, n - 1, 2):
        pairs += [(i, i + 1), (i + 1, i)]
    return pairs


def odd_pairs(n):
    pairs = []
    for i in range(1, n - 1, 2):
        pairs += [(i, i + 1), (i + 1, i)]
    return pairs + [(0, n - 1), (n - 1, 0)]


def split2(v):
    hi = v.astype(BF16)
    return hi, (v - hi.astype(F32)).astype(BF16)


def dot(a, b):
    return jnp.dot(a, b, preferred_element_type=F32)


def put_y_face(cur, out, high):
    cx, cy, _ = cur.shape
    start = cy - REACH if high else 0
    for i in range(cx // 2):
        out[i, 0:REACH, :] = cur[2 * i, start : start + REACH, :]
        out[i, REACH : 2 * REACH, :] = cur[2 * i + 1, start : start + REACH, :]


def put_faces(cur, gx_index, gy_index, ye, yo, xe, xo):
    cx, cy, _ = cur.shape
    y_even = gy_index % 2 == 0
    x_even = gx_index % 2 == 0

    @pl.when(y_even)
    def _():
        put_y_face(cur, ye, True)
        if yo is not None:
            put_y_face(cur, yo, False)

    @pl.when(jnp.logical_not(y_even))
    def _():
        put_y_face(cur, ye, False)
        if yo is not None:
            put_y_face(cur, yo, True)

    half = cy // 8
    low = jnp.where(x_even, cx - REACH, 0)
    for r in range(REACH):
        for h in range(half):
            xe[r * half + h, :, :] = cur[low + r, 8 * h : 8 * h + 8, :]
            if xo is not None:
                xo[r * half + h, :, :] = cur[cx - REACH - low + r, 8 * h : 8 * h + 8, :]


def add_y_halo(nxt, c2, recv, high):
    cx, cy, nz = nxt.shape
    w = LAPLACE_COEFS
    row = lax.broadcasted_iota(jnp.int32, (8, nz), 0) % REACH
    coefs = {}
    for k in range(1, REACH + 1):
        shift = REACH - k
        keep = (row >= shift) if high else (row < k)
        coefs[k] = jnp.where(keep, w[k], 0.0)
    start = cy - REACH if high else 0
    for i in range(cx // 2):
        m = recv[i, :, :]
        total = w[REACH] * m
        for k in range(1, REACH):
            shift = REACH - k
            total = total + coefs[k] * pltpu.roll(m, shift if high else 8 - shift, 0)
        for h in range(2):
            rows = slice(start, start + REACH)
            nxt[2 * i + h, rows, :] = (
                nxt[2 * i + h, rows, :] + c2[2 * i + h, rows, :] * total[REACH * h : REACH * h + REACH, :]
            )


def add_x_halo(nxt, c2, recv, high):
    cx, cy, _ = nxt.shape
    w = LAPLACE_COEFS
    half = cy // 8
    for r in range(REACH):
        x = cx - 1 - r if high else r
        for h in range(half):
            total = None
            for k in range(r + 1, REACH + 1):
                row = (k - r - 1) if high else (REACH + r - k)
                term = w[k] * recv[row * half + h, :, :]
                total = term if total is None else total + term
            ys = slice(8 * h, 8 * h + 8)
            nxt[x, ys, :] = nxt[x, ys, :] + c2[x, ys, :] * total


def add_halos(nxt, c2, gx_index, gy_index, ye, yo, xe, xo):
    for axis, index, even, odd, add in (("gy", gy_index, ye, yo, add_y_halo), ("gx", gx_index, xe, xo, add_x_halo)):
        is_even = index % 2 == 0
        inner = jnp.logical_and(index > 0, index < lax.axis_size(axis) - 1)

        @pl.when(is_even)
        def _(even=even, add=add):
            add(nxt, c2, even, True)

        @pl.when(jnp.logical_not(is_even))
        def _(even=even, add=add):
            add(nxt, c2, even, False)

        if odd is not None:

            @pl.when(jnp.logical_and(inner, is_even))
            def _(odd=odd, add=add):
                add(nxt, c2, odd, False)

            @pl.when(jnp.logical_and(inner, jnp.logical_not(is_even)))
            def _(odd=odd, add=add):
                add(nxt, c2, odd, True)


def load_kernel(
    cur_in, prev_in, c2_in, weights_in, traces_in, col_in, rb_in, counts,
    cur, prev, c2, weights, ye, yo, xe, own, toeplitz, select, owners,
    traces, col, rb, sems,
    *, with_yo, each, rblk,
):
    gx_index, gy_index = lax.axis_index("gx"), lax.axis_index("gy")
    me = gx_index * lax.axis_size("gy") + gy_index
    pairs = (
        (cur_in, cur), (col_in, col), (rb_in, rb), (traces_in, traces), (prev_in, prev), (c2_in, c2), (weights_in, weights),
    )
    copies = [pltpu.make_async_copy(src, dst, sems.at[i]) for i, (src, dst) in enumerate(pairs)]
    for copy in copies:
        copy.start()
    nz = toeplitz.shape[1]
    distance = jnp.abs(
        lax.broadcasted_iota(jnp.int32, (nz, nz), 0) - lax.broadcasted_iota(jnp.int32, (nz, nz), 1)
    )
    band = jnp.where(distance == 0, 3.0 * LAPLACE_COEFS[0], 0.0)
    for k in range(1, REACH + 1):
        band = band + jnp.where(distance == k, LAPLACE_COEFS[k], 0.0)
    hi, lo = split2(band)
    toeplitz[0:nz, :] = hi
    toeplitz[nz : 2 * nz, :] = lo
    for copy in copies[1:4]:
        copy.wait()
    wide = jnp.concatenate([col[...]] * 3, axis=1)
    rows = lax.broadcasted_iota(jnp.int32, select.shape, 0)
    select[...] = jnp.where(rows == wide, 1.0, 0.0).astype(BF16)
    slots, lanes = owners.shape
    eye = lax.broadcasted_iota(jnp.int32, (slots, slots), 0) == lax.broadcasted_iota(jnp.int32, (slots, slots), 1)
    block_of = jnp.sum(jnp.where(eye, jnp.broadcast_to(rb[...], (slots, slots)), 0), axis=1, keepdims=True)
    owner = lax.div(block_of, jnp.int32(each))
    group = block_of - owner * each
    slot = lax.broadcasted_iota(jnp.int32, (slots, lanes), 0)
    lane = lax.broadcasted_iota(jnp.int32, (slots, lanes), 1)
    used = jnp.logical_and(slot < counts[0, 0], lax.div(lane, jnp.int32(rblk)) == group)
    owners[...] = jnp.where(used, jnp.bitwise_xor(owner, me), -1)
    steps, per = traces.shape
    own[...] = jnp.zeros(own.shape, F32)
    own[0, 0:steps, 0:per] = traces[...].astype(F32)
    copies[0].wait()
    put_faces(cur, gx_index, gy_index, ye, yo if with_yo else None, xe, None)
    for copy in copies[4:]:
        copy.wait()


def flush_kernel(a_in, b_in, a_out, b_out, sems):
    copies = [
        pltpu.make_async_copy(src, dst, sems.at[i]) for i, (src, dst) in enumerate(((a_in, a_out), (b_in, b_out)))
    ]
    for copy in copies:
        copy.start()
    for copy in copies:
        copy.wait()


def update(cur, prev, c2, toeplitz, out, ypad, source=None, fine=None):
    cx, cy, nz = cur.shape
    w = LAPLACE_COEFS
    zero = jnp.zeros((8, nz), F32)
    for x in range(cx):
        ypad[x, 0:8, :] = zero
        ypad[x, 8 : 8 + cy, :] = cur[x, :, :]
        ypad[x, 8 + cy : 16 + cy, :] = zero
    chunk = 8
    rows = chunk * cy
    t_hi = toeplitz[0:nz, :]
    t_lo = toeplitz[nz : 2 * nz, :]
    for m in range(cx // chunk):
        v = cur[m * chunk : (m + 1) * chunk, :, :].reshape(rows, nz)
        hi, lo = split2(v)
        lz = dot(hi, t_hi) + dot(lo, t_hi) + dot(hi, t_lo)
        if source is not None:
            select, contrib = source
            src = dot(select[m * rows : (m + 1) * rows, :], contrib)
        for j in range(chunk):
            x = m * chunk + j
            total = lz[j * cy : (j + 1) * cy, :]
            for k in range(1, REACH + 1):
                pair = ypad[x, 8 - k : 8 - k + cy, :] + ypad[x, 8 + k : 8 + k + cy, :]
                if x - k >= 0:
                    pair = pair + cur[x - k, :, :]
                if x + k < cx:
                    pair = pair + cur[x + k, :, :]
                total = total + w[k] * pair
            here = cur[x, :, :]
            value = (2.0 * here - prev[x, :, :]) + c2[x, :, :] * total
            if source is not None:
                value = value + src[j * cy : (j + 1) * cy, :]
            out[x, :, :] = value
            if fine is not None:
                fine_in, accel, fine_out = fine
                term = accel[x, :, :].astype(F32) * here
                fine_out[x, :, :] = term if fine_in is None else fine_in[x, :, :] + term


def first_update_kernel(cur, prev, c2, toeplitz, out, ypad):
    update(cur, prev, c2, toeplitz, out, ypad)


def update_kernel(cur, prev, c2, toeplitz, select, contrib, accel, *rest, step):
    if step == 1:
        out, fine_out, ypad = rest
        fine_in = None
    else:
        fine_in, out, fine_out, ypad = rest
    update(
        cur, prev, c2, toeplitz, out, ypad,
        source=(select, contrib[step]), fine=(fine_in, accel.at[step - 1], fine_out),
    )


def contributions(owners, weights, blocks, patterns, contrib, wide):
    slots, rblk, nz = weights.shape
    steps = contrib.shape[0]
    lanes = 128
    picked = [jnp.zeros((slots, lanes), F32) for _ in range(steps)]
    for tile, pattern in zip(blocks, patterns):
        mask = owners[...] == pattern
        for t in range(steps):
            picked[t] = jnp.where(mask, tile[t : t + 1, :], picked[t])
    spread = (
        lax.rem(lax.broadcasted_iota(jnp.int32, (lanes, lanes), 0), jnp.int32(rblk))
        == lax.rem(lax.broadcasted_iota(jnp.int32, (lanes, lanes), 1), jnp.int32(rblk))
    )
    spread = jnp.where(spread, 1.0, 0.0).astype(BF16)
    tiled = [dot(p.astype(BF16), spread) for p in picked]
    together = lanes // rblk
    diagonal = lax.broadcasted_iota(jnp.int32, (together, lanes), 0) == lax.div(
        lax.broadcasted_iota(jnp.int32, (together, lanes), 1), jnp.int32(rblk)
    )
    for q in range(slots // together):
        rows = slice(q * together, (q + 1) * together)
        left = jnp.concatenate([jnp.where(diagonal, v[rows, :], 0.0) for v in tiled], axis=0).astype(BF16)
        right = weights[q * together : (q + 1) * together, :, :].reshape(together * rblk, nz)
        got = dot(left, right)
        for t in range(steps):
            wide[t, rows, :] = got[t * together : (t + 1) * together, :]
    for t in range(steps):
        hi, mid = split2(wide[t, :, :])
        rest = wide[t, :, :] - hi.astype(F32) - mid.astype(F32)
        contrib[t, 0:slots, :] = hi
        contrib[t, slots : 2 * slots, :] = mid
        contrib[t, 2 * slots : 3 * slots, :] = rest.astype(BF16)


def unpack(refs, with_yo, with_xo):
    refs = list(refs)
    ye = refs.pop(0)
    yo = refs.pop(0) if with_yo else None
    xe = refs.pop(0)
    xo = refs.pop(0) if with_xo else None
    return ye, yo, xe, xo, refs


def first_correct_kernel(owners, weights, select, part, c2, *refs, with_yo, with_xo, holds, patterns):
    gx_index, gy_index = lax.axis_index("gx"), lax.axis_index("gy")
    ye, yo, xe, xo, refs = unpack(refs, with_yo, with_xo)
    held, refs = refs[:holds], refs[holds:]
    nxt, contrib, refs = refs[0], refs[1], refs[2:]
    oye, oyo, oxe, oxo, refs = unpack(refs, with_yo, with_xo)
    wide = refs[0]
    lanes = 128
    tiles = []
    for ref in held:
        for i in range(ref.shape[0]):
            tiles += [ref[i][:, 0:lanes], ref[i][:, lanes : 2 * lanes]]
    contributions(owners, weights, tiles, patterns, contrib, wide)
    cx, cy, nz = nxt.shape
    chunk = 8
    rows = chunk * cy
    for m in range(cx // chunk):
        src = dot(select[m * rows : (m + 1) * rows, :], contrib[0])
        at = slice(m * chunk, (m + 1) * chunk)
        nxt[at, :, :] = part[at, :, :] + src.reshape(chunk, cy, nz)
    add_halos(nxt, c2, gx_index, gy_index, ye, yo, xe, xo)
    put_faces(nxt, gx_index, gy_index, oye, oyo, oxe, oxo)


def correct_kernel(part, c2, *refs, with_yo, with_xo):
    gx_index, gy_index = lax.axis_index("gx"), lax.axis_index("gy")
    ye, yo, xe, xo, refs = unpack(refs, with_yo, with_xo)
    nxt, refs = refs[0], refs[1:]
    oye, oyo, oxe, oxo, refs = unpack(refs, with_yo, with_xo)
    nxt[...] = part[...]
    add_halos(nxt, c2, gx_index, gy_index, ye, yo, xe, xo)
    put_faces(nxt, gx_index, gy_index, oye, oyo, oxe, oxo)


def last_kernel(part, c2, accel, fine, *refs, with_yo, with_xo, step):
    gx_index, gy_index = lax.axis_index("gx"), lax.axis_index("gy")
    ye, yo, xe, xo, refs = unpack(refs, with_yo, with_xo)
    nxt, coarse, middle = refs
    cx, cy, nz = nxt.shape
    nxt[...] = part[...]
    add_halos(nxt, c2, gx_index, gy_index, ye, yo, xe, xo)
    pairs = lax.div(lax.broadcasted_iota(jnp.int32, (nz, nz // 2), 0), jnp.int32(2)) == lax.broadcasted_iota(
        jnp.int32, (nz, nz // 2), 1
    )
    pairs = jnp.where(pairs, 0.125, 0.0).astype(BF16)
    chunk = 8
    for m in range(cx // (2 * chunk)):
        summed = []
        for j in range(chunk):
            x = 2 * (m * chunk + j)
            a = fine[x, :, :] + accel[step, x, :, :].astype(F32) * nxt[x, :, :]
            b = fine[x + 1, :, :] + accel[step, x + 1, :, :].astype(F32) * nxt[x + 1, :, :]
            summed.append(a + b)
        hi, lo = split2(jnp.concatenate(summed, axis=0))
        got = dot(hi, pairs) + dot(lo, pairs)
        middle[m * chunk * cy : (m + 1) * chunk * cy, :] = got
    half = cx * cy // 4
    both = middle[pl.ds(0, half, 2), :] + middle[pl.ds(1, half, 2), :]
    coarse[...] = both.reshape(coarse.shape)


def local(adj_prev, adj_cur, fwd_accel, courant2, traces, weights, rblock, column, counts):
    accel = fwd_accel[0]
    cx, cy, nz = courant2.shape
    steps = accel.shape[0]
    slots, rblk = weights.shape[2:4]
    per = traces.shape[2]
    nx, ny, nshot = lax.axis_size("gx"), lax.axis_size("gy"), lax.axis_size("shot")
    with_yo, with_xo = ny > 2, nx > 2
    y_msg, x_msg = (cx // 2, 8, nz), (REACH * cy // 8, 8, nz)
    tile = (cx, cy, nz)
    cells = cx * cy * nz
    lanes = 128

    def xor(size, bit):
        return [(i, i ^ bit) for i in range(size)]

    theirs = lax.ppermute(traces[0], "gy", even_pairs(ny))
    cur, prev, c2, wts, ye, yo, xe, own, toeplitz, select, owners = vmem_call(
        functools.partial(load_kernel, with_yo=with_yo, each=per // rblk, rblk=rblk),
        [
            sds(tile), sds(tile), sds(tile), sds((slots, rblk, nz), BF16),
            sds(y_msg), sds(y_msg), sds(x_msg), sds((1, 8, lanes)),
            sds((2 * nz, nz), BF16), sds((cx * cy, 3 * slots), BF16), sds((slots, lanes), jnp.int32),
        ],
            [adj_cur[0], adj_prev[0], courant2, weights[0, 0], traces[0], column[0], rblock[0], counts],
        [
            pltpu.VMEM((steps, per), BF16), pltpu.VMEM((1, slots), jnp.int32), pltpu.VMEM((1, slots), jnp.int32),
            pltpu.SemaphoreType.DMA((7,)),
        ],
        hbm_in=tuple(range(7)),
        smem_in=(7,),
    )

    theirs = jnp.pad(theirs.astype(F32), ((0, 8 - steps), (0, lanes - per)))[None]
    pair = jnp.concatenate([own, theirs], axis=2)
    rxe = lax.ppermute(jnp.concatenate([xe, pair], axis=0), "gx", even_pairs(nx))
    ryo = lax.ppermute(yo, "gy", odd_pairs(ny)) if with_yo else None
    rxo = None
    if with_xo:
        low = cur[0:REACH].reshape(x_msg)
        high = cur[cx - REACH :].reshape(x_msg)
        rxo = lax.ppermute(jnp.where(lax.axis_index("gx") % 2 == 0, low, high), "gx", odd_pairs(nx))
    patterns = [0, 1, ny, ny + 1]
    now = jnp.concatenate([pair, rxe[x_msg[0] :]], axis=0)
    held = [now]
    for axis, size, stride in (("gy", ny, 1), ("gx", nx, ny)):
        bit = 2
        while bit < size:
            got = lax.ppermute(now, axis, xor(size, bit))
            held.append(got)
            patterns = patterns + [p ^ (bit * stride) for p in patterns]
            bit *= 2
            now = jnp.concatenate([now, got], axis=0)
    rye = lax.ppermute(ye, "gy", even_pairs(ny))

    ypad = pltpu.VMEM((cx, cy + 16, nz), F32)
    part = vmem_call(first_update_kernel, [sds(tile)], [cur, prev, c2, toeplitz], [ypad], flops=cells * 60)[0]

    def given(ye, yo, xe, xo):
        return [a for a in (ye, yo, xe, xo) if a is not None]

    def face_shapes():
        return given(sds(y_msg), sds(y_msg) if with_yo else None, sds(x_msg), sds(x_msg) if with_xo else None)

    def taken(faces):
        faces = list(faces)
        ye = faces.pop(0)
        yo = faces.pop(0) if with_yo else None
        xe = faces.pop(0)
        xo = faces.pop(0) if with_xo else None
        return ye, yo, xe, xo

    nxt, contrib, *faces = vmem_call(
        functools.partial(
            first_correct_kernel, with_yo=with_yo, with_xo=with_xo, holds=len(held), patterns=tuple(patterns)
        ),
        [sds(tile), sds((steps, 3 * slots, nz), BF16)] + face_shapes(),
        [owners, wts, select, part, c2] + given(rye, ryo, rxe, rxo) + held,
        [pltpu.VMEM((steps, slots, nz), F32)],
    )
    previous, current = cur, nxt
    fine = None
    for step in range(1, steps):
        ye, yo, xe, xo = taken(faces)
        ryo = lax.ppermute(yo, "gy", odd_pairs(ny)) if with_yo else None
        rxe = lax.ppermute(xe, "gx", even_pairs(nx))
        rxo = lax.ppermute(xo, "gx", odd_pairs(nx)) if with_xo else None
        rye = lax.ppermute(ye, "gy", even_pairs(ny))
        args = [current, previous, c2, toeplitz, select, contrib, accel]
        if fine is not None:
            args.append(fine)
        part, fine = vmem_call(
            functools.partial(update_kernel, step=step), [sds(tile), sds(tile)], args, [ypad],
            flops=cells * 60,
        )
        halos = given(rye, ryo, rxe, rxo)
        if step < steps - 1:
            nxt, *faces = vmem_call(
                functools.partial(correct_kernel, with_yo=with_yo, with_xo=with_xo),
                [sds(tile)] + face_shapes(),
                [part, c2] + halos,
            )
        else:
            nxt, coarse = vmem_call(
                functools.partial(last_kernel, with_yo=with_yo, with_xo=with_xo, step=step),
                [sds(tile), sds((cx // 2, cy // 2, nz // 2))],
                [part, c2, accel, fine] + halos,
                [pltpu.VMEM((cx * cy // 2, nz // 2), F32)],
            )
        previous, current = current, nxt
    bit = 1
    while bit < nshot:
        coarse = coarse + lax.ppermute(coarse, "shot", xor(nshot, bit))
        bit *= 2
    previous, current = vmem_call(
        flush_kernel, [sds(tile), sds(tile)], [previous, current], [pltpu.SemaphoreType.DMA((2,))],
        hbm_out=(0, 1),
    )
    return (previous[None], current[None], coarse)


def solution(mesh):
    return jax.shard_map(
        local,
        mesh=mesh,
        in_specs=(
            P("shot", "gx", "gy", None),
            P("shot", "gx", "gy", None),
            P("shot", None, "gx", "gy", None),
            P("gx", "gy", None),
            P("shot", None, ("gx", "gy")),
            P("gx", "gy", None, None, None),
            P("gx", "gy", None),
            P("gx", "gy", None),
            P("gx", "gy"),
        ),
        out_specs=(P("shot", "gx", "gy", None), P("shot", "gx", "gy", None), P("gx", "gy", None)),
        check_vma=False,
    )
```

```python
import functools

import jax
import jax.numpy as jnp
from jax import lax
from jax.experimental import pallas as pl
from jax.experimental.pallas import tpu as pltpu
from jax.sharding import PartitionSpec as P


LAPLACE_COEFS = (-205.0 / 72.0, 8.0 / 5.0, -1.0 / 5.0, 8.0 / 315.0, -1.0 / 560.0)
REACH = 4
CHUNK = 8
VMEM_LIMIT = 16 << 20
F32 = jnp.float32
BF16 = jnp.bfloat16


def vmem_call(kernel, outs, args, scratch=(), flops=0, hbm_in=(), hbm_out=(), smem_in=()):
    in_specs = [
        pl.BlockSpec(memory_space=pltpu.HBM if i in hbm_in else pltpu.SMEM if i in smem_in else pltpu.VMEM)
        for i in range(len(args))
    ]
    args = [pltpu.with_memory_space_constraint(a, pltpu.HBM) if i in hbm_in else a for i, a in enumerate(args)]
    moved = sum(a.size * a.dtype.itemsize for a in args) + sum(o.size * o.dtype.itemsize for o in outs)
    return pl.pallas_call(
        kernel,
        out_shape=tuple(outs),
        in_specs=in_specs,
        out_specs=tuple(
            pl.BlockSpec(memory_space=pltpu.HBM if i in hbm_out else pltpu.VMEM) for i in range(len(outs))
        ),
        scratch_shapes=list(scratch),
        cost_estimate=pl.CostEstimate(flops=flops, bytes_accessed=moved, transcendentals=0),
        compiler_params=pltpu.CompilerParams(vmem_limit_bytes=VMEM_LIMIT),
    )(*args)


def sds(shape, dtype=F32):
    return jax.ShapeDtypeStruct(shape, dtype)


def even_pairs(n):
    pairs = []
    for i in range(0, n - 1, 2):
        pairs += [(i, i + 1), (i + 1, i)]
    return pairs


def odd_swap(x, axis):
    n, shots = lax.axis_size(axis), lax.axis_size("shot")
    if shots % 2:
        pairs = [(0, n - 1), (n - 1, 0)]
        for i in range(1, n - 1, 2):
            pairs += [(i, i + 1), (i + 1, i)]
        return lax.ppermute(x, axis, pairs)
    pairs = []
    for s in range(shots):
        for i in (0, n - 1):
            pairs.append((i * shots + s, i * shots + (s ^ 1)))
        for i in range(1, n - 1, 2):
            pairs += [(i * shots + s, (i + 1) * shots + s), ((i + 1) * shots + s, i * shots + s)]
    return lax.ppermute(x, (axis, "shot"), pairs)


def split2(v):
    hi = v.astype(BF16)
    return hi, (v - hi.astype(F32)).astype(BF16)


def dot(a, b):
    return jnp.dot(a, b, preferred_element_type=F32)


def put_y_face(cur, out, high):
    cx, cy, _ = cur.shape
    start = cy - REACH if high else 0
    for i in range(cx // 2):
        out[i, 0:REACH, :] = cur[2 * i, start : start + REACH, :]
        out[i, REACH : 2 * REACH, :] = cur[2 * i + 1, start : start + REACH, :]


def put_faces(cur, gx_index, gy_index, ye, yo, xe, xo):
    cx, cy, _ = cur.shape
    y_even = gy_index % 2 == 0
    x_even = gx_index % 2 == 0

    @pl.when(y_even)
    def _():
        put_y_face(cur, ye, True)
        if yo is not None:
            put_y_face(cur, yo, False)

    @pl.when(jnp.logical_not(y_even))
    def _():
        put_y_face(cur, ye, False)
        if yo is not None:
            put_y_face(cur, yo, True)

    half = cy // 8
    low = jnp.where(x_even, cx - REACH, 0)
    for r in range(REACH):
        for h in range(half):
            xe[r * half + h, :, :] = cur[low + r, 8 * h : 8 * h + 8, :]
            if xo is not None:
                xo[r * half + h, :, :] = cur[cx - REACH - low + r, 8 * h : 8 * h + 8, :]


def add_y_halo(nxt, c2, recv, high):
    cx, cy, nz = nxt.shape
    w = LAPLACE_COEFS
    row = lax.broadcasted_iota(jnp.int32, (8, nz), 0) % REACH
    coefs = {}
    for k in range(1, REACH + 1):
        shift = REACH - k
        keep = (row >= shift) if high else (row < k)
        coefs[k] = jnp.where(keep, w[k], 0.0)
    start = cy - REACH if high else 0
    for i in range(cx // 2):
        m = recv[i, :, :]
        total = w[REACH] * m
        for k in range(1, REACH):
            shift = REACH - k
            total = total + coefs[k] * pltpu.roll(m, shift if high else 8 - shift, 0)
        for h in range(2):
            rows = slice(start, start + REACH)
            nxt[2 * i + h, rows, :] = (
                nxt[2 * i + h, rows, :] + c2[2 * i + h, rows, :] * total[REACH * h : REACH * h + REACH, :]
            )


def add_x_halo(nxt, c2, recv, high):
    cx, cy, _ = nxt.shape
    w = LAPLACE_COEFS
    half = cy // 8
    for r in range(REACH):
        x = cx - 1 - r if high else r
        for h in range(half):
            total = None
            for k in range(r + 1, REACH + 1):
                row = (k - r - 1) if high else (REACH + r - k)
                term = w[k] * recv[row * half + h, :, :]
                total = term if total is None else total + term
            ys = slice(8 * h, 8 * h + 8)
            nxt[x, ys, :] = nxt[x, ys, :] + c2[x, ys, :] * total


def add_halos(nxt, c2, gx_index, gy_index, ye, yo, xe, xo):
    for axis, index, even, odd, add in (("gy", gy_index, ye, yo, add_y_halo), ("gx", gx_index, xe, xo, add_x_halo)):
        is_even = index % 2 == 0
        inner = jnp.logical_and(index > 0, index < lax.axis_size(axis) - 1)

        @pl.when(is_even)
        def _(even=even, add=add):
            add(nxt, c2, even, True)

        @pl.when(jnp.logical_not(is_even))
        def _(even=even, add=add):
            add(nxt, c2, even, False)

        if odd is not None:

            @pl.when(jnp.logical_and(inner, is_even))
            def _(odd=odd, add=add):
                add(nxt, c2, odd, False)

            @pl.when(jnp.logical_and(inner, jnp.logical_not(is_even)))
            def _(odd=odd, add=add):
                add(nxt, c2, odd, True)


def load_kernel(
    cur_in, col_in, rb_in, traces_in, counts, cur, ye, yo, xe, toeplitz, select, owners, own, col, rb, traces, sems,
    *, with_yo, each, rblk,
):
    gx_index, gy_index = lax.axis_index("gx"), lax.axis_index("gy")
    pairs = ((cur_in, cur), (col_in, col), (rb_in, rb), (traces_in, traces))
    copies = [pltpu.make_async_copy(src, dst, sems.at[i]) for i, (src, dst) in enumerate(pairs)]
    for copy in copies:
        copy.start()
    nz = toeplitz.shape[1]
    distance = jnp.abs(
        lax.broadcasted_iota(jnp.int32, (nz, nz), 0) - lax.broadcasted_iota(jnp.int32, (nz, nz), 1)
    )
    band = jnp.where(distance == 0, 3.0 * LAPLACE_COEFS[0], 0.0)
    for k in range(1, REACH + 1):
        band = band + jnp.where(distance == k, LAPLACE_COEFS[k], 0.0)
    hi, lo = split2(band)
    toeplitz[0:nz, :] = hi
    toeplitz[nz : 2 * nz, :] = lo
    for copy in copies[1:]:
        copy.wait()
    wide = jnp.concatenate([col[...]] * 3, axis=1)
    rows = lax.broadcasted_iota(jnp.int32, select.shape, 0)
    select[...] = jnp.where(rows == wide, 1.0, 0.0).astype(BF16)
    slot_owners(rb, counts, owners, each, rblk)
    steps, per = traces.shape[1:]
    own[...] = jnp.zeros(own.shape, F32)
    own[0, 0:steps, 0:per] = traces[0].astype(F32)
    copies[0].wait()
    put_faces(cur, gx_index, gy_index, ye, yo if with_yo else None, xe, None)


def slot_owners(rb, counts, owners, each, rblk):
    me = lax.axis_index("gx") * lax.axis_size("gy") + lax.axis_index("gy")
    slots, lanes = owners.shape
    eye = lax.broadcasted_iota(jnp.int32, (slots, slots), 0) == lax.broadcasted_iota(jnp.int32, (slots, slots), 1)
    block_of = jnp.sum(jnp.where(eye, jnp.broadcast_to(rb[...], (slots, slots)), 0), axis=1, keepdims=True)
    owner = lax.div(block_of, jnp.int32(each))
    group = block_of - owner * each
    lane = lax.broadcasted_iota(jnp.int32, (slots, lanes), 1)
    live = lax.broadcasted_iota(jnp.int32, (slots, lanes), 0) < counts[0, 0]
    used = jnp.logical_and(live, lax.div(lane, jnp.int32(rblk)) == group)
    owners[...] = jnp.where(used, jnp.bitwise_xor(owner, me), -1)


def flush_kernel(a_in, b_in, a_out, b_out, sems):
    copies = [
        pltpu.make_async_copy(src, dst, sems.at[i]) for i, (src, dst) in enumerate(((a_in, a_out), (b_in, b_out)))
    ]
    for copy in copies:
        copy.start()
    for copy in copies:
        copy.wait()


def update(cur, prev, c2, toeplitz, out, ypad, source=None, fine=None):
    cx, cy, nz = cur.shape
    w = LAPLACE_COEFS
    zero = jnp.zeros((8, nz), F32)
    for x in range(cx):
        ypad[x, 0:8, :] = zero
        ypad[x, 8 : 8 + cy, :] = cur[x, :, :]
        ypad[x, 8 + cy : 16 + cy, :] = zero
    chunk = CHUNK
    rows = chunk * cy
    t_hi = toeplitz[0:nz, :]
    t_lo = toeplitz[nz : 2 * nz, :]
    for m in range(cx // chunk):
        v = cur[m * chunk : (m + 1) * chunk, :, :].reshape(rows, nz)
        hi, lo = split2(v)
        lz = dot(hi, t_hi) + dot(lo, t_hi) + dot(hi, t_lo)
        if source is not None:
            select, contrib = source
            src = dot(select[m * rows : (m + 1) * rows, :], contrib)
        for j in range(chunk):
            x = m * chunk + j
            total = lz[j * cy : (j + 1) * cy, :]
            for k in range(1, REACH + 1):
                pair = ypad[x, 8 - k : 8 - k + cy, :] + ypad[x, 8 + k : 8 + k + cy, :]
                if x - k >= 0:
                    pair = pair + cur[x - k, :, :]
                if x + k < cx:
                    pair = pair + cur[x + k, :, :]
                total = total + w[k] * pair
            if prev is None:
                out[x, :, :] = total
                continue
            here = cur[x, :, :]
            value = (2.0 * here - prev[x, :, :]) + c2[x, :, :] * total
            if source is not None:
                value = value + src[j * cy : (j + 1) * cy, :]
            out[x, :, :] = value
            if fine is not None:
                fine_in, accel, fine_out = fine
                term = accel[x, :, :].astype(F32) * here
                fine_out[x, :, :] = term if fine_in is None else fine_in[x, :, :] + term


def first_update_kernel(cur, toeplitz, prev_in, c2_in, weights_in, out, prev, c2, weights, ypad, sems):
    copies = [
        pltpu.make_async_copy(src, dst, sems.at[i])
        for i, (src, dst) in enumerate(((prev_in, prev), (c2_in, c2), (weights_in, weights)))
    ]
    for copy in copies:
        copy.start()
    update(cur, None, None, toeplitz, out, ypad)
    copies[0].wait()
    copies[1].wait()
    for x in range(cur.shape[0]):
        out[x, :, :] = (2.0 * cur[x, :, :] - prev[x, :, :]) + c2[x, :, :] * out[x, :, :]
    copies[2].wait()


def update_kernel(cur, prev, c2, toeplitz, select, contrib, accel, *rest, step):
    if step == 1:
        out, fine_out, ypad = rest
        fine_in = None
    else:
        fine_in, out, fine_out, ypad = rest
    update(
        cur, prev, c2, toeplitz, out, ypad,
        source=(select, contrib[step]), fine=(fine_in, accel.at[step - 1], fine_out),
    )


def contributions(owners, weights, blocks, patterns, contrib, wide):
    slots, rblk, nz = weights.shape
    steps = contrib.shape[0]
    lanes = 128
    picked = [jnp.zeros((slots, lanes), F32) for _ in range(steps)]
    for tile, pattern in zip(blocks, patterns):
        mask = owners[...] == pattern
        for t in range(steps):
            picked[t] = jnp.where(mask, tile[t : t + 1, :], picked[t])
    spread = (
        lax.rem(lax.broadcasted_iota(jnp.int32, (lanes, lanes), 0), jnp.int32(rblk))
        == lax.rem(lax.broadcasted_iota(jnp.int32, (lanes, lanes), 1), jnp.int32(rblk))
    )
    spread = jnp.where(spread, 1.0, 0.0).astype(BF16)
    tiled = [dot(p.astype(BF16), spread) for p in picked]
    together = lanes // rblk
    diagonal = lax.broadcasted_iota(jnp.int32, (together, lanes), 0) == lax.div(
        lax.broadcasted_iota(jnp.int32, (together, lanes), 1), jnp.int32(rblk)
    )
    for q in range(slots // together):
        rows = slice(q * together, (q + 1) * together)
        left = jnp.concatenate([jnp.where(diagonal, v[rows, :], 0.0) for v in tiled], axis=0).astype(BF16)
        right = weights[q * together : (q + 1) * together, :, :].reshape(together * rblk, nz)
        got = dot(left, right)
        for t in range(steps):
            wide[t, rows, :] = got[t * together : (t + 1) * together, :]
    for t in range(steps):
        hi, mid = split2(wide[t, :, :])
        rest = wide[t, :, :] - hi.astype(F32) - mid.astype(F32)
        contrib[t, 0:slots, :] = hi
        contrib[t, slots : 2 * slots, :] = mid
        contrib[t, 2 * slots : 3 * slots, :] = rest.astype(BF16)


def unpack(refs, with_yo, with_xo):
    refs = list(refs)
    ye = refs.pop(0)
    yo = refs.pop(0) if with_yo else None
    xe = refs.pop(0)
    xo = refs.pop(0) if with_xo else None
    return ye, yo, xe, xo, refs


def first_correct_kernel(owners, weights, select, part, c2, *refs, with_yo, with_xo, patterns):
    gx_index, gy_index = lax.axis_index("gx"), lax.axis_index("gy")
    ye, yo, xe, xo, refs = unpack(refs, with_yo, with_xo)
    pairs, refs = refs[0], refs[1:]
    nxt, contrib, refs = refs[0], refs[1], refs[2:]
    oye, oyo, oxe, oxo, refs = unpack(refs, with_yo, with_xo)
    wide = refs[0]
    lanes = 128
    tiles = []
    n = pairs.shape[0]
    y_last, x_last = ye.shape[0] - n, xe.shape[0] - 2 * n
    for ref, first in ((pairs, 0), (ye, y_last), (xe, x_last), (xe, x_last + n)):
        for i in range(n):
            tiles += [ref[first + i][:, 0:lanes], ref[first + i][:, lanes : 2 * lanes]]
    contributions(owners, weights, tiles, patterns, contrib, wide)
    cx, cy, nz = nxt.shape
    chunk = 8
    rows = chunk * cy
    for m in range(cx // chunk):
        src = dot(select[m * rows : (m + 1) * rows, :], contrib[0])
        at = slice(m * chunk, (m + 1) * chunk)
        nxt[at, :, :] = part[at, :, :] + src.reshape(chunk, cy, nz)
    add_halos(nxt, c2, gx_index, gy_index, ye, yo, xe, xo)
    put_faces(nxt, gx_index, gy_index, oye, oyo, oxe, oxo)


def correct_kernel(part, c2, *refs, with_yo, with_xo):
    gx_index, gy_index = lax.axis_index("gx"), lax.axis_index("gy")
    ye, yo, xe, xo, refs = unpack(refs, with_yo, with_xo)
    nxt, refs = refs[0], refs[1:]
    oye, oyo, oxe, oxo, refs = unpack(refs, with_yo, with_xo)
    nxt[...] = part[...]
    add_halos(nxt, c2, gx_index, gy_index, ye, yo, xe, xo)
    put_faces(nxt, gx_index, gy_index, oye, oyo, oxe, oxo)


def last_kernel(part, c2, accel, fine, *refs, with_yo, with_xo, step):
    gx_index, gy_index = lax.axis_index("gx"), lax.axis_index("gy")
    ye, yo, xe, xo, refs = unpack(refs, with_yo, with_xo)
    nxt, coarse, middle = refs
    cx, cy, nz = nxt.shape
    nxt[...] = part[...]
    add_halos(nxt, c2, gx_index, gy_index, ye, yo, xe, xo)
    pairs = lax.div(lax.broadcasted_iota(jnp.int32, (nz, nz // 2), 0), jnp.int32(2)) == lax.broadcasted_iota(
        jnp.int32, (nz, nz // 2), 1
    )
    pairs = jnp.where(pairs, 0.125, 0.0).astype(BF16)
    chunk = 8
    for m in range(cx // (2 * chunk)):
        summed = []
        for j in range(chunk):
            x = 2 * (m * chunk + j)
            a = fine[x, :, :] + accel[step, x, :, :].astype(F32) * nxt[x, :, :]
            b = fine[x + 1, :, :] + accel[step, x + 1, :, :].astype(F32) * nxt[x + 1, :, :]
            summed.append(a + b)
        hi, lo = split2(jnp.concatenate(summed, axis=0))
        got = dot(hi, pairs) + dot(lo, pairs)
        middle[m * chunk * cy : (m + 1) * chunk * cy, :] = got
    half = cx * cy // 4
    both = middle[pl.ds(0, half, 2), :] + middle[pl.ds(1, half, 2), :]
    coarse[...] = both.reshape(coarse.shape)


def local(adj_prev, adj_cur, fwd_accel, courant2, traces, weights, rblock, column, counts):
    accel = fwd_accel[0]
    cx, cy, nz = courant2.shape
    steps = accel.shape[0]
    slots, rblk = weights.shape[2:4]
    per = traces.shape[2]
    nx, ny, nshot = lax.axis_size("gx"), lax.axis_size("gy"), lax.axis_size("shot")
    with_yo, with_xo = ny > 2, nx > 2
    y_msg, x_msg = (cx // 2, 8, nz), (REACH * cy // 8, 8, nz)
    tile = (cx, cy, nz)
    cells = cx * cy * nz
    lanes = 128

    def swap(x, axis, pairs=None):
        return odd_swap(x, axis) if pairs is None else lax.ppermute(x, axis, pairs)

    def xor(size, bit):
        return [(i, i ^ bit) for i in range(size)]

    blocks, others, patterns = traces, [], [0]
    for axis, size, stride in (("gy", ny, 1), ("gx", nx, ny)):
        bit = 2
        while bit < size:
            got = swap(blocks, axis, xor(size, bit))
            others.append(got)
            patterns = patterns + [p ^ (bit * stride) for p in patterns]
            bit *= 2
            if bit < size or (axis == "gy" and nx > 2):
                blocks = jnp.concatenate([blocks, got], axis=0)
    if not others:
        others, patterns = [jnp.zeros_like(traces)], [0, -2]
    cur, ye, yo, xe, toeplitz, select, owners, own = vmem_call(
        functools.partial(load_kernel, with_yo=with_yo, each=per // rblk, rblk=rblk),
        [
            sds(tile), sds(y_msg), sds(y_msg), sds(x_msg), sds((2 * nz, nz), BF16),
            sds((cx * cy, 3 * slots), BF16), sds((slots, lanes), jnp.int32), sds((1, 8, lanes)),
        ],
        [adj_cur[0], column[0], rblock[0], traces, counts],
        [
            pltpu.VMEM((1, slots), jnp.int32), pltpu.VMEM((1, slots), jnp.int32), pltpu.VMEM((1, steps, per), BF16),
            pltpu.SemaphoreType.DMA((4,)),
        ],
        hbm_in=(0, 1, 2, 3), smem_in=(4,),
    )
    others = [jnp.pad(a.astype(F32), ((0, 0), (0, 8 - steps), (0, lanes - per))) for a in others]
    tiles = jnp.concatenate([own] + others, axis=0)
    pairs = jnp.concatenate([tiles[0::2], tiles[1::2]], axis=2)
    rye = swap(jnp.concatenate([ye, pairs], axis=0), "gy", even_pairs(ny))
    ryo = swap(yo, "gy") if with_yo else None
    rxo = None
    if with_xo:
        low = cur[0:REACH].reshape(x_msg)
        high = cur[cx - REACH :].reshape(x_msg)
        rxo = swap(jnp.where(lax.axis_index("gx") % 2 == 0, low, high), "gx")
    rxe = swap(jnp.concatenate([xe, pairs, rye[y_msg[0] :]], axis=0), "gx", even_pairs(nx))
    for stride in (1, ny):
        patterns = patterns + [p ^ stride if p >= 0 else p for p in patterns]

    ypad = pltpu.VMEM((cx, cy + 16, nz), F32)
    part, _, c2, wts = vmem_call(
        first_update_kernel,
        [sds(tile), sds(tile), sds(tile), sds((slots, rblk, nz), BF16)],
        [cur, toeplitz, adj_prev[0], courant2, weights[0, 0]],
        [ypad, pltpu.SemaphoreType.DMA((3,))],
        hbm_in=(2, 3, 4), flops=cells * 60,
    )

    def given(ye, yo, xe, xo):
        return [a for a in (ye, yo, xe, xo) if a is not None]

    def face_shapes():
        return given(sds(y_msg), sds(y_msg) if with_yo else None, sds(x_msg), sds(x_msg) if with_xo else None)

    def taken(faces):
        faces = list(faces)
        ye = faces.pop(0)
        yo = faces.pop(0) if with_yo else None
        xe = faces.pop(0)
        xo = faces.pop(0) if with_xo else None
        return ye, yo, xe, xo

    nxt, contrib, *faces = vmem_call(
        functools.partial(
            first_correct_kernel, with_yo=with_yo, with_xo=with_xo, patterns=tuple(patterns)
        ),
        [sds(tile), sds((steps, 3 * slots, nz), BF16)] + face_shapes(),
        [owners, wts, select, part, c2] + given(rye, ryo, rxe, rxo) + [pairs],
        [pltpu.VMEM((steps, slots, nz), F32)],
    )
    previous, current = cur, nxt
    fine = None
    for step in range(1, steps):
        ye, yo, xe, xo = taken(faces)
        ryo = swap(yo, "gy") if with_yo else None
        rxe = swap(xe, "gx", even_pairs(nx))
        rxo = swap(xo, "gx") if with_xo else None
        rye = swap(ye, "gy", even_pairs(ny))
        args = [current, previous, c2, toeplitz, select, contrib, accel]
        if fine is not None:
            args.append(fine)
        part, fine = vmem_call(
            functools.partial(update_kernel, step=step), [sds(tile), sds(tile)], args, [ypad],
            flops=cells * 60,
        )
        halos = given(rye, ryo, rxe, rxo)
        if step < steps - 1:
            nxt, *faces = vmem_call(
                functools.partial(correct_kernel, with_yo=with_yo, with_xo=with_xo),
                [sds(tile)] + face_shapes(),
                [part, c2] + halos,
            )
        else:
            nxt, coarse = vmem_call(
                functools.partial(last_kernel, with_yo=with_yo, with_xo=with_xo, step=step),
                [sds(tile), sds((cx // 2, cy // 2, nz // 2))],
                [part, c2, accel, fine] + halos,
                [pltpu.VMEM((cx * cy // 2, nz // 2), F32)],
            )
        previous, current = current, nxt
    bit = 1
    while bit < nshot:
        coarse = coarse + swap(coarse, "shot", xor(nshot, bit))
        bit *= 2
    previous, current = vmem_call(
        flush_kernel, [sds(tile), sds(tile)], [previous, current], [pltpu.SemaphoreType.DMA((2,))],
        hbm_out=(0, 1),
    )
    return (previous[None], current[None], coarse)


def solution(mesh):
    return jax.shard_map(
        local,
        mesh=mesh,
        in_specs=(
            P("shot", "gx", "gy", None),
            P("shot", "gx", "gy", None),
            P("shot", None, "gx", "gy", None),
            P("gx", "gy", None),
            P("shot", None, ("gx", "gy")),
            P("gx", "gy", None, None, None),
            P("gx", "gy", None),
            P("gx", "gy", None),
            P("gx", "gy"),
        ),
        out_specs=(P("shot", "gx", "gy", None), P("shot", "gx", "gy", None), P("gx", "gy", None)),
        check_vma=False,
    )
```

```python
import functools

import jax
import jax.numpy as jnp
from jax import lax
from jax.experimental import pallas as pl
from jax.experimental.pallas import tpu as pltpu
from jax.sharding import PartitionSpec as P


LAPLACE_COEFS = (-205.0 / 72.0, 8.0 / 5.0, -1.0 / 5.0, 8.0 / 315.0, -1.0 / 560.0)
REACH = 4
CHUNK = 8
VMEM_LIMIT = 16 << 20
F32 = jnp.float32
BF16 = jnp.bfloat16


def vmem_call(kernel, outs, args, scratch=(), flops=0, hbm_in=(), hbm_out=(), smem_in=()):
    in_specs = [
        pl.BlockSpec(memory_space=pltpu.HBM if i in hbm_in else pltpu.SMEM if i in smem_in else pltpu.VMEM)
        for i in range(len(args))
    ]
    args = [pltpu.with_memory_space_constraint(a, pltpu.HBM) if i in hbm_in else a for i, a in enumerate(args)]
    moved = sum(a.size * a.dtype.itemsize for a in args) + sum(o.size * o.dtype.itemsize for o in outs)
    return pl.pallas_call(
        kernel,
        out_shape=tuple(outs),
        in_specs=in_specs,
        out_specs=tuple(
            pl.BlockSpec(memory_space=pltpu.HBM if i in hbm_out else pltpu.VMEM) for i in range(len(outs))
        ),
        scratch_shapes=list(scratch),
        cost_estimate=pl.CostEstimate(flops=flops, bytes_accessed=moved, transcendentals=0),
        compiler_params=pltpu.CompilerParams(vmem_limit_bytes=VMEM_LIMIT),
    )(*args)


def sds(shape, dtype=F32):
    return jax.ShapeDtypeStruct(shape, dtype)


def even_pairs(n):
    pairs = []
    for i in range(0, n - 1, 2):
        pairs += [(i, i + 1), (i + 1, i)]
    return pairs


def odd_swap(x, axis):
    n, shots = lax.axis_size(axis), lax.axis_size("shot")
    if shots % 2:
        pairs = [(0, n - 1), (n - 1, 0)]
        for i in range(1, n - 1, 2):
            pairs += [(i, i + 1), (i + 1, i)]
        return lax.ppermute(x, axis, pairs)
    pairs = []
    for s in range(shots):
        for i in (0, n - 1):
            pairs.append((i * shots + s, i * shots + (s ^ 1)))
        for i in range(1, n - 1, 2):
            pairs += [(i * shots + s, (i + 1) * shots + s), ((i + 1) * shots + s, i * shots + s)]
    return lax.ppermute(x, (axis, "shot"), pairs)


def split2(v):
    hi = v.astype(BF16)
    return hi, (v - hi.astype(F32)).astype(BF16)


def dot(a, b):
    return jnp.dot(a, b, preferred_element_type=F32)


def put_y_face(cur, out, high):
    cx, cy, _ = cur.shape
    start = cy - REACH if high else 0
    for i in range(cx // 2):
        out[i, 0:REACH, :] = cur[2 * i, start : start + REACH, :]
        out[i, REACH : 2 * REACH, :] = cur[2 * i + 1, start : start + REACH, :]


def put_faces(cur, gx_index, gy_index, ye, yo, xe, xo):
    cx, cy, _ = cur.shape
    y_even = gy_index % 2 == 0
    x_even = gx_index % 2 == 0

    @pl.when(y_even)
    def _():
        put_y_face(cur, ye, True)
        if yo is not None:
            put_y_face(cur, yo, False)

    @pl.when(jnp.logical_not(y_even))
    def _():
        put_y_face(cur, ye, False)
        if yo is not None:
            put_y_face(cur, yo, True)

    half = cy // 8
    low = jnp.where(x_even, cx - REACH, 0)
    for r in range(REACH):
        for h in range(half):
            xe[r * half + h, :, :] = cur[low + r, 8 * h : 8 * h + 8, :]
            if xo is not None:
                xo[r * half + h, :, :] = cur[cx - REACH - low + r, 8 * h : 8 * h + 8, :]


def add_y_halo(nxt, c2, recv, high):
    cx, cy, nz = nxt.shape
    w = LAPLACE_COEFS
    row = lax.broadcasted_iota(jnp.int32, (8, nz), 0) % REACH
    coefs = {}
    for k in range(1, REACH + 1):
        shift = REACH - k
        keep = (row >= shift) if high else (row < k)
        coefs[k] = jnp.where(keep, w[k], 0.0)
    start = cy - REACH if high else 0
    for i in range(cx // 2):
        m = recv[i, :, :]
        total = w[REACH] * m
        for k in range(1, REACH):
            shift = REACH - k
            total = total + coefs[k] * pltpu.roll(m, shift if high else 8 - shift, 0)
        for h in range(2):
            rows = slice(start, start + REACH)
            nxt[2 * i + h, rows, :] = (
                nxt[2 * i + h, rows, :] + c2[2 * i + h, rows, :] * total[REACH * h : REACH * h + REACH, :]
            )


def add_x_halo(nxt, c2, recv, high):
    cx, cy, _ = nxt.shape
    w = LAPLACE_COEFS
    half = cy // 8
    for r in range(REACH):
        x = cx - 1 - r if high else r
        for h in range(half):
            total = None
            for k in range(r + 1, REACH + 1):
                row = (k - r - 1) if high else (REACH + r - k)
                term = w[k] * recv[row * half + h, :, :]
                total = term if total is None else total + term
            ys = slice(8 * h, 8 * h + 8)
            nxt[x, ys, :] = nxt[x, ys, :] + c2[x, ys, :] * total


def add_halos(nxt, c2, gx_index, gy_index, ye, yo, xe, xo):
    for axis, index, even, odd, add in (("gy", gy_index, ye, yo, add_y_halo), ("gx", gx_index, xe, xo, add_x_halo)):
        is_even = index % 2 == 0
        inner = jnp.logical_and(index > 0, index < lax.axis_size(axis) - 1)

        @pl.when(is_even)
        def _(even=even, add=add):
            add(nxt, c2, even, True)

        @pl.when(jnp.logical_not(is_even))
        def _(even=even, add=add):
            add(nxt, c2, even, False)

        if odd is not None:

            @pl.when(jnp.logical_and(inner, is_even))
            def _(odd=odd, add=add):
                add(nxt, c2, odd, False)

            @pl.when(jnp.logical_and(inner, jnp.logical_not(is_even)))
            def _(odd=odd, add=add):
                add(nxt, c2, odd, True)


def load_kernel(
    cur_in, col_in, rb_in, traces_in, counts, cur, ye, yo, xe, toeplitz, select, owners, own, col, rb, traces, sems,
    *, with_yo, each, rblk,
):
    gx_index, gy_index = lax.axis_index("gx"), lax.axis_index("gy")
    pairs = ((cur_in, cur), (col_in, col), (rb_in, rb), (traces_in, traces))
    copies = [pltpu.make_async_copy(src, dst, sems.at[i]) for i, (src, dst) in enumerate(pairs)]
    for copy in copies:
        copy.start()
    nz = toeplitz.shape[1]
    distance = jnp.abs(
        lax.broadcasted_iota(jnp.int32, (nz, nz), 0) - lax.broadcasted_iota(jnp.int32, (nz, nz), 1)
    )
    band = jnp.where(distance == 0, 3.0 * LAPLACE_COEFS[0], 0.0)
    for k in range(1, REACH + 1):
        band = band + jnp.where(distance == k, LAPLACE_COEFS[k], 0.0)
    hi, lo = split2(band)
    toeplitz[0:nz, :] = hi
    toeplitz[nz : 2 * nz, :] = lo
    for copy in copies[1:]:
        copy.wait()
    wide = jnp.concatenate([col[...]] * 3, axis=1)
    rows = lax.broadcasted_iota(jnp.int32, select.shape, 0)
    select[...] = jnp.where(rows == wide, 1.0, 0.0).astype(BF16)
    slot_owners(rb, counts, owners, each, rblk)
    steps, per = traces.shape[1:]
    own[...] = jnp.zeros(own.shape, F32)
    own[0, 0:steps, 0:per] = traces[0].astype(F32)
    copies[0].wait()
    put_faces(cur, gx_index, gy_index, ye, yo if with_yo else None, xe, None)


def slot_owners(rb, counts, owners, each, rblk):
    me = lax.axis_index("gx") * lax.axis_size("gy") + lax.axis_index("gy")
    slots, lanes = owners.shape
    eye = lax.broadcasted_iota(jnp.int32, (slots, slots), 0) == lax.broadcasted_iota(jnp.int32, (slots, slots), 1)
    block_of = jnp.sum(jnp.where(eye, jnp.broadcast_to(rb[...], (slots, slots)), 0), axis=1, keepdims=True)
    owner = lax.div(block_of, jnp.int32(each))
    group = block_of - owner * each
    lane = lax.broadcasted_iota(jnp.int32, (slots, lanes), 1)
    live = lax.broadcasted_iota(jnp.int32, (slots, lanes), 0) < counts[0, 0]
    used = jnp.logical_and(live, lax.div(lane, jnp.int32(rblk)) == group)
    owners[...] = jnp.where(used, jnp.bitwise_xor(owner, me), -1)


def flush_kernel(a_in, b_in, a_out, b_out, sems):
    copies = [
        pltpu.make_async_copy(src, dst, sems.at[i]) for i, (src, dst) in enumerate(((a_in, a_out), (b_in, b_out)))
    ]
    for copy in copies:
        copy.start()
    for copy in copies:
        copy.wait()


def update(cur, prev, c2, toeplitz, out, ypad, source=None, fine=None):
    cx, cy, nz = cur.shape
    w = LAPLACE_COEFS
    zero = jnp.zeros((8, nz), F32)
    for x in range(cx):
        ypad[x, 0:8, :] = zero
        ypad[x, 8 : 8 + cy, :] = cur[x, :, :]
        ypad[x, 8 + cy : 16 + cy, :] = zero
    chunk = CHUNK
    rows = chunk * cy
    t_hi = toeplitz[0:nz, :]
    t_lo = toeplitz[nz : 2 * nz, :]
    for m in range(cx // chunk):
        v = cur[m * chunk : (m + 1) * chunk, :, :].reshape(rows, nz)
        hi, lo = split2(v)
        lz = dot(hi, t_hi) + dot(lo, t_hi) + dot(hi, t_lo)
        if source is not None:
            select, contrib = source
            src = dot(select[m * rows : (m + 1) * rows, :], contrib)
        for j in range(chunk):
            x = m * chunk + j
            total = lz[j * cy : (j + 1) * cy, :]
            for k in range(1, REACH + 1):
                pair = ypad[x, 8 - k : 8 - k + cy, :] + ypad[x, 8 + k : 8 + k + cy, :]
                if x - k >= 0:
                    pair = pair + cur[x - k, :, :]
                if x + k < cx:
                    pair = pair + cur[x + k, :, :]
                total = total + w[k] * pair
            if prev is None:
                out[x, :, :] = total
                continue
            here = cur[x, :, :]
            value = (2.0 * here - prev[x, :, :]) + c2[x, :, :] * total
            if source is not None:
                value = value + src[j * cy : (j + 1) * cy, :]
            out[x, :, :] = value
            if fine is not None:
                fine_in, accel, fine_out = fine
                term = accel[x, :, :].astype(F32) * here
                fine_out[x, :, :] = term if fine_in is None else fine_in[x, :, :] + term


def first_update_kernel(cur, toeplitz, prev_in, c2_in, weights_in, out, prev, c2, weights, ypad, sems):
    copies = [
        pltpu.make_async_copy(src, dst, sems.at[i])
        for i, (src, dst) in enumerate(((prev_in, prev), (c2_in, c2), (weights_in, weights)))
    ]
    for copy in copies:
        copy.start()
    update(cur, None, None, toeplitz, out, ypad)
    copies[0].wait()
    copies[1].wait()
    for x in range(cur.shape[0]):
        out[x, :, :] = (2.0 * cur[x, :, :] - prev[x, :, :]) + c2[x, :, :] * out[x, :, :]
    copies[2].wait()


def update_kernel(cur, prev, c2, toeplitz, select, contrib, accel, *rest, step):
    if step == 1:
        out, fine_out, ypad = rest
        fine_in = None
    else:
        fine_in, out, fine_out, ypad = rest
    update(
        cur, prev, c2, toeplitz, out, ypad,
        source=(select, contrib[step]), fine=(fine_in, accel.at[step - 1], fine_out),
    )


def contributions(owners, weights, blocks, patterns, contrib, wide):
    slots, rblk, nz = weights.shape
    steps = contrib.shape[0]
    lanes = 128
    picked = [jnp.zeros((slots, lanes), F32) for _ in range(steps)]
    for tile, pattern in zip(blocks, patterns):
        mask = owners[...] == pattern
        for t in range(steps):
            picked[t] = jnp.where(mask, tile[t : t + 1, :], picked[t])
    spread = (
        lax.rem(lax.broadcasted_iota(jnp.int32, (lanes, lanes), 0), jnp.int32(rblk))
        == lax.rem(lax.broadcasted_iota(jnp.int32, (lanes, lanes), 1), jnp.int32(rblk))
    )
    spread = jnp.where(spread, 1.0, 0.0).astype(BF16)
    tiled = [dot(p.astype(BF16), spread) for p in picked]
    together = lanes // rblk
    diagonal = lax.broadcasted_iota(jnp.int32, (together, lanes), 0) == lax.div(
        lax.broadcasted_iota(jnp.int32, (together, lanes), 1), jnp.int32(rblk)
    )
    for q in range(slots // together):
        rows = slice(q * together, (q + 1) * together)
        left = jnp.concatenate([jnp.where(diagonal, v[rows, :], 0.0) for v in tiled], axis=0).astype(BF16)
        right = weights[q * together : (q + 1) * together, :, :].reshape(together * rblk, nz)
        got = dot(left, right)
        for t in range(steps):
            wide[t, rows, :] = got[t * together : (t + 1) * together, :]
    for t in range(steps):
        hi, mid = split2(wide[t, :, :])
        rest = wide[t, :, :] - hi.astype(F32) - mid.astype(F32)
        contrib[t, 0:slots, :] = hi
        contrib[t, slots : 2 * slots, :] = mid
        contrib[t, 2 * slots : 3 * slots, :] = rest.astype(BF16)


def unpack(refs, with_yo, with_xo):
    refs = list(refs)
    ye = refs.pop(0)
    yo = refs.pop(0) if with_yo else None
    xe = refs.pop(0)
    xo = refs.pop(0) if with_xo else None
    return ye, yo, xe, xo, refs


def first_correct_kernel(owners, weights, select, part, c2, *refs, with_yo, with_xo, patterns):
    gx_index, gy_index = lax.axis_index("gx"), lax.axis_index("gy")
    ye, yo, xe, xo, refs = unpack(refs, with_yo, with_xo)
    pairs, refs = refs[0], refs[1:]
    nxt, contrib, refs = refs[0], refs[1], refs[2:]
    oye, oyo, oxe, oxo, refs = unpack(refs, with_yo, with_xo)
    wide = refs[0]
    lanes = 128
    tiles = []
    n = pairs.shape[0]
    y_last, x_last = ye.shape[0] - n, xe.shape[0] - 2 * n
    for ref, first in ((pairs, 0), (ye, y_last), (xe, x_last), (xe, x_last + n)):
        for i in range(n):
            tiles += [ref[first + i][:, 0:lanes], ref[first + i][:, lanes : 2 * lanes]]
    contributions(owners, weights, tiles, patterns, contrib, wide)
    cx, cy, nz = nxt.shape
    chunk = 8
    rows = chunk * cy
    for m in range(cx // chunk):
        src = dot(select[m * rows : (m + 1) * rows, :], contrib[0])
        at = slice(m * chunk, (m + 1) * chunk)
        nxt[at, :, :] = part[at, :, :] + src.reshape(chunk, cy, nz)
    add_halos(nxt, c2, gx_index, gy_index, ye, yo, xe, xo)
    put_faces(nxt, gx_index, gy_index, oye, oyo, oxe, oxo)


def correct_kernel(part, c2, *refs, with_yo, with_xo):
    gx_index, gy_index = lax.axis_index("gx"), lax.axis_index("gy")
    ye, yo, xe, xo, refs = unpack(refs, with_yo, with_xo)
    nxt, refs = refs[0], refs[1:]
    oye, oyo, oxe, oxo, refs = unpack(refs, with_yo, with_xo)
    nxt[...] = part[...]
    add_halos(nxt, c2, gx_index, gy_index, ye, yo, xe, xo)
    put_faces(nxt, gx_index, gy_index, oye, oyo, oxe, oxo)


def last_kernel(part, c2, accel, fine, *refs, with_yo, with_xo, step):
    gx_index, gy_index = lax.axis_index("gx"), lax.axis_index("gy")
    ye, yo, xe, xo, refs = unpack(refs, with_yo, with_xo)
    nxt, coarse, middle = refs
    cx, cy, nz = nxt.shape
    nxt[...] = part[...]
    add_halos(nxt, c2, gx_index, gy_index, ye, yo, xe, xo)
    pairs = lax.div(lax.broadcasted_iota(jnp.int32, (nz, nz // 2), 0), jnp.int32(2)) == lax.broadcasted_iota(
        jnp.int32, (nz, nz // 2), 1
    )
    pairs = jnp.where(pairs, 0.125, 0.0).astype(BF16)
    chunk = 8
    for m in range(cx // (2 * chunk)):
        summed = []
        for j in range(chunk):
            x = 2 * (m * chunk + j)
            a = fine[x, :, :] + accel[step, x, :, :].astype(F32) * nxt[x, :, :]
            b = fine[x + 1, :, :] + accel[step, x + 1, :, :].astype(F32) * nxt[x + 1, :, :]
            summed.append(a + b)
        hi, lo = split2(jnp.concatenate(summed, axis=0))
        got = dot(hi, pairs) + dot(lo, pairs)
        middle[m * chunk * cy : (m + 1) * chunk * cy, :] = got
    half = cx * cy // 4
    both = middle[pl.ds(0, half, 2), :] + middle[pl.ds(1, half, 2), :]
    coarse[...] = both.reshape(coarse.shape)


def local(adj_prev, adj_cur, fwd_accel, courant2, traces, weights, rblock, column, counts):
    accel = fwd_accel[0]
    cx, cy, nz = courant2.shape
    steps = accel.shape[0]
    slots, rblk = weights.shape[2:4]
    per = traces.shape[2]
    nx, ny, nshot = lax.axis_size("gx"), lax.axis_size("gy"), lax.axis_size("shot")
    with_yo, with_xo = ny > 2, nx > 2
    y_msg, x_msg = (cx // 2, 8, nz), (REACH * cy // 8, 8, nz)
    tile = (cx, cy, nz)
    cells = cx * cy * nz
    lanes = 128

    def swap(x, axis, pairs=None):
        return odd_swap(x, axis) if pairs is None else lax.ppermute(x, axis, pairs)

    def xor(size, bit):
        return [(i, i ^ bit) for i in range(size)]

    blocks, others, patterns = traces, [], [0]
    for axis, size, stride in (("gy", ny, 1), ("gx", nx, ny)):
        bit = 2
        while bit < size:
            got = swap(blocks, axis, xor(size, bit))
            others.append(got)
            patterns = patterns + [p ^ (bit * stride) for p in patterns]
            bit *= 2
            if bit < size or (axis == "gy" and nx > 2):
                blocks = jnp.concatenate([blocks, got], axis=0)
    if not others:
        others, patterns = [jnp.zeros_like(traces)], [0, -2]
    cur, ye, yo, xe, toeplitz, select, owners, own = vmem_call(
        functools.partial(load_kernel, with_yo=with_yo, each=per // rblk, rblk=rblk),
        [
            sds(tile), sds(y_msg), sds(y_msg), sds(x_msg), sds((2 * nz, nz), BF16),
            sds((cx * cy, 3 * slots), BF16), sds((slots, lanes), jnp.int32), sds((1, 8, lanes)),
        ],
        [adj_cur[0], column[0], rblock[0], traces, counts],
        [
            pltpu.VMEM((1, slots), jnp.int32), pltpu.VMEM((1, slots), jnp.int32), pltpu.VMEM((1, steps, per), BF16),
            pltpu.SemaphoreType.DMA((4,)),
        ],
        hbm_in=(0, 1, 2, 3), smem_in=(4,),
    )
    others = [jnp.pad(a.astype(F32), ((0, 0), (0, 8 - steps), (0, lanes - per))) for a in others]
    tiles = jnp.concatenate([own] + others, axis=0)
    pairs = jnp.concatenate([tiles[0::2], tiles[1::2]], axis=2)
    rye = swap(jnp.concatenate([ye, pairs], axis=0), "gy", even_pairs(ny))
    ryo = swap(yo, "gy") if with_yo else None
    rxo = None
    if with_xo:
        low = cur[0:REACH].reshape(x_msg)
        high = cur[cx - REACH :].reshape(x_msg)
        rxo = swap(jnp.where(lax.axis_index("gx") % 2 == 0, low, high), "gx")
    rxe = swap(jnp.concatenate([xe, pairs, rye[y_msg[0] :]], axis=0), "gx", even_pairs(nx))
    for stride in (1, ny):
        patterns = patterns + [p ^ stride if p >= 0 else p for p in patterns]

    ypad = pltpu.VMEM((cx, cy + 16, nz), F32)
    part, _, c2, wts = vmem_call(
        first_update_kernel,
        [sds(tile), sds(tile), sds(tile), sds((slots, rblk, nz), BF16)],
        [cur, toeplitz, adj_prev[0], courant2, weights[0, 0]],
        [ypad, pltpu.SemaphoreType.DMA((3,))],
        hbm_in=(2, 3, 4), flops=cells * 60,
    )

    def given(ye, yo, xe, xo):
        return [a for a in (ye, yo, xe, xo) if a is not None]

    def face_shapes():
        return given(sds(y_msg), sds(y_msg) if with_yo else None, sds(x_msg), sds(x_msg) if with_xo else None)

    def taken(faces):
        faces = list(faces)
        ye = faces.pop(0)
        yo = faces.pop(0) if with_yo else None
        xe = faces.pop(0)
        xo = faces.pop(0) if with_xo else None
        return ye, yo, xe, xo

    nxt, contrib, *faces = vmem_call(
        functools.partial(
            first_correct_kernel, with_yo=with_yo, with_xo=with_xo, patterns=tuple(patterns)
        ),
        [sds(tile), sds((steps, 3 * slots, nz), BF16)] + face_shapes(),
        [owners, wts, select, part, c2] + given(rye, ryo, rxe, rxo) + [pairs],
        [pltpu.VMEM((steps, slots, nz), F32)],
    )
    previous, current = cur, nxt
    fine = None
    for step in range(1, steps):
        ye, yo, xe, xo = taken(faces)
        ryo = swap(yo, "gy") if with_yo else None
        rxe = swap(xe, "gx", even_pairs(nx))
        rxo = swap(xo, "gx") if with_xo else None
        rye = swap(ye, "gy", even_pairs(ny))
        args = [current, previous, c2, toeplitz, select, contrib, accel]
        if fine is not None:
            args.append(fine)
        part, fine = vmem_call(
            functools.partial(update_kernel, step=step), [sds(tile), sds(tile)], args, [ypad],
            flops=cells * 60,
        )
        halos = given(rye, ryo, rxe, rxo)
        if step < steps - 1:
            nxt, *faces = vmem_call(
                functools.partial(correct_kernel, with_yo=with_yo, with_xo=with_xo),
                [sds(tile)] + face_shapes(),
                [part, c2] + halos,
            )
        else:
            nxt, coarse = vmem_call(
                functools.partial(last_kernel, with_yo=with_yo, with_xo=with_xo, step=step),
                [sds(tile), sds((cx // 2, cy // 2, nz // 2))],
                [part, c2, accel, fine] + halos,
                [pltpu.VMEM((cx * cy // 2, nz // 2), F32)],
            )
        previous, current = current, nxt
    bit = 1
    while bit < nshot:
        one = swap(coarse, "shot", xor(nshot, bit))
        if nshot % (4 * bit) == 0:
            two = swap(coarse, "shot", xor(nshot, 2 * bit))
            three = swap(coarse, "shot", xor(nshot, 3 * bit))
            coarse = (coarse + one) + (two + three)
            bit *= 4
        else:
            coarse = coarse + one
            bit *= 2
    previous, current = vmem_call(
        flush_kernel, [sds(tile), sds(tile)], [previous, current], [pltpu.SemaphoreType.DMA((2,))],
        hbm_out=(0, 1),
    )
    return (previous[None], current[None], coarse)


def solution(mesh):
    return jax.shard_map(
        local,
        mesh=mesh,
        in_specs=(
            P("shot", "gx", "gy", None),
            P("shot", "gx", "gy", None),
            P("shot", None, "gx", "gy", None),
            P("gx", "gy", None),
            P("shot", None, ("gx", "gy")),
            P("gx", "gy", None, None, None),
            P("gx", "gy", None),
            P("gx", "gy", None),
            P("gx", "gy"),
        ),
        out_specs=(P("shot", "gx", "gy", None), P("shot", "gx", "gy", None), P("gx", "gy", None)),
        check_vma=False,
    )
```

```python
import functools

import jax
import jax.numpy as jnp
from jax import lax
from jax.experimental import pallas as pl
from jax.experimental.pallas import tpu as pltpu
from jax.sharding import PartitionSpec as P


LAPLACE_COEFS = (-205.0 / 72.0, 8.0 / 5.0, -1.0 / 5.0, 8.0 / 315.0, -1.0 / 560.0)
REACH = 4
CHUNK = 8
VMEM_LIMIT = 16 << 20
F32 = jnp.float32
BF16 = jnp.bfloat16


def vmem_call(kernel, outs, args, scratch=(), flops=0, hbm_in=(), hbm_out=(), smem_in=()):
    in_specs = [
        pl.BlockSpec(memory_space=pltpu.HBM if i in hbm_in else pltpu.SMEM if i in smem_in else pltpu.VMEM)
        for i in range(len(args))
    ]
    args = [pltpu.with_memory_space_constraint(a, pltpu.HBM) if i in hbm_in else a for i, a in enumerate(args)]
    moved = sum(a.size * a.dtype.itemsize for a in args) + sum(o.size * o.dtype.itemsize for o in outs)
    return pl.pallas_call(
        kernel,
        out_shape=tuple(outs),
        in_specs=in_specs,
        out_specs=tuple(
            pl.BlockSpec(memory_space=pltpu.HBM if i in hbm_out else pltpu.VMEM) for i in range(len(outs))
        ),
        scratch_shapes=list(scratch),
        cost_estimate=pl.CostEstimate(flops=flops, bytes_accessed=moved, transcendentals=0),
        compiler_params=pltpu.CompilerParams(vmem_limit_bytes=VMEM_LIMIT),
    )(*args)


def sds(shape, dtype=F32):
    return jax.ShapeDtypeStruct(shape, dtype)


def even_pairs(n):
    pairs = []
    for i in range(0, n - 1, 2):
        pairs += [(i, i + 1), (i + 1, i)]
    return pairs


def odd_swap(x, axis):
    n, shots = lax.axis_size(axis), lax.axis_size("shot")
    if shots % 2:
        pairs = [(0, n - 1), (n - 1, 0)]
        for i in range(1, n - 1, 2):
            pairs += [(i, i + 1), (i + 1, i)]
        return lax.ppermute(x, axis, pairs)
    pairs = []
    for s in range(shots):
        for i in (0, n - 1):
            pairs.append((i * shots + s, i * shots + (s ^ 1)))
        for i in range(1, n - 1, 2):
            pairs += [(i * shots + s, (i + 1) * shots + s), ((i + 1) * shots + s, i * shots + s)]
    return lax.ppermute(x, (axis, "shot"), pairs)


def split2(v):
    hi = v.astype(BF16)
    return hi, (v - hi.astype(F32)).astype(BF16)


def dot(a, b):
    return jnp.dot(a, b, preferred_element_type=F32)


def put_y_face(cur, out, stage, high):
    cx, cy, _ = cur.shape
    start = cy - REACH if high else 0
    for h in range(stage.shape[0]):
        at = slice(h * 128, (h + 1) * 128)
        for x in range(cx):
            stage[h, REACH * x : REACH * (x + 1), :] = cur[x, start : start + REACH, at]
        out[0 : REACH * cx, at] = stage[h, :, :].astype(BF16)
        near = stage[h, pl.ds(REACH - 1 if high else 0, cx, REACH), :]
        out[REACH * cx : (REACH + 1) * cx, at] = split2(near)[1]


def put_x_face(cur, out, high):
    cx, cy, _ = cur.shape
    low = jnp.where(high, cx - REACH, 0)
    for r in range(REACH):
        out[r * cy : (r + 1) * cy, :] = cur[low + r, :, :].astype(BF16)
    out[REACH * cy : (REACH + 1) * cy, :] = split2(cur[jnp.where(high, cx - 1, 0), :, :])[1]


def put_faces(cur, gx_index, gy_index, ye, yo, xe, xo, stage):
    y_even = gy_index % 2 == 0
    x_even = gx_index % 2 == 0

    @pl.when(y_even)
    def _():
        put_y_face(cur, ye, stage, True)
        if yo is not None:
            put_y_face(cur, yo, stage, False)

    @pl.when(jnp.logical_not(y_even))
    def _():
        put_y_face(cur, ye, stage, False)
        if yo is not None:
            put_y_face(cur, yo, stage, True)

    put_x_face(cur, xe, x_even)
    if xo is not None:
        put_x_face(cur, xo, jnp.logical_not(x_even))


def add_y_halo(nxt, c2, recv, stage, high):
    cx, cy, nz = nxt.shape
    w = LAPLACE_COEFS
    near = pl.ds(0 if high else REACH - 1, cx, REACH)
    for h in range(stage.shape[0]):
        at = slice(h * 128, (h + 1) * 128)
        stage[h, :, :] = recv[0 : REACH * cx, at].astype(F32)
        stage[h, near, :] = stage[h, near, :] + recv[REACH * cx : (REACH + 1) * cx, at].astype(F32)
    row = lax.broadcasted_iota(jnp.int32, (8, nz), 0) % REACH
    coefs = {}
    for k in range(1, REACH + 1):
        shift = REACH - k
        keep = (row >= shift) if high else (row < k)
        coefs[k] = jnp.where(keep, w[k], 0.0)
    start = cy - REACH if high else 0
    for i in range(cx // 2):
        m = jnp.concatenate([stage[h, 8 * i : 8 * i + 8, :] for h in range(stage.shape[0])], axis=1)
        total = w[REACH] * m
        for k in range(1, REACH):
            shift = REACH - k
            total = total + coefs[k] * pltpu.roll(m, shift if high else 8 - shift, 0)
        for h in range(2):
            rows = slice(start, start + REACH)
            nxt[2 * i + h, rows, :] = (
                nxt[2 * i + h, rows, :] + c2[2 * i + h, rows, :] * total[REACH * h : REACH * h + REACH, :]
            )


def add_x_halo(nxt, c2, recv, stage, high):
    cx, cy, _ = nxt.shape
    w = LAPLACE_COEFS
    layers = [recv[r * cy : (r + 1) * cy, :].astype(F32) for r in range(REACH + 1)]
    near = 0 if high else REACH - 1
    layers[near] = layers[near] + layers[REACH]
    for r in range(REACH):
        x = cx - 1 - r if high else r
        total = None
        for k in range(r + 1, REACH + 1):
            term = w[k] * layers[(k - r - 1) if high else (REACH + r - k)]
            total = term if total is None else total + term
        nxt[x, :, :] = nxt[x, :, :] + c2[x, :, :] * total


def add_halos(nxt, c2, gx_index, gy_index, ye, yo, xe, xo, stage):
    for axis, index, even, odd, add in (("gy", gy_index, ye, yo, add_y_halo), ("gx", gx_index, xe, xo, add_x_halo)):
        is_even = index % 2 == 0
        inner = jnp.logical_and(index > 0, index < lax.axis_size(axis) - 1)

        @pl.when(is_even)
        def _(even=even, add=add):
            add(nxt, c2, even, stage, True)

        @pl.when(jnp.logical_not(is_even))
        def _(even=even, add=add):
            add(nxt, c2, even, stage, False)

        if odd is not None:

            @pl.when(jnp.logical_and(inner, is_even))
            def _(odd=odd, add=add):
                add(nxt, c2, odd, stage, False)

            @pl.when(jnp.logical_and(inner, jnp.logical_not(is_even)))
            def _(odd=odd, add=add):
                add(nxt, c2, odd, stage, True)


def load_kernel(
    cur_in, col_in, rb_in, traces_in, counts, cur, toeplitz, select, owners, own, *refs,
    with_yo, with_xo, each, rblk,
):
    ye, yo, xe, xo, (col, rb, traces, stage, sems) = unpack(refs, with_yo, with_xo)
    gx_index, gy_index = lax.axis_index("gx"), lax.axis_index("gy")
    pairs = ((cur_in, cur), (col_in, col), (rb_in, rb), (traces_in, traces))
    copies = [pltpu.make_async_copy(src, dst, sems.at[i]) for i, (src, dst) in enumerate(pairs)]
    for copy in copies:
        copy.start()
    nz = toeplitz.shape[1]
    distance = jnp.abs(
        lax.broadcasted_iota(jnp.int32, (nz, nz), 0) - lax.broadcasted_iota(jnp.int32, (nz, nz), 1)
    )
    band = jnp.where(distance == 0, 3.0 * LAPLACE_COEFS[0], 0.0)
    for k in range(1, REACH + 1):
        band = band + jnp.where(distance == k, LAPLACE_COEFS[k], 0.0)
    hi, lo = split2(band)
    toeplitz[0:nz, :] = hi
    toeplitz[nz : 2 * nz, :] = lo
    for copy in copies[1:]:
        copy.wait()
    wide = jnp.concatenate([col[...]] * 3, axis=1)
    rows = lax.broadcasted_iota(jnp.int32, select.shape, 0)
    select[...] = jnp.where(rows == wide, 1.0, 0.0).astype(BF16)
    slot_owners(rb, counts, owners, each, rblk)
    steps, per = traces.shape[1:]
    own[...] = jnp.zeros(own.shape, F32)
    own[0, 0:steps, 0:per] = traces[0].astype(F32)
    copies[0].wait()
    put_faces(cur, gx_index, gy_index, ye, yo, xe, xo, stage)


def slot_owners(rb, counts, owners, each, rblk):
    me = lax.axis_index("gx") * lax.axis_size("gy") + lax.axis_index("gy")
    slots, lanes = owners.shape
    eye = lax.broadcasted_iota(jnp.int32, (slots, slots), 0) == lax.broadcasted_iota(jnp.int32, (slots, slots), 1)
    block_of = jnp.sum(jnp.where(eye, jnp.broadcast_to(rb[...], (slots, slots)), 0), axis=1, keepdims=True)
    owner = lax.div(block_of, jnp.int32(each))
    group = block_of - owner * each
    lane = lax.broadcasted_iota(jnp.int32, (slots, lanes), 1)
    live = lax.broadcasted_iota(jnp.int32, (slots, lanes), 0) < counts[0, 0]
    used = jnp.logical_and(live, lax.div(lane, jnp.int32(rblk)) == group)
    owners[...] = jnp.where(used, jnp.bitwise_xor(owner, me), -1)


def flush_kernel(a_in, b_in, a_out, b_out, sems):
    copies = [
        pltpu.make_async_copy(src, dst, sems.at[i]) for i, (src, dst) in enumerate(((a_in, a_out), (b_in, b_out)))
    ]
    for copy in copies:
        copy.start()
    for copy in copies:
        copy.wait()


def update(cur, prev, c2, toeplitz, out, ypad, source=None, fine=None):
    cx, cy, nz = cur.shape
    w = LAPLACE_COEFS
    zero = jnp.zeros((8, nz), F32)
    for x in range(cx):
        ypad[x, 0:8, :] = zero
        ypad[x, 8 : 8 + cy, :] = cur[x, :, :]
        ypad[x, 8 + cy : 16 + cy, :] = zero
    chunk = CHUNK
    rows = chunk * cy
    t_hi = toeplitz[0:nz, :]
    t_lo = toeplitz[nz : 2 * nz, :]
    for m in range(cx // chunk):
        v = cur[m * chunk : (m + 1) * chunk, :, :].reshape(rows, nz)
        hi, lo = split2(v)
        lz = dot(hi, t_hi) + dot(lo, t_hi) + dot(hi, t_lo)
        if source is not None:
            select, contrib = source
            src = dot(select[m * rows : (m + 1) * rows, :], contrib)
        for j in range(chunk):
            x = m * chunk + j
            total = lz[j * cy : (j + 1) * cy, :]
            for k in range(1, REACH + 1):
                pair = ypad[x, 8 - k : 8 - k + cy, :] + ypad[x, 8 + k : 8 + k + cy, :]
                if x - k >= 0:
                    pair = pair + cur[x - k, :, :]
                if x + k < cx:
                    pair = pair + cur[x + k, :, :]
                total = total + w[k] * pair
            if prev is None:
                out[x, :, :] = total
                continue
            here = cur[x, :, :]
            value = (2.0 * here - prev[x, :, :]) + c2[x, :, :] * total
            if source is not None:
                value = value + src[j * cy : (j + 1) * cy, :]
            out[x, :, :] = value
            if fine is not None:
                fine_in, accel, fine_out = fine
                term = accel[x, :, :].astype(F32) * here
                fine_out[x, :, :] = term if fine_in is None else fine_in[x, :, :] + term


def first_update_kernel(cur, toeplitz, prev_in, c2_in, weights_in, out, prev, c2, weights, ypad, sems):
    copies = [
        pltpu.make_async_copy(src, dst, sems.at[i])
        for i, (src, dst) in enumerate(((prev_in, prev), (c2_in, c2), (weights_in, weights)))
    ]
    for copy in copies:
        copy.start()
    update(cur, None, None, toeplitz, out, ypad)
    copies[0].wait()
    copies[1].wait()
    for x in range(cur.shape[0]):
        out[x, :, :] = (2.0 * cur[x, :, :] - prev[x, :, :]) + c2[x, :, :] * out[x, :, :]
    copies[2].wait()


def update_kernel(cur, prev, c2, toeplitz, select, contrib, accel, *rest, step):
    if step == 1:
        out, fine_out, ypad = rest
        fine_in = None
    else:
        fine_in, out, fine_out, ypad = rest
    update(
        cur, prev, c2, toeplitz, out, ypad,
        source=(select, contrib[step]), fine=(fine_in, accel.at[step - 1], fine_out),
    )


def contributions(owners, weights, blocks, patterns, contrib, wide):
    slots, rblk, nz = weights.shape
    steps = contrib.shape[0]
    lanes = 128
    picked = [jnp.zeros((slots, lanes), F32) for _ in range(steps)]
    for tile, pattern in zip(blocks, patterns):
        mask = owners[...] == pattern
        for t in range(steps):
            picked[t] = jnp.where(mask, tile[t : t + 1, :], picked[t])
    spread = (
        lax.rem(lax.broadcasted_iota(jnp.int32, (lanes, lanes), 0), jnp.int32(rblk))
        == lax.rem(lax.broadcasted_iota(jnp.int32, (lanes, lanes), 1), jnp.int32(rblk))
    )
    spread = jnp.where(spread, 1.0, 0.0).astype(BF16)
    tiled = [dot(p.astype(BF16), spread) for p in picked]
    together = lanes // rblk
    diagonal = lax.broadcasted_iota(jnp.int32, (together, lanes), 0) == lax.div(
        lax.broadcasted_iota(jnp.int32, (together, lanes), 1), jnp.int32(rblk)
    )
    for q in range(slots // together):
        rows = slice(q * together, (q + 1) * together)
        left = jnp.concatenate([jnp.where(diagonal, v[rows, :], 0.0) for v in tiled], axis=0).astype(BF16)
        right = weights[q * together : (q + 1) * together, :, :].reshape(together * rblk, nz)
        got = dot(left, right)
        for t in range(steps):
            wide[t, rows, :] = got[t * together : (t + 1) * together, :]
    for t in range(steps):
        hi, mid = split2(wide[t, :, :])
        rest = wide[t, :, :] - hi.astype(F32) - mid.astype(F32)
        contrib[t, 0:slots, :] = hi
        contrib[t, slots : 2 * slots, :] = mid
        contrib[t, 2 * slots : 3 * slots, :] = rest.astype(BF16)


def unpack(refs, with_yo, with_xo):
    refs = list(refs)
    ye = refs.pop(0)
    yo = refs.pop(0) if with_yo else None
    xe = refs.pop(0)
    xo = refs.pop(0) if with_xo else None
    return ye, yo, xe, xo, refs


def first_correct_kernel(owners, weights, select, part, c2, *refs, with_yo, with_xo, patterns):
    gx_index, gy_index = lax.axis_index("gx"), lax.axis_index("gy")
    ye, yo, xe, xo, refs = unpack(refs, with_yo, with_xo)
    pairs, refs = refs[0], refs[1:]
    nxt, contrib, refs = refs[0], refs[1], refs[2:]
    oye, oyo, oxe, oxo, refs = unpack(refs, with_yo, with_xo)
    wide, stage = refs
    lanes = 128
    tiles = []
    rows = pairs.shape[0]
    y_last, x_last = ye.shape[0] - rows, xe.shape[0] - 2 * rows
    for block in (pairs[...], ye[y_last : y_last + rows, :], xe[x_last : x_last + 2 * rows, :]):
        block = block.astype(F32)
        for i in range(0, block.shape[0], 8):
            tiles += [block[i : i + 8, 0:lanes], block[i : i + 8, lanes : 2 * lanes]]
    contributions(owners, weights, tiles, patterns, contrib, wide)
    cx, cy, nz = nxt.shape
    chunk = 8
    rows = chunk * cy
    for m in range(cx // chunk):
        src = dot(select[m * rows : (m + 1) * rows, :], contrib[0])
        at = slice(m * chunk, (m + 1) * chunk)
        nxt[at, :, :] = part[at, :, :] + src.reshape(chunk, cy, nz)
    add_halos(nxt, c2, gx_index, gy_index, ye, yo, xe, xo, stage)
    put_faces(nxt, gx_index, gy_index, oye, oyo, oxe, oxo, stage)


def correct_kernel(part, c2, *refs, with_yo, with_xo):
    gx_index, gy_index = lax.axis_index("gx"), lax.axis_index("gy")
    ye, yo, xe, xo, refs = unpack(refs, with_yo, with_xo)
    nxt, refs = refs[0], refs[1:]
    oye, oyo, oxe, oxo, (stage,) = unpack(refs, with_yo, with_xo)
    nxt[...] = part[...]
    add_halos(nxt, c2, gx_index, gy_index, ye, yo, xe, xo, stage)
    put_faces(nxt, gx_index, gy_index, oye, oyo, oxe, oxo, stage)


def last_kernel(part, c2, accel, fine, *refs, with_yo, with_xo, step):
    gx_index, gy_index = lax.axis_index("gx"), lax.axis_index("gy")
    ye, yo, xe, xo, refs = unpack(refs, with_yo, with_xo)
    nxt, coarse, middle, stage = refs
    cx, cy, nz = nxt.shape
    nxt[...] = part[...]
    add_halos(nxt, c2, gx_index, gy_index, ye, yo, xe, xo, stage)
    pairs = lax.div(lax.broadcasted_iota(jnp.int32, (nz, nz // 2), 0), jnp.int32(2)) == lax.broadcasted_iota(
        jnp.int32, (nz, nz // 2), 1
    )
    pairs = jnp.where(pairs, 0.125, 0.0).astype(BF16)
    chunk = 8
    for m in range(cx // (2 * chunk)):
        summed = []
        for j in range(chunk):
            x = 2 * (m * chunk + j)
            a = fine[x, :, :] + accel[step, x, :, :].astype(F32) * nxt[x, :, :]
            b = fine[x + 1, :, :] + accel[step, x + 1, :, :].astype(F32) * nxt[x + 1, :, :]
            summed.append(a + b)
        hi, lo = split2(jnp.concatenate(summed, axis=0))
        got = dot(hi, pairs) + dot(lo, pairs)
        middle[m * chunk * cy : (m + 1) * chunk * cy, :] = got
    half = cx * cy // 4
    both = middle[pl.ds(0, half, 2), :] + middle[pl.ds(1, half, 2), :]
    coarse[...] = both.reshape(coarse.shape)


def local(adj_prev, adj_cur, fwd_accel, courant2, traces, weights, rblock, column, counts):
    accel = fwd_accel[0]
    cx, cy, nz = courant2.shape
    steps = accel.shape[0]
    slots, rblk = weights.shape[2:4]
    per = traces.shape[2]
    nx, ny, nshot = lax.axis_size("gx"), lax.axis_size("gy"), lax.axis_size("shot")
    with_yo, with_xo = ny > 2, nx > 2
    y_msg, x_msg = ((REACH + 1) * cx, nz), ((REACH + 1) * cy, nz)
    tile = (cx, cy, nz)
    cells = cx * cy * nz
    lanes = 128

    def swap(x, axis, pairs=None):
        return odd_swap(x, axis) if pairs is None else lax.ppermute(x, axis, pairs)

    def xor(size, bit):
        return [(i, i ^ bit) for i in range(size)]

    def given(ye, yo, xe, xo):
        return [a for a in (ye, yo, xe, xo) if a is not None]

    def face_shapes():
        y, x = sds(y_msg, BF16), sds(x_msg, BF16)
        return given(y, y if with_yo else None, x, x if with_xo else None)

    def taken(faces):
        faces = list(faces)
        ye = faces.pop(0)
        yo = faces.pop(0) if with_yo else None
        xe = faces.pop(0)
        xo = faces.pop(0) if with_xo else None
        return ye, yo, xe, xo

    blocks, others, patterns = traces, [], [0]
    for axis, size, stride in (("gy", ny, 1), ("gx", nx, ny)):
        bit = 2
        while bit < size:
            got = swap(blocks, axis, xor(size, bit))
            others.append(got)
            patterns = patterns + [p ^ (bit * stride) for p in patterns]
            bit *= 2
            if bit < size or (axis == "gy" and nx > 2):
                blocks = jnp.concatenate([blocks, got], axis=0)
    if not others:
        others, patterns = [jnp.zeros_like(traces)], [0, -2]
    stage = pltpu.VMEM((nz // lanes, REACH * cx, lanes), F32)
    cur, toeplitz, select, owners, own, *faces = vmem_call(
        functools.partial(load_kernel, with_yo=with_yo, with_xo=with_xo, each=per // rblk, rblk=rblk),
        [
            sds(tile), sds((2 * nz, nz), BF16), sds((cx * cy, 3 * slots), BF16), sds((slots, lanes), jnp.int32),
            sds((1, 8, lanes)),
        ] + face_shapes(),
        [adj_cur[0], column[0], rblock[0], traces, counts],
        [
            pltpu.VMEM((1, slots), jnp.int32), pltpu.VMEM((1, slots), jnp.int32), pltpu.VMEM((1, steps, per), BF16),
            stage, pltpu.SemaphoreType.DMA((4,)),
        ],
        hbm_in=(0, 1, 2, 3), smem_in=(4,),
    )
    ye, yo, xe, xo = taken(faces)
    others = [jnp.pad(a.astype(F32), ((0, 0), (0, 8 - steps), (0, lanes - per))) for a in others]
    tiles = jnp.concatenate([own] + others, axis=0)
    pairs = jnp.concatenate([tiles[0::2], tiles[1::2]], axis=2).astype(BF16).reshape(-1, nz)
    rye = swap(jnp.concatenate([ye, pairs], axis=0), "gy", even_pairs(ny))
    ryo = swap(yo, "gy") if with_yo else None
    rxo = swap(xo, "gx") if with_xo else None
    rxe = swap(jnp.concatenate([xe, pairs, rye[y_msg[0] :]], axis=0), "gx", even_pairs(nx))
    for stride in (1, ny):
        patterns = patterns + [p ^ stride if p >= 0 else p for p in patterns]

    ypad = pltpu.VMEM((cx, cy + 16, nz), F32)
    part, _, c2, wts = vmem_call(
        first_update_kernel,
        [sds(tile), sds(tile), sds(tile), sds((slots, rblk, nz), BF16)],
        [cur, toeplitz, adj_prev[0], courant2, weights[0, 0]],
        [ypad, pltpu.SemaphoreType.DMA((3,))],
        hbm_in=(2, 3, 4), flops=cells * 60,
    )

    nxt, contrib, *faces = vmem_call(
        functools.partial(
            first_correct_kernel, with_yo=with_yo, with_xo=with_xo, patterns=tuple(patterns)
        ),
        [sds(tile), sds((steps, 3 * slots, nz), BF16)] + face_shapes(),
        [owners, wts, select, part, c2] + given(rye, ryo, rxe, rxo) + [pairs],
        [pltpu.VMEM((steps, slots, nz), F32), stage],
    )
    previous, current = cur, nxt
    fine = None
    for step in range(1, steps):
        ye, yo, xe, xo = taken(faces)
        ryo = swap(yo, "gy") if with_yo else None
        rxe = swap(xe, "gx", even_pairs(nx))
        rxo = swap(xo, "gx") if with_xo else None
        rye = swap(ye, "gy", even_pairs(ny))
        args = [current, previous, c2, toeplitz, select, contrib, accel]
        if fine is not None:
            args.append(fine)
        part, fine = vmem_call(
            functools.partial(update_kernel, step=step), [sds(tile), sds(tile)], args, [ypad],
            flops=cells * 60,
        )
        halos = given(rye, ryo, rxe, rxo)
        if step < steps - 1:
            nxt, *faces = vmem_call(
                functools.partial(correct_kernel, with_yo=with_yo, with_xo=with_xo),
                [sds(tile)] + face_shapes(),
                [part, c2] + halos,
                [stage],
            )
        else:
            nxt, coarse = vmem_call(
                functools.partial(last_kernel, with_yo=with_yo, with_xo=with_xo, step=step),
                [sds(tile), sds((cx // 2, cy // 2, nz // 2))],
                [part, c2, accel, fine] + halos,
                [pltpu.VMEM((cx * cy // 2, nz // 2), F32), stage],
            )
        previous, current = current, nxt
    bit = 1
    while bit < nshot:
        one = swap(coarse, "shot", xor(nshot, bit))
        if nshot % (4 * bit) == 0:
            two = swap(coarse, "shot", xor(nshot, 2 * bit))
            three = swap(coarse, "shot", xor(nshot, 3 * bit))
            coarse = (coarse + one) + (two + three)
            bit *= 4
        else:
            coarse = coarse + one
            bit *= 2
    previous, current = vmem_call(
        flush_kernel, [sds(tile), sds(tile)], [previous, current], [pltpu.SemaphoreType.DMA((2,))],
        hbm_out=(0, 1),
    )
    return (previous[None], current[None], coarse)


def solution(mesh):
    return jax.shard_map(
        local,
        mesh=mesh,
        in_specs=(
            P("shot", "gx", "gy", None),
            P("shot", "gx", "gy", None),
            P("shot", None, "gx", "gy", None),
            P("gx", "gy", None),
            P("shot", None, ("gx", "gy")),
            P("gx", "gy", None, None, None),
            P("gx", "gy", None),
            P("gx", "gy", None),
            P("gx", "gy"),
        ),
        out_specs=(P("shot", "gx", "gy", None), P("shot", "gx", "gy", None), P("gx", "gy", None)),
        check_vma=False,
    )
```

```python
import functools

import jax
import jax.numpy as jnp
from jax import lax
from jax.experimental import pallas as pl
from jax.experimental.pallas import tpu as pltpu
from jax.sharding import PartitionSpec as P


LAPLACE_COEFS = (-205.0 / 72.0, 8.0 / 5.0, -1.0 / 5.0, 8.0 / 315.0, -1.0 / 560.0)
REACH = 4
CHUNK = 8
VMEM_LIMIT = 16 << 20
F32 = jnp.float32
BF16 = jnp.bfloat16


def vmem_call(kernel, outs, args, scratch=(), flops=0, hbm_in=(), hbm_out=(), smem_in=()):
    in_specs = [
        pl.BlockSpec(memory_space=pltpu.HBM if i in hbm_in else pltpu.SMEM if i in smem_in else pltpu.VMEM)
        for i in range(len(args))
    ]
    args = [pltpu.with_memory_space_constraint(a, pltpu.HBM) if i in hbm_in else a for i, a in enumerate(args)]
    moved = sum(a.size * a.dtype.itemsize for a in args) + sum(o.size * o.dtype.itemsize for o in outs)
    return pl.pallas_call(
        kernel,
        out_shape=tuple(outs),
        in_specs=in_specs,
        out_specs=tuple(
            pl.BlockSpec(memory_space=pltpu.HBM if i in hbm_out else pltpu.VMEM) for i in range(len(outs))
        ),
        scratch_shapes=list(scratch),
        cost_estimate=pl.CostEstimate(flops=flops, bytes_accessed=moved, transcendentals=0),
        compiler_params=pltpu.CompilerParams(vmem_limit_bytes=VMEM_LIMIT),
    )(*args)


def sds(shape, dtype=F32):
    return jax.ShapeDtypeStruct(shape, dtype)


def even_pairs(n):
    pairs = []
    for i in range(0, n - 1, 2):
        pairs += [(i, i + 1), (i + 1, i)]
    return pairs


def odd_swap(x, axis):
    n, shots = lax.axis_size(axis), lax.axis_size("shot")
    if shots % 2:
        pairs = [(0, n - 1), (n - 1, 0)]
        for i in range(1, n - 1, 2):
            pairs += [(i, i + 1), (i + 1, i)]
        return lax.ppermute(x, axis, pairs)
    pairs = []
    for s in range(shots):
        for i in (0, n - 1):
            pairs.append((i * shots + s, i * shots + (s ^ 1)))
        for i in range(1, n - 1, 2):
            pairs += [(i * shots + s, (i + 1) * shots + s), ((i + 1) * shots + s, i * shots + s)]
    return lax.ppermute(x, (axis, "shot"), pairs)


def split2(v):
    hi = v.astype(BF16)
    return hi, (v - hi.astype(F32)).astype(BF16)


def dot(a, b):
    return jnp.dot(a, b, preferred_element_type=F32)


def put_y_face(cur, out, stage, high):
    cx, cy, _ = cur.shape
    start = cy - REACH if high else 0
    for h in range(stage.shape[0]):
        at = slice(h * 128, (h + 1) * 128)
        for x in range(cx):
            stage[h, REACH * x : REACH * (x + 1), :] = cur[x, start : start + REACH, at]
        out[0 : REACH * cx, at] = stage[h, :, :].astype(BF16)
        near = stage[h, pl.ds(REACH - 1 if high else 0, cx, REACH), :]
        out[REACH * cx : (REACH + 1) * cx, at] = split2(near)[1]


def put_x_face(cur, out, high):
    cx, cy, _ = cur.shape
    low = jnp.where(high, cx - REACH, 0)
    for r in range(REACH):
        out[r * cy : (r + 1) * cy, :] = cur[low + r, :, :].astype(BF16)
    out[REACH * cy : (REACH + 1) * cy, :] = split2(cur[jnp.where(high, cx - 1, 0), :, :])[1]


def put_faces(cur, gx_index, gy_index, ye, yo, xe, xo, stage):
    y_even = gy_index % 2 == 0
    x_even = gx_index % 2 == 0

    @pl.when(y_even)
    def _():
        put_y_face(cur, ye, stage, True)
        if yo is not None:
            put_y_face(cur, yo, stage, False)

    @pl.when(jnp.logical_not(y_even))
    def _():
        put_y_face(cur, ye, stage, False)
        if yo is not None:
            put_y_face(cur, yo, stage, True)

    put_x_face(cur, xe, x_even)
    if xo is not None:
        put_x_face(cur, xo, jnp.logical_not(x_even))


def add_y_halo(nxt, c2, recv, stage, high):
    cx, cy, nz = nxt.shape
    w = LAPLACE_COEFS
    near = pl.ds(0 if high else REACH - 1, cx, REACH)
    for h in range(stage.shape[0]):
        at = slice(h * 128, (h + 1) * 128)
        stage[h, :, :] = recv[0 : REACH * cx, at].astype(F32)
        stage[h, near, :] = stage[h, near, :] + recv[REACH * cx : (REACH + 1) * cx, at].astype(F32)
    row = lax.broadcasted_iota(jnp.int32, (8, nz), 0) % REACH
    coefs = {}
    for k in range(1, REACH + 1):
        shift = REACH - k
        keep = (row >= shift) if high else (row < k)
        coefs[k] = jnp.where(keep, w[k], 0.0)
    start = cy - REACH if high else 0
    for i in range(cx // 2):
        m = jnp.concatenate([stage[h, 8 * i : 8 * i + 8, :] for h in range(stage.shape[0])], axis=1)
        total = w[REACH] * m
        for k in range(1, REACH):
            shift = REACH - k
            total = total + coefs[k] * pltpu.roll(m, shift if high else 8 - shift, 0)
        for h in range(2):
            rows = slice(start, start + REACH)
            nxt[2 * i + h, rows, :] = (
                nxt[2 * i + h, rows, :] + c2[2 * i + h, rows, :] * total[REACH * h : REACH * h + REACH, :]
            )


def add_x_halo(nxt, c2, recv, stage, high):
    cx, cy, _ = nxt.shape
    w = LAPLACE_COEFS
    layers = [recv[r * cy : (r + 1) * cy, :].astype(F32) for r in range(REACH + 1)]
    near = 0 if high else REACH - 1
    layers[near] = layers[near] + layers[REACH]
    for r in range(REACH):
        x = cx - 1 - r if high else r
        total = None
        for k in range(r + 1, REACH + 1):
            term = w[k] * layers[(k - r - 1) if high else (REACH + r - k)]
            total = term if total is None else total + term
        nxt[x, :, :] = nxt[x, :, :] + c2[x, :, :] * total


def add_halos(nxt, c2, gx_index, gy_index, ye, yo, xe, xo, stage):
    for axis, index, even, odd, add in (("gy", gy_index, ye, yo, add_y_halo), ("gx", gx_index, xe, xo, add_x_halo)):
        is_even = index % 2 == 0
        inner = jnp.logical_and(index > 0, index < lax.axis_size(axis) - 1)

        @pl.when(is_even)
        def _(even=even, add=add):
            add(nxt, c2, even, stage, True)

        @pl.when(jnp.logical_not(is_even))
        def _(even=even, add=add):
            add(nxt, c2, even, stage, False)

        if odd is not None:

            @pl.when(jnp.logical_and(inner, is_even))
            def _(odd=odd, add=add):
                add(nxt, c2, odd, stage, False)

            @pl.when(jnp.logical_and(inner, jnp.logical_not(is_even)))
            def _(odd=odd, add=add):
                add(nxt, c2, odd, stage, True)


def put_band(out, size, span, centre):
    row = lax.broadcasted_iota(jnp.int32, (size, size), 0)
    column = lax.broadcasted_iota(jnp.int32, (size, size), 1)
    distance = jnp.abs(row - column)
    band = jnp.where(distance == 0, centre, 0.0)
    for k in range(1, REACH + 1):
        band = band + jnp.where(distance == k, LAPLACE_COEFS[k], 0.0)
    if span < size:
        band = jnp.where(lax.div(row, jnp.int32(span)) == lax.div(column, jnp.int32(span)), band, 0.0)
    hi, lo = split2(band)
    out[0:size, :] = hi
    out[size : 2 * size, :] = lo


def load_kernel(
    cur_in, col_in, rb_in, traces_in, counts, cur, toeplitz, blocks, select, owners, own, *refs,
    with_yo, with_xo, each, rblk,
):
    ye, yo, xe, xo, (col, rb, traces, stage, sems) = unpack(refs, with_yo, with_xo)
    gx_index, gy_index = lax.axis_index("gx"), lax.axis_index("gy")
    pairs = ((cur_in, cur), (col_in, col), (rb_in, rb), (traces_in, traces))
    copies = [pltpu.make_async_copy(src, dst, sems.at[i]) for i, (src, dst) in enumerate(pairs)]
    for copy in copies:
        copy.start()
    nz, rows, cy = toeplitz.shape[1], blocks.shape[1], cur.shape[1]
    put_band(toeplitz, nz, nz, 3.0 * LAPLACE_COEFS[0])
    put_band(blocks, rows, cy, 0.0)
    for copy in copies[1:]:
        copy.wait()
    wide = jnp.concatenate([col[...]] * 3, axis=1)
    rows = lax.broadcasted_iota(jnp.int32, select.shape, 0)
    select[...] = jnp.where(rows == wide, 1.0, 0.0).astype(BF16)
    slot_owners(rb, counts, owners, each, rblk)
    steps, per = traces.shape[1:]
    own[...] = jnp.zeros(own.shape, F32)
    own[0, 0:steps, 0:per] = traces[0].astype(F32)
    copies[0].wait()
    put_faces(cur, gx_index, gy_index, ye, yo, xe, xo, stage)


def slot_owners(rb, counts, owners, each, rblk):
    me = lax.axis_index("gx") * lax.axis_size("gy") + lax.axis_index("gy")
    slots, lanes = owners.shape
    eye = lax.broadcasted_iota(jnp.int32, (slots, slots), 0) == lax.broadcasted_iota(jnp.int32, (slots, slots), 1)
    block_of = jnp.sum(jnp.where(eye, jnp.broadcast_to(rb[...], (slots, slots)), 0), axis=1, keepdims=True)
    owner = lax.div(block_of, jnp.int32(each))
    group = block_of - owner * each
    lane = lax.broadcasted_iota(jnp.int32, (slots, lanes), 1)
    live = lax.broadcasted_iota(jnp.int32, (slots, lanes), 0) < counts[0, 0]
    used = jnp.logical_and(live, lax.div(lane, jnp.int32(rblk)) == group)
    owners[...] = jnp.where(used, jnp.bitwise_xor(owner, me), -1)


def flush_kernel(a_in, b_in, a_out, b_out, sems):
    copies = [
        pltpu.make_async_copy(src, dst, sems.at[i]) for i, (src, dst) in enumerate(((a_in, a_out), (b_in, b_out)))
    ]
    for copy in copies:
        copy.start()
    for copy in copies:
        copy.wait()


def update(cur, prev, c2, toeplitz, blocks, out, source=None, fine=None):
    cx, cy, nz = cur.shape
    w = LAPLACE_COEFS
    chunk = CHUNK
    rows = chunk * cy
    t_hi = toeplitz[0:nz, :]
    t_lo = toeplitz[nz : 2 * nz, :]
    b_hi = blocks[0:rows, :]
    b_lo = blocks[rows : 2 * rows, :]
    for m in range(cx // chunk):
        v = cur[m * chunk : (m + 1) * chunk, :, :].reshape(rows, nz)
        hi, lo = split2(v)
        lz = dot(hi, t_hi) + dot(lo, t_hi) + dot(hi, t_lo)
        lz = lz + dot(b_hi, hi) + dot(b_hi, lo) + dot(b_lo, hi)
        if source is not None:
            select, contrib = source
            src = dot(select[m * rows : (m + 1) * rows, :], contrib)
        for j in range(chunk):
            x = m * chunk + j
            total = lz[j * cy : (j + 1) * cy, :]
            for k in range(1, REACH + 1):
                near = [cur[i, :, :] for i in (x - k, x + k) if 0 <= i < cx]
                if near:
                    total = total + w[k] * (near[0] if len(near) == 1 else near[0] + near[1])
            if prev is None:
                out[x, :, :] = total
                continue
            here = cur[x, :, :]
            value = (2.0 * here - prev[x, :, :]) + c2[x, :, :] * total
            if source is not None:
                value = value + src[j * cy : (j + 1) * cy, :]
            out[x, :, :] = value
            if fine is not None:
                fine_in, accel, fine_out = fine
                term = accel[x, :, :].astype(F32) * here
                fine_out[x, :, :] = term if fine_in is None else fine_in[x, :, :] + term


def first_update_kernel(cur, toeplitz, blocks, prev_in, c2_in, weights_in, out, prev, c2, weights, sems):
    copies = [
        pltpu.make_async_copy(src, dst, sems.at[i])
        for i, (src, dst) in enumerate(((prev_in, prev), (c2_in, c2), (weights_in, weights)))
    ]
    for copy in copies:
        copy.start()
    update(cur, None, None, toeplitz, blocks, out)
    copies[0].wait()
    copies[1].wait()
    for x in range(cur.shape[0]):
        out[x, :, :] = (2.0 * cur[x, :, :] - prev[x, :, :]) + c2[x, :, :] * out[x, :, :]
    copies[2].wait()


def update_kernel(cur, prev, c2, toeplitz, blocks, select, contrib, accel, *rest, step):
    if step == 1:
        out, fine_out = rest
        fine_in = None
    else:
        fine_in, out, fine_out = rest
    update(
        cur, prev, c2, toeplitz, blocks, out,
        source=(select, contrib[step]), fine=(fine_in, accel.at[step - 1], fine_out),
    )


def contributions(owners, weights, blocks, patterns, contrib, wide):
    slots, rblk, nz = weights.shape
    steps = contrib.shape[0]
    lanes = 128
    picked = [jnp.zeros((slots, lanes), F32) for _ in range(steps)]
    for tile, pattern in zip(blocks, patterns):
        mask = owners[...] == pattern
        for t in range(steps):
            picked[t] = jnp.where(mask, tile[t : t + 1, :], picked[t])
    spread = (
        lax.rem(lax.broadcasted_iota(jnp.int32, (lanes, lanes), 0), jnp.int32(rblk))
        == lax.rem(lax.broadcasted_iota(jnp.int32, (lanes, lanes), 1), jnp.int32(rblk))
    )
    spread = jnp.where(spread, 1.0, 0.0).astype(BF16)
    tiled = [dot(p.astype(BF16), spread) for p in picked]
    together = lanes // rblk
    diagonal = lax.broadcasted_iota(jnp.int32, (together, lanes), 0) == lax.div(
        lax.broadcasted_iota(jnp.int32, (together, lanes), 1), jnp.int32(rblk)
    )
    for q in range(slots // together):
        rows = slice(q * together, (q + 1) * together)
        left = jnp.concatenate([jnp.where(diagonal, v[rows, :], 0.0) for v in tiled], axis=0).astype(BF16)
        right = weights[q * together : (q + 1) * together, :, :].reshape(together * rblk, nz)
        got = dot(left, right)
        for t in range(steps):
            wide[t, rows, :] = got[t * together : (t + 1) * together, :]
    for t in range(steps):
        hi, mid = split2(wide[t, :, :])
        rest = wide[t, :, :] - hi.astype(F32) - mid.astype(F32)
        contrib[t, 0:slots, :] = hi
        contrib[t, slots : 2 * slots, :] = mid
        contrib[t, 2 * slots : 3 * slots, :] = rest.astype(BF16)


def unpack(refs, with_yo, with_xo):
    refs = list(refs)
    ye = refs.pop(0)
    yo = refs.pop(0) if with_yo else None
    xe = refs.pop(0)
    xo = refs.pop(0) if with_xo else None
    return ye, yo, xe, xo, refs


def first_correct_kernel(owners, weights, select, part, c2, *refs, with_yo, with_xo, patterns):
    gx_index, gy_index = lax.axis_index("gx"), lax.axis_index("gy")
    ye, yo, xe, xo, refs = unpack(refs, with_yo, with_xo)
    pairs, refs = refs[0], refs[1:]
    nxt, contrib, refs = refs[0], refs[1], refs[2:]
    oye, oyo, oxe, oxo, refs = unpack(refs, with_yo, with_xo)
    wide, stage = refs
    lanes = 128
    tiles = []
    rows = pairs.shape[0]
    y_last, x_last = ye.shape[0] - rows, xe.shape[0] - 2 * rows
    for block in (pairs[...], ye[y_last : y_last + rows, :], xe[x_last : x_last + 2 * rows, :]):
        block = block.astype(F32)
        for i in range(0, block.shape[0], 8):
            tiles += [block[i : i + 8, 0:lanes], block[i : i + 8, lanes : 2 * lanes]]
    contributions(owners, weights, tiles, patterns, contrib, wide)
    cx, cy, nz = nxt.shape
    chunk = 8
    rows = chunk * cy
    for m in range(cx // chunk):
        src = dot(select[m * rows : (m + 1) * rows, :], contrib[0])
        at = slice(m * chunk, (m + 1) * chunk)
        nxt[at, :, :] = part[at, :, :] + src.reshape(chunk, cy, nz)
    add_halos(nxt, c2, gx_index, gy_index, ye, yo, xe, xo, stage)
    put_faces(nxt, gx_index, gy_index, oye, oyo, oxe, oxo, stage)


def correct_kernel(part, c2, *refs, with_yo, with_xo):
    gx_index, gy_index = lax.axis_index("gx"), lax.axis_index("gy")
    ye, yo, xe, xo, refs = unpack(refs, with_yo, with_xo)
    nxt, refs = refs[0], refs[1:]
    oye, oyo, oxe, oxo, (stage,) = unpack(refs, with_yo, with_xo)
    nxt[...] = part[...]
    add_halos(nxt, c2, gx_index, gy_index, ye, yo, xe, xo, stage)
    put_faces(nxt, gx_index, gy_index, oye, oyo, oxe, oxo, stage)


def last_kernel(part, c2, accel, fine, *refs, with_yo, with_xo, step):
    gx_index, gy_index = lax.axis_index("gx"), lax.axis_index("gy")
    ye, yo, xe, xo, refs = unpack(refs, with_yo, with_xo)
    nxt, coarse, middle, stage = refs
    cx, cy, nz = nxt.shape
    nxt[...] = part[...]
    add_halos(nxt, c2, gx_index, gy_index, ye, yo, xe, xo, stage)
    pairs = lax.div(lax.broadcasted_iota(jnp.int32, (nz, nz // 2), 0), jnp.int32(2)) == lax.broadcasted_iota(
        jnp.int32, (nz, nz // 2), 1
    )
    pairs = jnp.where(pairs, 0.125, 0.0).astype(BF16)
    chunk = 8
    for m in range(cx // (2 * chunk)):
        summed = []
        for j in range(chunk):
            x = 2 * (m * chunk + j)
            a = fine[x, :, :] + accel[step, x, :, :].astype(F32) * nxt[x, :, :]
            b = fine[x + 1, :, :] + accel[step, x + 1, :, :].astype(F32) * nxt[x + 1, :, :]
            summed.append(a + b)
        hi, lo = split2(jnp.concatenate(summed, axis=0))
        got = dot(hi, pairs) + dot(lo, pairs)
        middle[m * chunk * cy : (m + 1) * chunk * cy, :] = got
    half = cx * cy // 4
    both = middle[pl.ds(0, half, 2), :] + middle[pl.ds(1, half, 2), :]
    coarse[...] = both.reshape(coarse.shape)


def local(adj_prev, adj_cur, fwd_accel, courant2, traces, weights, rblock, column, counts):
    accel = fwd_accel[0]
    cx, cy, nz = courant2.shape
    steps = accel.shape[0]
    slots, rblk = weights.shape[2:4]
    per = traces.shape[2]
    nx, ny, nshot = lax.axis_size("gx"), lax.axis_size("gy"), lax.axis_size("shot")
    with_yo, with_xo = ny > 2, nx > 2
    y_msg, x_msg = ((REACH + 1) * cx, nz), ((REACH + 1) * cy, nz)
    tile = (cx, cy, nz)
    cells = cx * cy * nz
    lanes = 128

    def swap(x, axis, pairs=None):
        return odd_swap(x, axis) if pairs is None else lax.ppermute(x, axis, pairs)

    def xor(size, bit):
        return [(i, i ^ bit) for i in range(size)]

    def given(ye, yo, xe, xo):
        return [a for a in (ye, yo, xe, xo) if a is not None]

    def face_shapes():
        y, x = sds(y_msg, BF16), sds(x_msg, BF16)
        return given(y, y if with_yo else None, x, x if with_xo else None)

    def taken(faces):
        faces = list(faces)
        ye = faces.pop(0)
        yo = faces.pop(0) if with_yo else None
        xe = faces.pop(0)
        xo = faces.pop(0) if with_xo else None
        return ye, yo, xe, xo

    blocks, others, patterns = traces, [], [0]
    for axis, size, stride in (("gy", ny, 1), ("gx", nx, ny)):
        bit = 2
        while bit < size:
            got = swap(blocks, axis, xor(size, bit))
            others.append(got)
            patterns = patterns + [p ^ (bit * stride) for p in patterns]
            bit *= 2
            if bit < size or (axis == "gy" and nx > 2):
                blocks = jnp.concatenate([blocks, got], axis=0)
    if not others:
        others, patterns = [jnp.zeros_like(traces)], [0, -2]
    stage = pltpu.VMEM((nz // lanes, REACH * cx, lanes), F32)
    cur, toeplitz, bands, select, owners, own, *faces = vmem_call(
        functools.partial(load_kernel, with_yo=with_yo, with_xo=with_xo, each=per // rblk, rblk=rblk),
        [
            sds(tile), sds((2 * nz, nz), BF16), sds((2 * CHUNK * cy, CHUNK * cy), BF16),
            sds((cx * cy, 3 * slots), BF16), sds((slots, lanes), jnp.int32), sds((1, 8, lanes)),
        ] + face_shapes(),
        [adj_cur[0], column[0], rblock[0], traces, counts],
        [
            pltpu.VMEM((1, slots), jnp.int32), pltpu.VMEM((1, slots), jnp.int32), pltpu.VMEM((1, steps, per), BF16),
            stage, pltpu.SemaphoreType.DMA((4,)),
        ],
        hbm_in=(0, 1, 2, 3), smem_in=(4,),
    )
    ye, yo, xe, xo = taken(faces)
    others = [jnp.pad(a.astype(F32), ((0, 0), (0, 8 - steps), (0, lanes - per))) for a in others]
    tiles = jnp.concatenate([own] + others, axis=0)
    pairs = jnp.concatenate([tiles[0::2], tiles[1::2]], axis=2).astype(BF16).reshape(-1, nz)
    rye = swap(jnp.concatenate([ye, pairs], axis=0), "gy", even_pairs(ny))
    ryo = swap(yo, "gy") if with_yo else None
    rxo = swap(xo, "gx") if with_xo else None
    rxe = swap(jnp.concatenate([xe, pairs, rye[y_msg[0] :]], axis=0), "gx", even_pairs(nx))
    for stride in (1, ny):
        patterns = patterns + [p ^ stride if p >= 0 else p for p in patterns]

    part, _, c2, wts = vmem_call(
        first_update_kernel,
        [sds(tile), sds(tile), sds(tile), sds((slots, rblk, nz), BF16)],
        [cur, toeplitz, bands, adj_prev[0], courant2, weights[0, 0]],
        [pltpu.SemaphoreType.DMA((3,))],
        hbm_in=(3, 4, 5), flops=cells * 60,
    )

    nxt, contrib, *faces = vmem_call(
        functools.partial(
            first_correct_kernel, with_yo=with_yo, with_xo=with_xo, patterns=tuple(patterns)
        ),
        [sds(tile), sds((steps, 3 * slots, nz), BF16)] + face_shapes(),
        [owners, wts, select, part, c2] + given(rye, ryo, rxe, rxo) + [pairs],
        [pltpu.VMEM((steps, slots, nz), F32), stage],
    )
    previous, current = cur, nxt
    fine = None
    for step in range(1, steps):
        ye, yo, xe, xo = taken(faces)
        ryo = swap(yo, "gy") if with_yo else None
        rxe = swap(xe, "gx", even_pairs(nx))
        rxo = swap(xo, "gx") if with_xo else None
        rye = swap(ye, "gy", even_pairs(ny))
        args = [current, previous, c2, toeplitz, bands, select, contrib, accel]
        if fine is not None:
            args.append(fine)
        part, fine = vmem_call(
            functools.partial(update_kernel, step=step), [sds(tile), sds(tile)], args,
            flops=cells * 60,
        )
        halos = given(rye, ryo, rxe, rxo)
        if step < steps - 1:
            nxt, *faces = vmem_call(
                functools.partial(correct_kernel, with_yo=with_yo, with_xo=with_xo),
                [sds(tile)] + face_shapes(),
                [part, c2] + halos,
                [stage],
            )
        else:
            nxt, coarse = vmem_call(
                functools.partial(last_kernel, with_yo=with_yo, with_xo=with_xo, step=step),
                [sds(tile), sds((cx // 2, cy // 2, nz // 2))],
                [part, c2, accel, fine] + halos,
                [pltpu.VMEM((cx * cy // 2, nz // 2), F32), stage],
            )
        previous, current = current, nxt
    bit = 1
    while bit < nshot:
        one = swap(coarse, "shot", xor(nshot, bit))
        if nshot % (4 * bit) == 0:
            two = swap(coarse, "shot", xor(nshot, 2 * bit))
            three = swap(coarse, "shot", xor(nshot, 3 * bit))
            coarse = (coarse + one) + (two + three)
            bit *= 4
        else:
            coarse = coarse + one
            bit *= 2
    previous, current = vmem_call(
        flush_kernel, [sds(tile), sds(tile)], [previous, current], [pltpu.SemaphoreType.DMA((2,))],
        hbm_out=(0, 1),
    )
    return (previous[None], current[None], coarse)


def solution(mesh):
    return jax.shard_map(
        local,
        mesh=mesh,
        in_specs=(
            P("shot", "gx", "gy", None),
            P("shot", "gx", "gy", None),
            P("shot", None, "gx", "gy", None),
            P("gx", "gy", None),
            P("shot", None, ("gx", "gy")),
            P("gx", "gy", None, None, None),
            P("gx", "gy", None),
            P("gx", "gy", None),
            P("gx", "gy"),
        ),
        out_specs=(P("shot", "gx", "gy", None), P("shot", "gx", "gy", None), P("gx", "gy", None)),
        check_vma=False,
    )
```

```python
import functools

import jax
import jax.numpy as jnp
from jax import lax
from jax.experimental import pallas as pl
from jax.experimental.pallas import tpu as pltpu
from jax.sharding import PartitionSpec as P


LAPLACE_COEFS = (-205.0 / 72.0, 8.0 / 5.0, -1.0 / 5.0, 8.0 / 315.0, -1.0 / 560.0)
REACH = 4
CHUNK = 8
VMEM_LIMIT = 16 << 20
F32 = jnp.float32
BF16 = jnp.bfloat16


def vmem_call(kernel, outs, args, scratch=(), flops=0, hbm_in=(), hbm_out=(), smem_in=()):
    in_specs = [
        pl.BlockSpec(memory_space=pltpu.HBM if i in hbm_in else pltpu.SMEM if i in smem_in else pltpu.VMEM)
        for i in range(len(args))
    ]
    args = [pltpu.with_memory_space_constraint(a, pltpu.HBM) if i in hbm_in else a for i, a in enumerate(args)]
    moved = sum(a.size * a.dtype.itemsize for a in args) + sum(o.size * o.dtype.itemsize for o in outs)
    return pl.pallas_call(
        kernel,
        out_shape=tuple(outs),
        in_specs=in_specs,
        out_specs=tuple(
            pl.BlockSpec(memory_space=pltpu.HBM if i in hbm_out else pltpu.VMEM) for i in range(len(outs))
        ),
        scratch_shapes=list(scratch),
        cost_estimate=pl.CostEstimate(flops=flops, bytes_accessed=moved, transcendentals=0),
        compiler_params=pltpu.CompilerParams(vmem_limit_bytes=VMEM_LIMIT),
    )(*args)


def sds(shape, dtype=F32):
    return jax.ShapeDtypeStruct(shape, dtype)


def even_pairs(n):
    pairs = []
    for i in range(0, n - 1, 2):
        pairs += [(i, i + 1), (i + 1, i)]
    return pairs


def odd_swap(x, axis):
    n, shots = lax.axis_size(axis), lax.axis_size("shot")
    if shots % 2:
        pairs = [(0, n - 1), (n - 1, 0)]
        for i in range(1, n - 1, 2):
            pairs += [(i, i + 1), (i + 1, i)]
        return lax.ppermute(x, axis, pairs)
    pairs = []
    for s in range(shots):
        for i in (0, n - 1):
            pairs.append((i * shots + s, i * shots + (s ^ 1)))
        for i in range(1, n - 1, 2):
            pairs += [(i * shots + s, (i + 1) * shots + s), ((i + 1) * shots + s, i * shots + s)]
    return lax.ppermute(x, (axis, "shot"), pairs)


def split2(v):
    hi = v.astype(BF16)
    return hi, (v - hi.astype(F32)).astype(BF16)


def dot(a, b):
    return jnp.dot(a, b, preferred_element_type=F32)


def put_y_face(cur, out, stage, high):
    cx, cy, _ = cur.shape
    start = cy - REACH if high else 0
    for h in range(stage.shape[0]):
        at = slice(h * 128, (h + 1) * 128)
        for x in range(cx):
            stage[h, REACH * x : REACH * (x + 1), :] = cur[x, start : start + REACH, at]
        out[0 : REACH * cx, at] = stage[h, :, :].astype(BF16)
        near = stage[h, pl.ds(REACH - 1 if high else 0, cx, REACH), :]
        out[REACH * cx : (REACH + 1) * cx, at] = split2(near)[1]


def put_x_face(cur, out, high):
    cx, cy, _ = cur.shape
    low = jnp.where(high, cx - REACH, 0)
    for r in range(REACH):
        out[r * cy : (r + 1) * cy, :] = cur[low + r, :, :].astype(BF16)
    out[REACH * cy : (REACH + 1) * cy, :] = split2(cur[jnp.where(high, cx - 1, 0), :, :])[1]


def put_faces(cur, gx_index, gy_index, ye, yo, xe, xo, stage):
    y_even = gy_index % 2 == 0
    x_even = gx_index % 2 == 0

    @pl.when(y_even)
    def _():
        put_y_face(cur, ye, stage, True)
        if yo is not None:
            put_y_face(cur, yo, stage, False)

    @pl.when(jnp.logical_not(y_even))
    def _():
        put_y_face(cur, ye, stage, False)
        if yo is not None:
            put_y_face(cur, yo, stage, True)

    put_x_face(cur, xe, x_even)
    if xo is not None:
        put_x_face(cur, xo, jnp.logical_not(x_even))


def add_y_halo(nxt, c2, recv, stage, high):
    cx, cy, nz = nxt.shape
    w = LAPLACE_COEFS
    near = pl.ds(0 if high else REACH - 1, cx, REACH)
    for h in range(stage.shape[0]):
        at = slice(h * 128, (h + 1) * 128)
        stage[h, :, :] = recv[0 : REACH * cx, at].astype(F32)
        stage[h, near, :] = stage[h, near, :] + recv[REACH * cx : (REACH + 1) * cx, at].astype(F32)
    row = lax.broadcasted_iota(jnp.int32, (8, nz), 0) % REACH
    coefs = {}
    for k in range(1, REACH + 1):
        shift = REACH - k
        keep = (row >= shift) if high else (row < k)
        coefs[k] = jnp.where(keep, w[k], 0.0)
    start = cy - REACH if high else 0
    for i in range(cx // 2):
        m = jnp.concatenate([stage[h, 8 * i : 8 * i + 8, :] for h in range(stage.shape[0])], axis=1)
        total = w[REACH] * m
        for k in range(1, REACH):
            shift = REACH - k
            total = total + coefs[k] * pltpu.roll(m, shift if high else 8 - shift, 0)
        for h in range(2):
            rows = slice(start, start + REACH)
            nxt[2 * i + h, rows, :] = (
                nxt[2 * i + h, rows, :] + c2[2 * i + h, rows, :] * total[REACH * h : REACH * h + REACH, :]
            )


def add_x_halo(nxt, c2, recv, stage, high):
    cx, cy, _ = nxt.shape
    w = LAPLACE_COEFS
    layers = [recv[r * cy : (r + 1) * cy, :].astype(F32) for r in range(REACH + 1)]
    near = 0 if high else REACH - 1
    layers[near] = layers[near] + layers[REACH]
    for r in range(REACH):
        x = cx - 1 - r if high else r
        total = None
        for k in range(r + 1, REACH + 1):
            term = w[k] * layers[(k - r - 1) if high else (REACH + r - k)]
            total = term if total is None else total + term
        nxt[x, :, :] = nxt[x, :, :] + c2[x, :, :] * total


def add_halos(nxt, c2, name, even, odd, stage):
    index, add = lax.axis_index(name), add_y_halo if name == "gy" else add_x_halo
    is_even = index % 2 == 0
    inner = jnp.logical_and(index > 0, index < lax.axis_size(name) - 1)

    @pl.when(is_even)
    def _():
        add(nxt, c2, even, stage, True)

    @pl.when(jnp.logical_not(is_even))
    def _():
        add(nxt, c2, even, stage, False)

    if odd is not None:

        @pl.when(jnp.logical_and(inner, is_even))
        def _():
            add(nxt, c2, odd, stage, False)

        @pl.when(jnp.logical_and(inner, jnp.logical_not(is_even)))
        def _():
            add(nxt, c2, odd, stage, True)


def put_band(out, size, span, centre):
    row = lax.broadcasted_iota(jnp.int32, (size, size), 0)
    column = lax.broadcasted_iota(jnp.int32, (size, size), 1)
    distance = jnp.abs(row - column)
    band = jnp.where(distance == 0, centre, 0.0)
    for k in range(1, REACH + 1):
        band = band + jnp.where(distance == k, LAPLACE_COEFS[k], 0.0)
    if span < size:
        band = jnp.where(lax.div(row, jnp.int32(span)) == lax.div(column, jnp.int32(span)), band, 0.0)
    hi, lo = split2(band)
    out[0:size, :] = hi
    out[size : 2 * size, :] = lo


def load_kernel(
    cur_in, col_in, rb_in, traces_in, counts, cur, toeplitz, blocks, select, owners, own, *refs,
    with_yo, with_xo, each, rblk,
):
    ye, yo, xe, xo, (col, rb, traces, stage, sems) = unpack(refs, with_yo, with_xo)
    gx_index, gy_index = lax.axis_index("gx"), lax.axis_index("gy")
    pairs = ((cur_in, cur), (col_in, col), (rb_in, rb), (traces_in, traces))
    copies = [pltpu.make_async_copy(src, dst, sems.at[i]) for i, (src, dst) in enumerate(pairs)]
    for copy in copies:
        copy.start()
    nz, rows, cy = toeplitz.shape[1], blocks.shape[1], cur.shape[1]
    put_band(toeplitz, nz, nz, 3.0 * LAPLACE_COEFS[0])
    put_band(blocks, rows, cy, 0.0)
    for copy in copies[1:]:
        copy.wait()
    wide = jnp.concatenate([col[...]] * 3, axis=1)
    rows = lax.broadcasted_iota(jnp.int32, select.shape, 0)
    select[...] = jnp.where(rows == wide, 1.0, 0.0).astype(BF16)
    slot_owners(rb, counts, owners, each, rblk)
    steps, per = traces.shape[1:]
    own[...] = jnp.zeros(own.shape, F32)
    own[0, 0:steps, 0:per] = traces[0].astype(F32)
    copies[0].wait()
    put_faces(cur, gx_index, gy_index, ye, yo, xe, xo, stage)


def slot_owners(rb, counts, owners, each, rblk):
    me = lax.axis_index("gx") * lax.axis_size("gy") + lax.axis_index("gy")
    slots, lanes = owners.shape
    eye = lax.broadcasted_iota(jnp.int32, (slots, slots), 0) == lax.broadcasted_iota(jnp.int32, (slots, slots), 1)
    block_of = jnp.sum(jnp.where(eye, jnp.broadcast_to(rb[...], (slots, slots)), 0), axis=1, keepdims=True)
    owner = lax.div(block_of, jnp.int32(each))
    group = block_of - owner * each
    lane = lax.broadcasted_iota(jnp.int32, (slots, lanes), 1)
    live = lax.broadcasted_iota(jnp.int32, (slots, lanes), 0) < counts[0, 0]
    used = jnp.logical_and(live, lax.div(lane, jnp.int32(rblk)) == group)
    owners[...] = jnp.where(used, jnp.bitwise_xor(owner, me), -1)


def flush_kernel(a_in, b_in, a_out, b_out, sems):
    copies = [
        pltpu.make_async_copy(src, dst, sems.at[i]) for i, (src, dst) in enumerate(((a_in, a_out), (b_in, b_out)))
    ]
    for copy in copies:
        copy.start()
    for copy in copies:
        copy.wait()


def update(cur, prev, c2, toeplitz, blocks, out, source=None, fine=None):
    cx, cy, nz = cur.shape
    w = LAPLACE_COEFS
    chunk = CHUNK
    rows = chunk * cy
    t_hi = toeplitz[0:nz, :]
    t_lo = toeplitz[nz : 2 * nz, :]
    b_hi = blocks[0:rows, :]
    b_lo = blocks[rows : 2 * rows, :]
    for m in range(cx // chunk):
        v = cur[m * chunk : (m + 1) * chunk, :, :].reshape(rows, nz)
        hi, lo = split2(v)
        lz = dot(hi, t_hi) + dot(lo, t_hi) + dot(hi, t_lo)
        lz = lz + dot(b_hi, hi) + dot(b_hi, lo) + dot(b_lo, hi)
        if source is not None:
            select, contrib = source
            src = dot(select[m * rows : (m + 1) * rows, :], contrib)
        for j in range(chunk):
            x = m * chunk + j
            total = lz[j * cy : (j + 1) * cy, :]
            for k in range(1, REACH + 1):
                near = [cur[i, :, :] for i in (x - k, x + k) if 0 <= i < cx]
                if near:
                    total = total + w[k] * (near[0] if len(near) == 1 else near[0] + near[1])
            if prev is None:
                out[x, :, :] = total
                continue
            here = cur[x, :, :]
            value = (2.0 * here - prev[x, :, :]) + c2[x, :, :] * total
            if source is not None:
                value = value + src[j * cy : (j + 1) * cy, :]
            out[x, :, :] = value
            if fine is not None:
                fine_in, accel, fine_out = fine
                term = accel[x, :, :].astype(F32) * here
                fine_out[x, :, :] = term if fine_in is None else fine_in[x, :, :] + term


def first_update_kernel(cur, toeplitz, blocks, prev_in, c2_in, weights_in, out, prev, c2, weights, sems):
    copies = [
        pltpu.make_async_copy(src, dst, sems.at[i])
        for i, (src, dst) in enumerate(((prev_in, prev), (c2_in, c2), (weights_in, weights)))
    ]
    for copy in copies:
        copy.start()
    update(cur, None, None, toeplitz, blocks, out)
    copies[0].wait()
    copies[1].wait()
    for x in range(cur.shape[0]):
        out[x, :, :] = (2.0 * cur[x, :, :] - prev[x, :, :]) + c2[x, :, :] * out[x, :, :]
    copies[2].wait()


def update_kernel(cur, prev, c2, toeplitz, blocks, select, contrib, accel, *rest, step):
    if step == 1:
        out, fine_out = rest
        fine_in = None
    else:
        fine_in, out, fine_out = rest
    update(
        cur, prev, c2, toeplitz, blocks, out,
        source=(select, contrib[step]), fine=(fine_in, accel.at[step - 1], fine_out),
    )


def contributions(owners, weights, blocks, patterns, contrib, wide):
    slots, rblk, nz = weights.shape
    steps = contrib.shape[0]
    lanes = 128
    picked = [jnp.zeros((slots, lanes), F32) for _ in range(steps)]
    for tile, pattern in zip(blocks, patterns):
        mask = owners[...] == pattern
        for t in range(steps):
            picked[t] = jnp.where(mask, tile[t : t + 1, :], picked[t])
    spread = (
        lax.rem(lax.broadcasted_iota(jnp.int32, (lanes, lanes), 0), jnp.int32(rblk))
        == lax.rem(lax.broadcasted_iota(jnp.int32, (lanes, lanes), 1), jnp.int32(rblk))
    )
    spread = jnp.where(spread, 1.0, 0.0).astype(BF16)
    tiled = [dot(p.astype(BF16), spread) for p in picked]
    together = lanes // rblk
    diagonal = lax.broadcasted_iota(jnp.int32, (together, lanes), 0) == lax.div(
        lax.broadcasted_iota(jnp.int32, (together, lanes), 1), jnp.int32(rblk)
    )
    for q in range(slots // together):
        rows = slice(q * together, (q + 1) * together)
        left = jnp.concatenate([jnp.where(diagonal, v[rows, :], 0.0) for v in tiled], axis=0).astype(BF16)
        right = weights[q * together : (q + 1) * together, :, :].reshape(together * rblk, nz)
        got = dot(left, right)
        for t in range(steps):
            wide[t, rows, :] = got[t * together : (t + 1) * together, :]
    for t in range(steps):
        hi, mid = split2(wide[t, :, :])
        rest = wide[t, :, :] - hi.astype(F32) - mid.astype(F32)
        contrib[t, 0:slots, :] = hi
        contrib[t, slots : 2 * slots, :] = mid
        contrib[t, 2 * slots : 3 * slots, :] = rest.astype(BF16)


def unpack(refs, with_yo, with_xo):
    refs = list(refs)
    ye = refs.pop(0)
    yo = refs.pop(0) if with_yo else None
    xe = refs.pop(0)
    xo = refs.pop(0) if with_xo else None
    return ye, yo, xe, xo, refs


def first_correct_kernel(owners, weights, select, part, c2, *refs, with_yo, with_xo, patterns):
    gx_index, gy_index = lax.axis_index("gx"), lax.axis_index("gy")
    ye, _, xe, xo, refs = unpack(refs, with_yo, with_xo)
    pairs, refs = refs[0], refs[1:]
    nxt, contrib, refs = refs[0], refs[1], refs[2:]
    oye, oyo, oxe, oxo, refs = unpack(refs, with_yo, with_xo)
    wide, stage = refs
    lanes = 128
    tiles = []
    rows = pairs.shape[0]
    y_last, x_last = ye.shape[0] - rows, xe.shape[0] - 2 * rows
    for block in (pairs[...], ye[y_last : y_last + rows, :], xe[x_last : x_last + 2 * rows, :]):
        block = block.astype(F32)
        for i in range(0, block.shape[0], 8):
            tiles += [block[i : i + 8, 0:lanes], block[i : i + 8, lanes : 2 * lanes]]
    contributions(owners, weights, tiles, patterns, contrib, wide)
    cx, cy, nz = nxt.shape
    chunk = 8
    rows = chunk * cy
    for m in range(cx // chunk):
        src = dot(select[m * rows : (m + 1) * rows, :], contrib[0])
        at = slice(m * chunk, (m + 1) * chunk)
        nxt[at, :, :] = part[at, :, :] + src.reshape(chunk, cy, nz)
    add_halos(nxt, c2, "gx", xe, xo, stage)
    put_faces(nxt, gx_index, gy_index, oye, oyo, oxe, oxo, stage)


def correct_y_kernel(part, c2, *refs):
    out, stage = refs[-2:]
    out[...] = part[...]
    add_halos(out, c2, "gy", refs[0], refs[1] if len(refs) == 4 else None, stage)


def correct_kernel(part, c2, *refs, with_yo, with_xo):
    gx_index, gy_index = lax.axis_index("gx"), lax.axis_index("gy")
    xe, xo = refs[0], refs[1] if with_xo else None
    refs = refs[1 + with_xo :]
    nxt, refs = refs[0], refs[1:]
    oye, oyo, oxe, oxo, (stage,) = unpack(refs, with_yo, with_xo)
    nxt[...] = part[...]
    add_halos(nxt, c2, "gx", xe, xo, stage)
    put_faces(nxt, gx_index, gy_index, oye, oyo, oxe, oxo, stage)


def last_kernel(part, c2, accel, fine, *refs, with_xo, step):
    xe, xo = refs[0], refs[1] if with_xo else None
    nxt, coarse, middle, stage = refs[1 + with_xo :]
    cx, cy, nz = nxt.shape
    nxt[...] = part[...]
    add_halos(nxt, c2, "gx", xe, xo, stage)
    pairs = lax.div(lax.broadcasted_iota(jnp.int32, (nz, nz // 2), 0), jnp.int32(2)) == lax.broadcasted_iota(
        jnp.int32, (nz, nz // 2), 1
    )
    pairs = jnp.where(pairs, 0.125, 0.0).astype(BF16)
    chunk = 8
    for m in range(cx // (2 * chunk)):
        summed = []
        for j in range(chunk):
            x = 2 * (m * chunk + j)
            a = fine[x, :, :] + accel[step, x, :, :].astype(F32) * nxt[x, :, :]
            b = fine[x + 1, :, :] + accel[step, x + 1, :, :].astype(F32) * nxt[x + 1, :, :]
            summed.append(a + b)
        hi, lo = split2(jnp.concatenate(summed, axis=0))
        got = dot(hi, pairs) + dot(lo, pairs)
        middle[m * chunk * cy : (m + 1) * chunk * cy, :] = got
    half = cx * cy // 4
    both = middle[pl.ds(0, half, 2), :] + middle[pl.ds(1, half, 2), :]
    coarse[...] = both.reshape(coarse.shape)


def local(adj_prev, adj_cur, fwd_accel, courant2, traces, weights, rblock, column, counts):
    accel = fwd_accel[0]
    cx, cy, nz = courant2.shape
    steps = accel.shape[0]
    slots, rblk = weights.shape[2:4]
    per = traces.shape[2]
    nx, ny, nshot = lax.axis_size("gx"), lax.axis_size("gy"), lax.axis_size("shot")
    with_yo, with_xo = ny > 2, nx > 2
    y_msg, x_msg = ((REACH + 1) * cx, nz), ((REACH + 1) * cy, nz)
    tile = (cx, cy, nz)
    cells = cx * cy * nz
    lanes = 128

    def swap(x, axis, pairs=None):
        return odd_swap(x, axis) if pairs is None else lax.ppermute(x, axis, pairs)

    def xor(size, bit):
        return [(i, i ^ bit) for i in range(size)]

    def given(ye, yo, xe, xo):
        return [a for a in (ye, yo, xe, xo) if a is not None]

    def face_shapes():
        y, x = sds(y_msg, BF16), sds(x_msg, BF16)
        return given(y, y if with_yo else None, x, x if with_xo else None)

    def taken(faces):
        faces = list(faces)
        ye = faces.pop(0)
        yo = faces.pop(0) if with_yo else None
        xe = faces.pop(0)
        xo = faces.pop(0) if with_xo else None
        return ye, yo, xe, xo

    blocks, others, patterns = traces, [], [0]
    for axis, size, stride in (("gy", ny, 1), ("gx", nx, ny)):
        bit = 2
        while bit < size:
            got = swap(blocks, axis, xor(size, bit))
            others.append(got)
            patterns = patterns + [p ^ (bit * stride) for p in patterns]
            bit *= 2
            if bit < size or (axis == "gy" and nx > 2):
                blocks = jnp.concatenate([blocks, got], axis=0)
    if not others:
        others, patterns = [jnp.zeros_like(traces)], [0, -2]
    stage = pltpu.VMEM((nz // lanes, REACH * cx, lanes), F32)
    cur, toeplitz, bands, select, owners, own, *faces = vmem_call(
        functools.partial(load_kernel, with_yo=with_yo, with_xo=with_xo, each=per // rblk, rblk=rblk),
        [
            sds(tile), sds((2 * nz, nz), BF16), sds((2 * CHUNK * cy, CHUNK * cy), BF16),
            sds((cx * cy, 3 * slots), BF16), sds((slots, lanes), jnp.int32), sds((1, 8, lanes)),
        ] + face_shapes(),
        [adj_cur[0], column[0], rblock[0], traces, counts],
        [
            pltpu.VMEM((1, slots), jnp.int32), pltpu.VMEM((1, slots), jnp.int32), pltpu.VMEM((1, steps, per), BF16),
            stage, pltpu.SemaphoreType.DMA((4,)),
        ],
        hbm_in=(0, 1, 2, 3), smem_in=(4,),
    )
    ye, yo, xe, xo = taken(faces)
    others = [jnp.pad(a.astype(F32), ((0, 0), (0, 8 - steps), (0, lanes - per))) for a in others]
    tiles = jnp.concatenate([own] + others, axis=0)
    pairs = jnp.concatenate([tiles[0::2], tiles[1::2]], axis=2).astype(BF16).reshape(-1, nz)
    rye = swap(jnp.concatenate([ye, pairs], axis=0), "gy", even_pairs(ny))
    ryo = swap(yo, "gy") if with_yo else None
    rxo = swap(xo, "gx") if with_xo else None
    rxe = swap(jnp.concatenate([xe, pairs, rye[y_msg[0] :]], axis=0), "gx", even_pairs(nx))
    for stride in (1, ny):
        patterns = patterns + [p ^ stride if p >= 0 else p for p in patterns]

    part, _, c2, wts = vmem_call(
        first_update_kernel,
        [sds(tile), sds(tile), sds(tile), sds((slots, rblk, nz), BF16)],
        [cur, toeplitz, bands, adj_prev[0], courant2, weights[0, 0]],
        [pltpu.SemaphoreType.DMA((3,))],
        hbm_in=(3, 4, 5), flops=cells * 60,
    )

    def correct_y(part, ye, yo):
        return vmem_call(correct_y_kernel, [sds(tile)], [part, c2] + [a for a in (ye, yo) if a is not None], [stage])[0]

    part = correct_y(part, rye, ryo)
    nxt, contrib, *faces = vmem_call(
        functools.partial(
            first_correct_kernel, with_yo=with_yo, with_xo=with_xo, patterns=tuple(patterns)
        ),
        [sds(tile), sds((steps, 3 * slots, nz), BF16)] + face_shapes(),
        [owners, wts, select, part, c2] + given(rye, ryo, rxe, rxo) + [pairs],
        [pltpu.VMEM((steps, slots, nz), F32), stage],
    )
    previous, current = cur, nxt
    fine = None
    for step in range(1, steps):
        ye, yo, xe, xo = taken(faces)
        ryo = swap(yo, "gy") if with_yo else None
        rxe = swap(xe, "gx", even_pairs(nx))
        rxo = swap(xo, "gx") if with_xo else None
        rye = swap(ye, "gy", even_pairs(ny))
        args = [current, previous, c2, toeplitz, bands, select, contrib, accel]
        if fine is not None:
            args.append(fine)
        part, fine = vmem_call(
            functools.partial(update_kernel, step=step), [sds(tile), sds(tile)], args,
            flops=cells * 60,
        )
        part = correct_y(part, rye, ryo)
        halos = [a for a in (rxe, rxo) if a is not None]
        if step < steps - 1:
            nxt, *faces = vmem_call(
                functools.partial(correct_kernel, with_yo=with_yo, with_xo=with_xo),
                [sds(tile)] + face_shapes(),
                [part, c2] + halos,
                [stage],
            )
        else:
            nxt, coarse = vmem_call(
                functools.partial(last_kernel, with_xo=with_xo, step=step),
                [sds(tile), sds((cx // 2, cy // 2, nz // 2))],
                [part, c2, accel, fine] + halos,
                [pltpu.VMEM((cx * cy // 2, nz // 2), F32), stage],
            )
        previous, current = current, nxt
    bit = 1
    while bit < nshot:
        one = swap(coarse, "shot", xor(nshot, bit))
        if nshot % (4 * bit) == 0:
            two = swap(coarse, "shot", xor(nshot, 2 * bit))
            three = swap(coarse, "shot", xor(nshot, 3 * bit))
            coarse = (coarse + one) + (two + three)
            bit *= 4
        else:
            coarse = coarse + one
            bit *= 2
    previous, current = vmem_call(
        flush_kernel, [sds(tile), sds(tile)], [previous, current], [pltpu.SemaphoreType.DMA((2,))],
        hbm_out=(0, 1),
    )
    return (previous[None], current[None], coarse)


def solution(mesh):
    return jax.shard_map(
        local,
        mesh=mesh,
        in_specs=(
            P("shot", "gx", "gy", None),
            P("shot", "gx", "gy", None),
            P("shot", None, "gx", "gy", None),
            P("gx", "gy", None),
            P("shot", None, ("gx", "gy")),
            P("gx", "gy", None, None, None),
            P("gx", "gy", None),
            P("gx", "gy", None),
            P("gx", "gy"),
        ),
        out_specs=(P("shot", "gx", "gy", None), P("shot", "gx", "gy", None), P("gx", "gy", None)),
        check_vma=False,
    )
```

```python
import functools

import jax
import jax.numpy as jnp
from jax import lax
from jax.experimental import pallas as pl
from jax.experimental.pallas import tpu as pltpu
from jax.sharding import PartitionSpec as P


LAPLACE_COEFS = (-205.0 / 72.0, 8.0 / 5.0, -1.0 / 5.0, 8.0 / 315.0, -1.0 / 560.0)
REACH = 4
CHUNK = 8
VMEM_LIMIT = 16 << 20
F32 = jnp.float32
BF16 = jnp.bfloat16


def vmem_call(kernel, outs, args, scratch=(), flops=0, hbm_in=(), hbm_out=(), smem_in=(), aliases=None):
    in_specs = [
        pl.BlockSpec(memory_space=pltpu.HBM if i in hbm_in else pltpu.SMEM if i in smem_in else pltpu.VMEM)
        for i in range(len(args))
    ]
    args = [pltpu.with_memory_space_constraint(a, pltpu.HBM) if i in hbm_in else a for i, a in enumerate(args)]
    moved = sum(a.size * a.dtype.itemsize for a in args) + sum(o.size * o.dtype.itemsize for o in outs)
    return pl.pallas_call(
        kernel,
        out_shape=tuple(outs),
        in_specs=in_specs,
        out_specs=tuple(
            pl.BlockSpec(memory_space=pltpu.HBM if i in hbm_out else pltpu.VMEM) for i in range(len(outs))
        ),
        scratch_shapes=list(scratch),
        input_output_aliases=aliases or {},
        cost_estimate=pl.CostEstimate(flops=flops, bytes_accessed=moved, transcendentals=0),
        compiler_params=pltpu.CompilerParams(vmem_limit_bytes=VMEM_LIMIT),
    )(*args)


def sds(shape, dtype=F32):
    return jax.ShapeDtypeStruct(shape, dtype)


def even_pairs(n):
    pairs = []
    for i in range(0, n - 1, 2):
        pairs += [(i, i + 1), (i + 1, i)]
    return pairs


def odd_swap(x, axis):
    n, shots = lax.axis_size(axis), lax.axis_size("shot")
    if shots % 2:
        pairs = [(0, n - 1), (n - 1, 0)]
        for i in range(1, n - 1, 2):
            pairs += [(i, i + 1), (i + 1, i)]
        return lax.ppermute(x, axis, pairs)
    pairs = []
    for s in range(shots):
        for i in (0, n - 1):
            pairs.append((i * shots + s, i * shots + (s ^ 1)))
        for i in range(1, n - 1, 2):
            pairs += [(i * shots + s, (i + 1) * shots + s), ((i + 1) * shots + s, i * shots + s)]
    return lax.ppermute(x, (axis, "shot"), pairs)


def split2(v):
    hi = v.astype(BF16)
    return hi, (v - hi.astype(F32)).astype(BF16)


def dot(a, b):
    return jnp.dot(a, b, preferred_element_type=F32)


def put_y_face(cur, out, stage, high):
    cx, cy, _ = cur.shape
    start = cy - REACH if high else 0
    for h in range(stage.shape[0]):
        at = slice(h * 128, (h + 1) * 128)
        for x in range(cx):
            stage[h, REACH * x : REACH * (x + 1), :] = cur[x, start : start + REACH, at]
        out[0 : REACH * cx, at] = stage[h, :, :].astype(BF16)
        near = stage[h, pl.ds(REACH - 1 if high else 0, cx, REACH), :]
        out[REACH * cx : (REACH + 1) * cx, at] = split2(near)[1]


def put_x_face(cur, out, high):
    cx, cy, _ = cur.shape
    low = jnp.where(high, cx - REACH, 0)
    for r in range(REACH):
        out[r * cy : (r + 1) * cy, :] = cur[low + r, :, :].astype(BF16)
    out[REACH * cy : (REACH + 1) * cy, :] = split2(cur[jnp.where(high, cx - 1, 0), :, :])[1]


def put_faces(cur, gx_index, gy_index, ye, yo, xe, xo, stage):
    y_even = gy_index % 2 == 0
    x_even = gx_index % 2 == 0

    @pl.when(y_even)
    def _():
        put_y_face(cur, ye, stage, True)
        if yo is not None:
            put_y_face(cur, yo, stage, False)

    @pl.when(jnp.logical_not(y_even))
    def _():
        put_y_face(cur, ye, stage, False)
        if yo is not None:
            put_y_face(cur, yo, stage, True)

    put_x_face(cur, xe, x_even)
    if xo is not None:
        put_x_face(cur, xo, jnp.logical_not(x_even))


def add_y_halo(nxt, c2, recv, stage, high):
    cx, cy, nz = nxt.shape
    w = LAPLACE_COEFS
    near = pl.ds(0 if high else REACH - 1, cx, REACH)
    for h in range(stage.shape[0]):
        at = slice(h * 128, (h + 1) * 128)
        stage[h, :, :] = recv[0 : REACH * cx, at].astype(F32)
        stage[h, near, :] = stage[h, near, :] + recv[REACH * cx : (REACH + 1) * cx, at].astype(F32)
    row = lax.broadcasted_iota(jnp.int32, (8, nz), 0) % REACH
    coefs = {}
    for k in range(1, REACH + 1):
        shift = REACH - k
        keep = (row >= shift) if high else (row < k)
        coefs[k] = jnp.where(keep, w[k], 0.0)
    start = cy - REACH if high else 0
    for i in range(cx // 2):
        m = jnp.concatenate([stage[h, 8 * i : 8 * i + 8, :] for h in range(stage.shape[0])], axis=1)
        total = w[REACH] * m
        for k in range(1, REACH):
            shift = REACH - k
            total = total + coefs[k] * pltpu.roll(m, shift if high else 8 - shift, 0)
        for h in range(2):
            rows = slice(start, start + REACH)
            nxt[2 * i + h, rows, :] = (
                nxt[2 * i + h, rows, :] + c2[2 * i + h, rows, :] * total[REACH * h : REACH * h + REACH, :]
            )


def add_x_halo(nxt, c2, recv, stage, high):
    cx, cy, _ = nxt.shape
    w = LAPLACE_COEFS
    layers = [recv[r * cy : (r + 1) * cy, :].astype(F32) for r in range(REACH + 1)]
    near = 0 if high else REACH - 1
    layers[near] = layers[near] + layers[REACH]
    for r in range(REACH):
        x = cx - 1 - r if high else r
        total = None
        for k in range(r + 1, REACH + 1):
            term = w[k] * layers[(k - r - 1) if high else (REACH + r - k)]
            total = term if total is None else total + term
        nxt[x, :, :] = nxt[x, :, :] + c2[x, :, :] * total


def add_halos(nxt, c2, name, even, odd, stage):
    index, add = lax.axis_index(name), add_y_halo if name == "gy" else add_x_halo
    is_even = index % 2 == 0
    inner = jnp.logical_and(index > 0, index < lax.axis_size(name) - 1)

    @pl.when(is_even)
    def _():
        add(nxt, c2, even, stage, True)

    @pl.when(jnp.logical_not(is_even))
    def _():
        add(nxt, c2, even, stage, False)

    if odd is not None:

        @pl.when(jnp.logical_and(inner, is_even))
        def _():
            add(nxt, c2, odd, stage, False)

        @pl.when(jnp.logical_and(inner, jnp.logical_not(is_even)))
        def _():
            add(nxt, c2, odd, stage, True)


def put_band(out, size, span, centre):
    row = lax.broadcasted_iota(jnp.int32, (size, size), 0)
    column = lax.broadcasted_iota(jnp.int32, (size, size), 1)
    distance = jnp.abs(row - column)
    band = jnp.where(distance == 0, centre, 0.0)
    for k in range(1, REACH + 1):
        band = band + jnp.where(distance == k, LAPLACE_COEFS[k], 0.0)
    if span < size:
        band = jnp.where(lax.div(row, jnp.int32(span)) == lax.div(column, jnp.int32(span)), band, 0.0)
    hi, lo = split2(band)
    out[0:size, :] = hi
    out[size : 2 * size, :] = lo


def load_kernel(
    cur_in, col_in, rb_in, traces_in, counts, cur, toeplitz, blocks, select, owners, own, *refs,
    with_yo, with_xo, each, rblk,
):
    ye, yo, xe, xo, (col, rb, traces, stage, sems) = unpack(refs, with_yo, with_xo)
    gx_index, gy_index = lax.axis_index("gx"), lax.axis_index("gy")
    pairs = ((cur_in, cur), (col_in, col), (rb_in, rb), (traces_in, traces))
    copies = [pltpu.make_async_copy(src, dst, sems.at[i]) for i, (src, dst) in enumerate(pairs)]
    for copy in copies:
        copy.start()
    nz, rows, cy = toeplitz.shape[1], blocks.shape[1], cur.shape[1]
    put_band(toeplitz, nz, nz, 3.0 * LAPLACE_COEFS[0])
    put_band(blocks, rows, cy, 0.0)
    for copy in copies[1:]:
        copy.wait()
    wide = jnp.concatenate([col[...]] * 3, axis=1)
    rows = lax.broadcasted_iota(jnp.int32, select.shape, 0)
    select[...] = jnp.where(rows == wide, 1.0, 0.0).astype(BF16)
    slot_owners(rb, counts, owners, each, rblk)
    steps, per = traces.shape[1:]
    own[...] = jnp.zeros(own.shape, F32)
    own[0, 0:steps, 0:per] = traces[0].astype(F32)
    copies[0].wait()
    put_faces(cur, gx_index, gy_index, ye, yo, xe, xo, stage)


def slot_owners(rb, counts, owners, each, rblk):
    me = lax.axis_index("gx") * lax.axis_size("gy") + lax.axis_index("gy")
    slots, lanes = owners.shape
    eye = lax.broadcasted_iota(jnp.int32, (slots, slots), 0) == lax.broadcasted_iota(jnp.int32, (slots, slots), 1)
    block_of = jnp.sum(jnp.where(eye, jnp.broadcast_to(rb[...], (slots, slots)), 0), axis=1, keepdims=True)
    owner = lax.div(block_of, jnp.int32(each))
    group = block_of - owner * each
    lane = lax.broadcasted_iota(jnp.int32, (slots, lanes), 1)
    live = lax.broadcasted_iota(jnp.int32, (slots, lanes), 0) < counts[0, 0]
    used = jnp.logical_and(live, lax.div(lane, jnp.int32(rblk)) == group)
    owners[...] = jnp.where(used, jnp.bitwise_xor(owner, me), -1)


def flush_kernel(a_in, b_in, a_out, b_out, sems):
    copies = [
        pltpu.make_async_copy(src, dst, sems.at[i]) for i, (src, dst) in enumerate(((a_in, a_out), (b_in, b_out)))
    ]
    for copy in copies:
        copy.start()
    for copy in copies:
        copy.wait()


def update(cur, prev, c2, toeplitz, blocks, out, source=None, fine=None):
    cx, cy, nz = cur.shape
    w = LAPLACE_COEFS
    chunk = CHUNK
    rows = chunk * cy
    t_hi = toeplitz[0:nz, :]
    t_lo = toeplitz[nz : 2 * nz, :]
    b_hi = blocks[0:rows, :]
    b_lo = blocks[rows : 2 * rows, :]
    for m in range(cx // chunk):
        v = cur[m * chunk : (m + 1) * chunk, :, :].reshape(rows, nz)
        hi, lo = split2(v)
        lz = dot(hi, t_hi) + dot(lo, t_hi) + dot(hi, t_lo)
        lz = lz + dot(b_hi, hi) + dot(b_hi, lo) + dot(b_lo, hi)
        if source is not None:
            select, contrib = source
            src = dot(select[m * rows : (m + 1) * rows, :], contrib)
        for j in range(chunk):
            x = m * chunk + j
            total = lz[j * cy : (j + 1) * cy, :]
            for k in range(1, REACH + 1):
                near = [cur[i, :, :] for i in (x - k, x + k) if 0 <= i < cx]
                if near:
                    total = total + w[k] * (near[0] if len(near) == 1 else near[0] + near[1])
            if prev is None:
                out[x, :, :] = total
                continue
            here = cur[x, :, :]
            value = (2.0 * here - prev[x, :, :]) + c2[x, :, :] * total
            if source is not None:
                value = value + src[j * cy : (j + 1) * cy, :]
            out[x, :, :] = value
            if fine is not None:
                fine_in, accel, fine_out = fine
                term = accel[x, :, :].astype(F32) * here
                fine_out[x, :, :] = term if fine_in is None else fine_in[x, :, :] + term


def first_update_kernel(cur, toeplitz, blocks, prev_in, c2_in, weights_in, out, prev, c2, weights, sems):
    copies = [
        pltpu.make_async_copy(src, dst, sems.at[i])
        for i, (src, dst) in enumerate(((prev_in, prev), (c2_in, c2), (weights_in, weights)))
    ]
    for copy in copies:
        copy.start()
    update(cur, None, None, toeplitz, blocks, out)
    copies[0].wait()
    copies[1].wait()
    for x in range(cur.shape[0]):
        out[x, :, :] = (2.0 * cur[x, :, :] - prev[x, :, :]) + c2[x, :, :] * out[x, :, :]
    copies[2].wait()


def update_kernel(cur, prev, c2, toeplitz, blocks, select, contrib, accel, *rest, step):
    if step == 1:
        out, fine_out = rest
        fine_in = None
    else:
        fine_in, out, fine_out = rest
    update(
        cur, prev, c2, toeplitz, blocks, out,
        source=(select, contrib[step]), fine=(fine_in, accel.at[step - 1], fine_out),
    )


def contributions(owners, weights, blocks, patterns, contrib, wide):
    slots, rblk, nz = weights.shape
    steps = contrib.shape[0]
    lanes = 128
    picked = [jnp.zeros((slots, lanes), F32) for _ in range(steps)]
    for tile, pattern in zip(blocks, patterns):
        mask = owners[...] == pattern
        for t in range(steps):
            picked[t] = jnp.where(mask, tile[t : t + 1, :], picked[t])
    spread = (
        lax.rem(lax.broadcasted_iota(jnp.int32, (lanes, lanes), 0), jnp.int32(rblk))
        == lax.rem(lax.broadcasted_iota(jnp.int32, (lanes, lanes), 1), jnp.int32(rblk))
    )
    spread = jnp.where(spread, 1.0, 0.0).astype(BF16)
    tiled = [dot(p.astype(BF16), spread) for p in picked]
    together = lanes // rblk
    diagonal = lax.broadcasted_iota(jnp.int32, (together, lanes), 0) == lax.div(
        lax.broadcasted_iota(jnp.int32, (together, lanes), 1), jnp.int32(rblk)
    )
    for q in range(slots // together):
        rows = slice(q * together, (q + 1) * together)
        left = jnp.concatenate([jnp.where(diagonal, v[rows, :], 0.0) for v in tiled], axis=0).astype(BF16)
        right = weights[q * together : (q + 1) * together, :, :].reshape(together * rblk, nz)
        got = dot(left, right)
        for t in range(steps):
            wide[t, rows, :] = got[t * together : (t + 1) * together, :]
    for t in range(steps):
        hi, mid = split2(wide[t, :, :])
        rest = wide[t, :, :] - hi.astype(F32) - mid.astype(F32)
        contrib[t, 0:slots, :] = hi
        contrib[t, slots : 2 * slots, :] = mid
        contrib[t, 2 * slots : 3 * slots, :] = rest.astype(BF16)


def unpack(refs, with_yo, with_xo):
    refs = list(refs)
    ye = refs.pop(0)
    yo = refs.pop(0) if with_yo else None
    xe = refs.pop(0)
    xo = refs.pop(0) if with_xo else None
    return ye, yo, xe, xo, refs


def first_correct_kernel(owners, weights, select, part, c2, *refs, with_yo, with_xo, patterns):
    gx_index, gy_index = lax.axis_index("gx"), lax.axis_index("gy")
    ye, _, xe, xo, refs = unpack(refs, with_yo, with_xo)
    pairs, refs = refs[0], refs[1:]
    nxt, contrib, refs = refs[0], refs[1], refs[2:]
    oye, oyo, oxe, oxo, refs = unpack(refs, with_yo, with_xo)
    wide, stage = refs
    lanes = 128
    tiles = []
    rows = pairs.shape[0]
    y_last, x_last = ye.shape[0] - rows, xe.shape[0] - 2 * rows
    for block in (pairs[...], ye[y_last : y_last + rows, :], xe[x_last : x_last + 2 * rows, :]):
        block = block.astype(F32)
        for i in range(0, block.shape[0], 8):
            tiles += [block[i : i + 8, 0:lanes], block[i : i + 8, lanes : 2 * lanes]]
    contributions(owners, weights, tiles, patterns, contrib, wide)
    cx, cy, nz = nxt.shape
    chunk = 8
    rows = chunk * cy
    for m in range(cx // chunk):
        src = dot(select[m * rows : (m + 1) * rows, :], contrib[0])
        at = slice(m * chunk, (m + 1) * chunk)
        nxt[at, :, :] = part[at, :, :] + src.reshape(chunk, cy, nz)
    add_halos(nxt, c2, "gx", xe, xo, stage)
    put_faces(nxt, gx_index, gy_index, oye, oyo, oxe, oxo, stage)


def correct_y_kernel(part, c2, *refs):
    out, stage = refs[-2:]
    add_halos(out, c2, "gy", refs[0], refs[1] if len(refs) == 4 else None, stage)


def correct_kernel(part, c2, *refs, with_yo, with_xo):
    gx_index, gy_index = lax.axis_index("gx"), lax.axis_index("gy")
    xe, xo = refs[0], refs[1] if with_xo else None
    refs = refs[1 + with_xo :]
    nxt, refs = refs[0], refs[1:]
    oye, oyo, oxe, oxo, (stage,) = unpack(refs, with_yo, with_xo)
    add_halos(nxt, c2, "gx", xe, xo, stage)
    put_faces(nxt, gx_index, gy_index, oye, oyo, oxe, oxo, stage)


def last_kernel(part, c2, accel, fine, *refs, with_xo, step):
    xe, xo = refs[0], refs[1] if with_xo else None
    nxt, coarse, middle, stage = refs[1 + with_xo :]
    cx, cy, nz = nxt.shape
    add_halos(nxt, c2, "gx", xe, xo, stage)
    pairs = lax.div(lax.broadcasted_iota(jnp.int32, (nz, nz // 2), 0), jnp.int32(2)) == lax.broadcasted_iota(
        jnp.int32, (nz, nz // 2), 1
    )
    pairs = jnp.where(pairs, 0.125, 0.0).astype(BF16)
    chunk = 8
    for m in range(cx // (2 * chunk)):
        summed = []
        for j in range(chunk):
            x = 2 * (m * chunk + j)
            a = fine[x, :, :] + accel[step, x, :, :].astype(F32) * nxt[x, :, :]
            b = fine[x + 1, :, :] + accel[step, x + 1, :, :].astype(F32) * nxt[x + 1, :, :]
            summed.append(a + b)
        hi, lo = split2(jnp.concatenate(summed, axis=0))
        got = dot(hi, pairs) + dot(lo, pairs)
        middle[m * chunk * cy : (m + 1) * chunk * cy, :] = got
    half = cx * cy // 4
    both = middle[pl.ds(0, half, 2), :] + middle[pl.ds(1, half, 2), :]
    coarse[...] = both.reshape(coarse.shape)


def local(adj_prev, adj_cur, fwd_accel, courant2, traces, weights, rblock, column, counts):
    accel = fwd_accel[0]
    cx, cy, nz = courant2.shape
    steps = accel.shape[0]
    slots, rblk = weights.shape[2:4]
    per = traces.shape[2]
    nx, ny, nshot = lax.axis_size("gx"), lax.axis_size("gy"), lax.axis_size("shot")
    with_yo, with_xo = ny > 2, nx > 2
    y_msg, x_msg = ((REACH + 1) * cx, nz), ((REACH + 1) * cy, nz)
    tile = (cx, cy, nz)
    cells = cx * cy * nz
    lanes = 128

    def swap(x, axis, pairs=None):
        return odd_swap(x, axis) if pairs is None else lax.ppermute(x, axis, pairs)

    def xor(size, bit):
        return [(i, i ^ bit) for i in range(size)]

    def given(ye, yo, xe, xo):
        return [a for a in (ye, yo, xe, xo) if a is not None]

    def face_shapes():
        y, x = sds(y_msg, BF16), sds(x_msg, BF16)
        return given(y, y if with_yo else None, x, x if with_xo else None)

    def taken(faces):
        faces = list(faces)
        ye = faces.pop(0)
        yo = faces.pop(0) if with_yo else None
        xe = faces.pop(0)
        xo = faces.pop(0) if with_xo else None
        return ye, yo, xe, xo

    blocks, others, patterns = traces, [], [0]
    for axis, size, stride in (("gy", ny, 1), ("gx", nx, ny)):
        bit = 2
        while bit < size:
            got = swap(blocks, axis, xor(size, bit))
            others.append(got)
            patterns = patterns + [p ^ (bit * stride) for p in patterns]
            bit *= 2
            if bit < size or (axis == "gy" and nx > 2):
                blocks = jnp.concatenate([blocks, got], axis=0)
    if not others:
        others, patterns = [jnp.zeros_like(traces)], [0, -2]
    stage = pltpu.VMEM((nz // lanes, REACH * cx, lanes), F32)
    cur, toeplitz, bands, select, owners, own, *faces = vmem_call(
        functools.partial(load_kernel, with_yo=with_yo, with_xo=with_xo, each=per // rblk, rblk=rblk),
        [
            sds(tile), sds((2 * nz, nz), BF16), sds((2 * CHUNK * cy, CHUNK * cy), BF16),
            sds((cx * cy, 3 * slots), BF16), sds((slots, lanes), jnp.int32), sds((1, 8, lanes)),
        ] + face_shapes(),
        [adj_cur[0], column[0], rblock[0], traces, counts],
        [
            pltpu.VMEM((1, slots), jnp.int32), pltpu.VMEM((1, slots), jnp.int32), pltpu.VMEM((1, steps, per), BF16),
            stage, pltpu.SemaphoreType.DMA((4,)),
        ],
        hbm_in=(0, 1, 2, 3), smem_in=(4,),
    )
    ye, yo, xe, xo = taken(faces)
    others = [jnp.pad(a.astype(F32), ((0, 0), (0, 8 - steps), (0, lanes - per))) for a in others]
    tiles = jnp.concatenate([own] + others, axis=0)
    pairs = jnp.concatenate([tiles[0::2], tiles[1::2]], axis=2).astype(BF16).reshape(-1, nz)
    rye = swap(jnp.concatenate([ye, pairs], axis=0), "gy", even_pairs(ny))
    ryo = swap(yo, "gy") if with_yo else None
    rxo = swap(xo, "gx") if with_xo else None
    rxe = swap(jnp.concatenate([xe, pairs, rye[y_msg[0] :]], axis=0), "gx", even_pairs(nx))
    for stride in (1, ny):
        patterns = patterns + [p ^ stride if p >= 0 else p for p in patterns]

    part, _, c2, wts = vmem_call(
        first_update_kernel,
        [sds(tile), sds(tile), sds(tile), sds((slots, rblk, nz), BF16)],
        [cur, toeplitz, bands, adj_prev[0], courant2, weights[0, 0]],
        [pltpu.SemaphoreType.DMA((3,))],
        hbm_in=(3, 4, 5), flops=cells * 60,
    )

    def correct_y(part, ye, yo):
        return vmem_call(
            correct_y_kernel, [sds(tile)], [part, c2] + [a for a in (ye, yo) if a is not None], [stage],
            aliases={0: 0},
        )[0]

    part = correct_y(part, rye, ryo)
    nxt, contrib, *faces = vmem_call(
        functools.partial(
            first_correct_kernel, with_yo=with_yo, with_xo=with_xo, patterns=tuple(patterns)
        ),
        [sds(tile), sds((steps, 3 * slots, nz), BF16)] + face_shapes(),
        [owners, wts, select, part, c2] + given(rye, ryo, rxe, rxo) + [pairs],
        [pltpu.VMEM((steps, slots, nz), F32), stage],
    )
    previous, current = cur, nxt
    fine = None
    for step in range(1, steps):
        ye, yo, xe, xo = taken(faces)
        ryo = swap(yo, "gy") if with_yo else None
        rxe = swap(xe, "gx", even_pairs(nx))
        rxo = swap(xo, "gx") if with_xo else None
        rye = swap(ye, "gy", even_pairs(ny))
        args = [current, previous, c2, toeplitz, bands, select, contrib, accel]
        if fine is not None:
            args.append(fine)
        part, fine = vmem_call(
            functools.partial(update_kernel, step=step), [sds(tile), sds(tile)], args,
            flops=cells * 60,
        )
        part = correct_y(part, rye, ryo)
        halos = [a for a in (rxe, rxo) if a is not None]
        if step < steps - 1:
            nxt, *faces = vmem_call(
                functools.partial(correct_kernel, with_yo=with_yo, with_xo=with_xo),
                [sds(tile)] + face_shapes(),
                [part, c2] + halos,
                [stage],
                aliases={0: 0},
            )
        else:
            nxt, coarse = vmem_call(
                functools.partial(last_kernel, with_xo=with_xo, step=step),
                [sds(tile), sds((cx // 2, cy // 2, nz // 2))],
                [part, c2, accel, fine] + halos,
                [pltpu.VMEM((cx * cy // 2, nz // 2), F32), stage],
                aliases={0: 0},
            )
        previous, current = current, nxt
    bit = 1
    while bit < nshot:
        one = swap(coarse, "shot", xor(nshot, bit))
        if nshot % (4 * bit) == 0:
            two = swap(coarse, "shot", xor(nshot, 2 * bit))
            three = swap(coarse, "shot", xor(nshot, 3 * bit))
            coarse = (coarse + one) + (two + three)
            bit *= 4
        else:
            coarse = coarse + one
            bit *= 2
    previous, current = vmem_call(
        flush_kernel, [sds(tile), sds(tile)], [previous, current], [pltpu.SemaphoreType.DMA((2,))],
        hbm_out=(0, 1),
    )
    return (previous[None], current[None], coarse)


def solution(mesh):
    return jax.shard_map(
        local,
        mesh=mesh,
        in_specs=(
            P("shot", "gx", "gy", None),
            P("shot", "gx", "gy", None),
            P("shot", None, "gx", "gy", None),
            P("gx", "gy", None),
            P("shot", None, ("gx", "gy")),
            P("gx", "gy", None, None, None),
            P("gx", "gy", None),
            P("gx", "gy", None),
            P("gx", "gy"),
        ),
        out_specs=(P("shot", "gx", "gy", None), P("shot", "gx", "gy", None), P("gx", "gy", None)),
        check_vma=False,
    )
```
